32 devices in a mesh: space: 8 (over z, y), segment: 4 (over x, core).
Axes of the slice: x: 2, y: 2, z: 4, core: 2. Of those that a mesh axis runs over, the one named last changes fastest.
Arguments:
- saved_inputs: bfloat16 [4, 1048576], P('segment', 'space'), may hold values from -5.5 to 5.5
- conv_weights: bfloat16 [4, 221184], P('segment'), may hold values from -0.4375 to 0.4375
- top_gradient: bfloat16 [128, 8, 2, 32], P(None, 'space'), may hold values from -6 to 6
Outputs:
- weight_grads: float32 [4, 221184], P('segment')
The draws below stay inside these ranges and needn't reach their ends.
All inputs are finite; a program needn't handle non-finite values.
Results may differ from the reference program's by a relative error of at most 0.0023.
Values may be sent and summed in bfloat16 or wider, within the bound.
No kernel may reach another device: no remote copies, remote signals or barrier semaphores. Data moves between devices by JAX's collectives and lax.ppermute only.
A program may use at most 64 MiB of HBM per device.

```python
import math
import jax
import jax.numpy as jnp

C0 = 4
C1 = 16
C2 = 32
C3 = 64
C4 = 128
CZ = 4
CY = 8
CX = 128
SECTIONS = 4
NZ = 32
FLAT = 131072
ROW = 1048576
WMAX = 221184
N_SPACE = 8


def region_levels(key):
    return jax.random.uniform(jax.random.fold_in(key, 101), (NZ // CZ, 4), jnp.float32)


def draw_top_gradient(key, part):
    levels = region_levels(key)
    depth_block = jnp.arange(NZ // 4) // (CZ // 4)
    region = 4 * jnp.arange(CX // 4) // (CX // 4)
    chosen = levels[depth_block][:, region]
    loudness = 2.0 * jnp.exp(-3.0 * chosen)
    noise_key = jax.random.fold_in(key, 102)
    extent = (C4, NZ // 4, CY // 4, CX // 4)
    pattern = jnp.clip(jax.random.normal(noise_key, extent, jnp.float32), -3.0, 3.0)
    return (pattern * loudness[None, :, None, :]).astype(jnp.bfloat16)


def draw_saved_inputs(key, part):
    levels = region_levels(key)
    offsets = jnp.arange(FLAT)
    row_levels = []
    for section_row in range(SECTIONS):
        breadth = CX if section_row < 3 else CX // 2
        region = offsets % breadth * (CX // breadth) // (CX // 4)
        chosen = levels[:, region]
        row_levels.append(0.1 * jnp.exp(4.0 * chosen))
    loudness = jnp.stack(row_levels)
    pattern = jax.random.uniform(jax.random.fold_in(key, 103), (SECTIONS, NZ // CZ, FLAT), jnp.float32, -1.0, 1.0)
    return (pattern * loudness).reshape(SECTIONS, ROW).astype(jnp.bfloat16)


def level_of(key, dims, split, least, largest):
    gain, own = 1.0, jax.random.fold_in(key, 6)
    for dim, parts in split:
        steps = jnp.exp(jax.random.uniform(jax.random.fold_in(own, dim), (parts,), jnp.float32, least / len(split), largest / len(split)))
        gain = gain * jnp.repeat(steps, dims[dim] // parts).reshape([-1 if axis == dim else 1 for axis in range(len(dims))])
    return gain


def bell_draw(rng, dims, scale, bound, cuts=(), dtype=jnp.bfloat16):
    gain = level_of(rng, dims, cuts, -0.22, 0.18) if cuts else 1.0
    drawn = jax.random.normal(rng, dims, jnp.float32) * scale * gain
    return jnp.minimum(jnp.maximum(drawn, -bound), bound).astype(dtype)


def setup_inputs(seed: int = 0) -> dict:
    seeds = jax.random.split(jax.random.key(seed), 4)
    saved_inputs = draw_saved_inputs(jax.random.fold_in(seeds[3], 71), 0)
    conv_weights = bell_draw(seeds[1], (SECTIONS, WMAX), 216 ** -0.5, 0.4375, ((0, 4),))
    top_gradient = draw_top_gradient(jax.random.fold_in(seeds[3], 71), 0)
    return {"saved_inputs": saved_inputs, "conv_weights": conv_weights, "top_gradient": top_gradient}


slope_negative = 0.3

def layer_table():
    return [(C0, C1, 1, CZ, CY, CX), (C1, C2, 1, CZ, CY, CX), (C2, C3, 2, CZ, CY, CX), (C3, C4, 2, CZ // 2, CY // 2, CX // 2)]

def unpack_volume(packed_row, channels, depth_cells, height, breadth):
    volume_size = channels * depth_cells * height * breadth
    blocks = packed_row.reshape(N_SPACE, -1)[:, :volume_size]
    blocks = blocks.reshape(N_SPACE, channels, depth_cells, height, breadth)
    return jnp.transpose(blocks, (1, 0, 2, 3, 4)).reshape(channels, N_SPACE * depth_cells, height, breadth)

def weight_grad(activation, upstream, stride_size):
    if stride_size == 1:
        padded = jnp.pad(activation, ((0, 0), (1, 1), (1, 1), (1, 1)))
    else:
        padded = jnp.pad(activation, ((0, 0), (0, 1), (0, 1), (0, 1)))
    out_z, out_y, out_x = (upstream.shape[1], upstream.shape[2], upstream.shape[3])
    widened = upstream.astype(jnp.float32)
    results = []
    for tap_z in range(3):
        for tap_y in range(3):
            for tap_x in range(3):
                window = padded[:, tap_z:tap_z + stride_size * (out_z - 1) + 1:stride_size, tap_y:tap_y + stride_size * (out_y - 1) + 1:stride_size, tap_x:tap_x + stride_size * (out_x - 1) + 1:stride_size]
                results.append(jnp.einsum('dzyx,czyx->dc', widened, window.astype(jnp.float32)))
    return jnp.stack(results)

def input_grad(weights, upstream, stride_size):
    chan_out, out_z, out_y, out_x = upstream.shape
    widened = upstream.astype(jnp.float32)
    if stride_size == 1:
        padded = jnp.pad(widened, ((0, 0), (1, 1), (1, 1), (1, 1)))
    else:
        spread = jnp.zeros((chan_out, 2 * out_z, 2 * out_y, 2 * out_x), jnp.float32)
        spread = spread.at[:, ::2, ::2, ::2].set(widened)
        padded = jnp.pad(spread, ((0, 0), (2, 0), (2, 0), (2, 0)))
    size_z, size_y, size_x = (stride_size * out_z, stride_size * out_y, stride_size * out_x)
    weights_wide = weights.astype(jnp.float32)
    summed = jnp.zeros((weights.shape[2], size_z, size_y, size_x), jnp.float32)
    for tap_z in range(3):
        for tap_y in range(3):
            for tap_x in range(3):
                window = padded[:, 2 - tap_z:2 - tap_z + size_z, 2 - tap_y:2 - tap_y + size_y, 2 - tap_x:2 - tap_x + size_x]
                summed = summed + jnp.einsum('dc,dzyx->czyx', weights_wide[9 * tap_z + 3 * tap_y + tap_x], window)
    return summed

def reference(saved_inputs, conv_weights, top_gradient):
    upstream = top_gradient
    wide_rows = [None, None, None, None]
    for section in (3, 2, 1, 0):
        chan_in, chan_out, stride_size, depth_cells, height, breadth = layer_table()[section]
        activation = unpack_volume(saved_inputs[section], chan_in, depth_cells, height, breadth)
        weights = conv_weights[section][:27 * chan_out * chan_in].reshape(27, chan_out, chan_in)
        positions = upstream.shape[1] * upstream.shape[2] * upstream.shape[3]
        gradient = weight_grad(activation, upstream, stride_size) * (1.0 / math.sqrt(positions))
        flat_grad = gradient.reshape(-1)
        wide_rows[section] = jnp.pad(flat_grad, (0, conv_weights.shape[1] - flat_grad.shape[0]))
        if section > 0:
            backward = input_grad(weights, upstream, stride_size)
            upstream = (backward * jnp.where(activation > 0, 1.0, slope_negative)).astype(jnp.bfloat16)
    return jnp.stack(wide_rows)
```

```python
import functools
import math

import jax
import jax.numpy as jnp
from jax import lax
from jax.experimental import pallas as pl
from jax.experimental.pallas import tpu as pltpu
from jax.sharding import PartitionSpec as P

C0, C1, C2, C3, C4 = 4, 16, 32, 64, 128
LANES = 128
SLOPE = 0.3
BF16 = jnp.bfloat16
F32 = jnp.float32
GATHER_LIMIT = 8
VMEM_LIMIT = 48 * 1024 * 1024


def on_segment(index):
    return lax.axis_index("segment") == index


def is_last_block():
    return lax.axis_index("space") == lax.axis_size("space") - 1


def cols(row, count=1):
    return slice(LANES * row, LANES * (row + count))


def moved_lanes(block, distance):
    lane = lax.broadcasted_iota(jnp.int32, block.shape, 1)
    rolled = pltpu.roll(block.astype(F32), distance % LANES, 1)
    kept = lane >= distance if distance > 0 else lane < LANES + distance
    return jnp.where(kept, rolled, 0.0).astype(BF16)


def stack_moved(read, target, chans, rows, distances):
    for row in range(rows):
        block = read(row)
        for place, distance in enumerate(distances):
            moved = moved_lanes(block, distance) if distance else block
            target[place * chans : (place + 1) * chans, cols(row)] = moved


def spread(rows_in, rows_out, source, bound):
    entry = lax.broadcasted_iota(jnp.int32, (rows_in, rows_out), 0)
    place = lax.broadcasted_iota(jnp.int32, (rows_in, rows_out), 1)
    return jnp.where((place == source(entry)) & bound(entry), 1.0, 0.0).astype(BF16)


def taps_of(cell, low, high):
    if cell % 2:
        pairs = [(1, (cell - 1) // 2)]
    else:
        pairs = [(0, cell // 2), (2, cell // 2 - 1)]
    return [(tap, place) for tap, place in pairs if low <= place <= high]


def dot_rows(left, right):
    return lax.dot_general(left, right, (((1,), (1,)), ((), ())), preferred_element_type=F32)


def dot(left, right):
    return jnp.dot(left, right, preferred_element_type=F32)


def sloped(total, activation):
    return (total * jnp.where(activation > 0, 1.0, SLOPE)).astype(BF16)


def half_row(block, odd):
    lane = lax.broadcasted_iota(jnp.int32, block.shape, 1)
    wide = block.astype(F32)
    if odd:
        wide = pltpu.roll(wide, LANES // 2, 1)
    return jnp.where(lane < LANES // 2, wide, 0.0)


def plane_of_message(ref, chans, row):
    return ref[32 * (row // 4) : 32 * (row // 4) + chans, cols(row % 4)]


def spread_top(block, half):
    unit = spread(
        LANES,
        2 * LANES,
        lambda e: LANES * ((e % 64) // 32) + 2 * (e % 32),
        lambda e: (e // 64) == half,
    )
    return dot(block, unit).astype(BF16)


def section3_kernel(top_ref, up_ref, down_ref, own_ref, weights_ref, out_ref, wide, stacked, terms):
    @pl.when(on_segment(3))
    def _():
        planes = [up_ref[:, 256:384], top_ref[...], down_ref[:, 256:384]]
        for place, block in enumerate(planes):
            for half in range(2):
                wide[64 * half : 64 * half + 64, cols(2 * place, 2)] = spread_top(block, half)
        stack_moved(lambda row: wide[:, cols(row)], stacked, C4, 6, (0, 1, 2))
        terms[...] = dot(weights_ref[...], stacked[...])
        unit = spread(LANES, LANES, lambda e: 2 * e, lambda e: e < 64)
        last = is_last_block()
        for cell_z in range(-1, 3):
            for cell_y in range(4):
                total = None
                for tap_z, place_z in taps_of(cell_z, -1, 1):
                    for tap_y, place_y in taps_of(cell_y, 0, 1):
                        first = C3 * (3 * tap_z + tap_y)
                        part = terms[first : first + C3, cols(2 * (place_z + 1) + place_y)]
                        total = part if total is None else total + part
                if cell_z == -1:
                    mask = up_ref[:, cols(cell_y // 2)]
                elif cell_z == 2:
                    mask = down_ref[:, cols(cell_y // 2)]
                else:
                    mask = own_ref[:, cols(2 * cell_z + cell_y // 2)]
                result = sloped(total, half_row(mask, cell_y % 2))
                if cell_z == 2:
                    result = jnp.where(last, jnp.zeros_like(result), result)
                out_ref[:, cols(4 * (cell_z + 1) + cell_y)] = dot(result, unit).astype(BF16)


def section2_kernel(grad_ref, up_ref, down_ref, own_ref, weights_ref, out_ref, stacked, terms):
    @pl.when(on_segment(2))
    def _():
        stack_moved(lambda row: grad_ref[:, cols(row)], stacked, C3, 16, (0, 1, 2))
        terms[...] = dot(weights_ref[:288, :192], stacked[...])
        last = is_last_block()
        for cell_z in range(-1, 5):
            for cell_y in range(8):
                total = None
                for tap_z, place_z in taps_of(cell_z, -1, 2):
                    for tap_y, place_y in taps_of(cell_y, 0, 3):
                        first = C2 * (3 * tap_z + tap_y)
                        part = terms[first : first + C2, cols(4 * (place_z + 1) + place_y)]
                        total = part if total is None else total + part
                if cell_z == -1:
                    mask = plane_of_message(up_ref, C2, cell_y)
                elif cell_z == 4:
                    mask = plane_of_message(down_ref, C2, cell_y)
                else:
                    mask = own_ref[:, cols(8 * cell_z + cell_y)]
                result = sloped(total, mask.astype(F32))
                if cell_z == 4:
                    result = jnp.where(last, jnp.zeros_like(result), result)
                out_ref[:, cols(8 * (cell_z + 1) + cell_y)] = result


def weights2_kernel(scale, grad_ref, up_ref, down_ref, own_ref, out_ref, stacked, acts):
    @pl.when(on_segment(2))
    def _():
        stack_moved(lambda row: grad_ref[:, cols(4 + row)], stacked, C3, 8, (0, 1, 2))
        for tap_z in range(3):
            for tap_y in range(3):
                first = C2 * (3 * tap_z + tap_y)
                for place_z in range(2):
                    for place_y in range(4):
                        plane, row = 2 * place_z + tap_z, 2 * place_y + tap_y
                        if row == 8:
                            block = jnp.zeros((C2, LANES), BF16)
                        elif plane == 4:
                            block = plane_of_message(down_ref, C2, row)
                        else:
                            block = own_ref[:, cols(8 * plane + row)]
                        acts[first : first + C2, cols(4 * place_z + place_y)] = block
        out_ref[...] = dot_rows(stacked[...], acts[...]) * scale


def fine_acts(chans, up_ref, down_ref, own_ref, plane, row):
    if plane == -1:
        return plane_of_message(up_ref, chans, row)
    if plane == 4:
        return plane_of_message(down_ref, chans, row)
    return own_ref[:chans, cols(8 * plane + row)]


def section01_kernel(
    scale1,
    scale0,
    grad0_ref,
    grad1_ref,
    up_ref,
    down_ref,
    own_ref,
    next_own_ref,
    next_weights_ref,
    out_ref,
    stacked,
    terms,
    result,
    moved,
    acts0,
    acts1,
):
    @pl.when(on_segment(0))
    def _():
        stack_moved(lambda row: grad0_ref[:, cols(row)], stacked, C2, 48, (-1, 0, 1))
        terms[...] = dot(next_weights_ref[:144, :96], stacked[...])
        edge = jnp.zeros((C1, LANES), F32)
        for plane in range(4):
            sums = []
            for tap_y in range(3):
                total = None
                for tap_z in range(3):
                    first = C1 * (3 * tap_z + tap_y)
                    part = terms[first : first + C1, cols(8 * (plane + 2 - tap_z), 8)]
                    total = part if total is None else total + part
                sums.append(total)
            later = jnp.concatenate([sums[0][:, LANES:], edge], 1)
            earlier = jnp.concatenate([edge, sums[2][:, : 7 * LANES]], 1)
            mask = next_own_ref[:C1, cols(8 * plane, 8)].astype(F32)
            result[:, cols(8 * plane, 8)] = sloped(sums[1] + later + earlier, mask)
        none = jnp.zeros((C1, LANES), BF16)
        for place, distance in enumerate((-1, 0, 1)):
            for plane in range(4):
                for row in range(8):
                    block = result[:, cols(8 * plane + row)]
                    block = moved_lanes(block, distance) if distance else block
                    for tap_y in range(3):
                        first = C1 * (3 * tap_y + place)
                        target = row + tap_y - 1
                        if 0 <= target < 8:
                            moved[first : first + C1, cols(8 * plane + target)] = block
                    if row == 0:
                        moved[C1 * (6 + place) : C1 * (7 + place), cols(8 * plane)] = none
                    if row == 7:
                        moved[C1 * place : C1 * (place + 1), cols(8 * plane + 7)] = none
        for tap_z in range(3):
            for plane in range(4):
                for row in range(8):
                    acts0[C1 * tap_z : C1 * (tap_z + 1), cols(8 * plane + row)] = fine_acts(
                        C1, up_ref, down_ref, own_ref, plane + tap_z - 1, row
                    )
        out_ref[:48, :] = dot_rows(acts0[...], moved[...]) * scale0
        out_ref[48:, :] = jnp.zeros((48, 144), F32)

    @pl.when(on_segment(1))
    def _():
        none = jnp.zeros((C1, LANES), BF16)
        stack_moved(lambda row: grad1_ref[:, cols(8 + row)], stacked, C2, 32, (-1, 0, 1))
        for tap_z in range(3):
            for tap_y in range(3):
                first = C1 * (3 * tap_z + tap_y)
                for plane in range(4):
                    for row in range(8):
                        source = row + tap_y - 1
                        block = none
                        if 0 <= source < 8:
                            block = fine_acts(
                                C1, up_ref, down_ref, own_ref, plane + tap_z - 1, source
                            )
                        acts1[first : first + C1, cols(8 * plane + row)] = block
        out_ref[...] = dot_rows(stacked[:, :4096], acts1[...]) * scale1


def weights3_kernel(scale, places, blocks_ref, out_ref, wide, stacked, acts):
    @pl.when(on_segment(3))
    def _():
        me = lax.axis_index("space")
        count = len(places)
        for block in range(count):
            if count == 1:
                held = blocks_ref[0]
            else:
                wanted = lax.bitwise_xor(me, block)
                position = 0
                for bit, value in places_bits(places):
                    position = position + value * lax.rem(lax.div(wanted, bit), 2)
                held = blocks_ref[position]
            for half in range(2):
                wide[64 * half : 64 * half + 64, cols(2 * block, 2)] = spread_top(
                    held[:, 768:896], half
                )
            rows = [half_row(held[:, cols(r // 2)], r % 2).astype(BF16) for r in range(12)]
            for tap_z in range(3):
                for tap_y in range(3):
                    first = C3 * (3 * tap_z + tap_y)
                    for place_y in range(2):
                        row = 2 * place_y + tap_y
                        source = jnp.zeros_like(rows[0]) if row == 4 else rows[4 * tap_z + row]
                        acts[first : first + C3, cols(2 * block + place_y)] = source
        stack_moved(lambda row: wide[:, cols(row)], stacked, C4, 2 * count, (0, 1, 2))
        out_ref[...] = dot_rows(stacked[...], acts[...]) * scale


def places_bits(places):
    count = len(places)
    bits = []
    bit = 1
    while bit < count:
        bits.append((bit, places.index(bit)))
        bit *= 2
    return bits


def call(kernel, outs, scratch, *args, flops):
    shape = jax.ShapeDtypeStruct(*outs)
    moved = sum(a.size * a.dtype.itemsize for a in args) + shape.size * shape.dtype.itemsize
    return pl.pallas_call(
        kernel,
        out_shape=shape,
        scratch_shapes=[pltpu.VMEM(*entry) for entry in scratch],
        compiler_params=pltpu.CompilerParams(vmem_limit_bytes=VMEM_LIMIT),
        cost_estimate=pl.CostEstimate(flops=flops, bytes_accessed=moved, transcendentals=0),
    )(*args)


def fine_message(plane):
    return jnp.concatenate([plane[:, :512], plane[:, 512:]], 0)


def fine_layout(row, chans):
    acts = row[: chans * 4096].reshape(chans, 4096)
    return jnp.pad(acts, ((0, 32 - chans), (0, 0)))


def fine_start(row, top, chans):
    own = fine_layout(row, chans)
    up = fine_message(own[:, 3072:])
    down = fine_message(own[:, :1024])
    return up, down, jnp.zeros((64, 512), BF16), own


def deep_start(row, top):
    own = row[:32768].reshape(64, 512)
    rest = jnp.zeros((64, 128), BF16)
    up = jnp.concatenate([own[:, 256:], top, rest], 1)
    down = jnp.concatenate([own[:, :256], top, rest], 1)
    return up, down, own, jnp.zeros((32, 4096), BF16)


def by_tap(weights, chan_out, chan_in):
    taps = weights[: 27 * chan_out * chan_in].reshape(9, 3, chan_out, chan_in)
    grouped = jnp.transpose(taps, (0, 3, 1, 2)).reshape(9 * chan_in, 3 * chan_out)
    return jnp.pad(grouped, ((0, 576 - 9 * chan_in), (0, 384 - 3 * chan_out)))


def pairs_of(segments, route):
    total = lax.axis_size("segment")
    count = lax.axis_size("space")
    return [
        (a * total + s, b * total + s) for a, b in route(count) for s in segments
    ]


def over_space(block, segments, route):
    return lax.ppermute(block, ("space", "segment"), pairs_of(segments, route))


def summed(block, segments):
    count = lax.axis_size("space")
    if count & (count - 1):
        return lax.psum(block, "space")
    bit = 1
    while bit < count:
        block = block + over_space(
            block, segments, lambda n, bit=bit: [(i, i ^ bit) for i in range(n)]
        )
        bit *= 2
    return block


def flat_row(ordered, room):
    flat = ordered.reshape(-1)
    return jnp.pad(flat, (0, room - flat.shape[0]))[None]


def shards(saved_inputs, conv_weights, top_gradient):
    segment = lax.axis_index("segment")
    count = lax.axis_size("space")
    room = conv_weights.shape[1]
    row = saved_inputs[0]
    weights = conv_weights[0]
    scales = [1.0 / math.sqrt(count * cells) for cells in (4096, 4096, 512, 64)]
    top = top_gradient.reshape(C4, 64)
    top = jnp.concatenate([top[:64], top[64:]], 1)

    up, down, own3, own = lax.switch(
        segment,
        [
            functools.partial(fine_start, chans=C0),
            functools.partial(fine_start, chans=C1),
            functools.partial(fine_start, chans=C2),
            deep_start,
        ],
        row,
        top,
    )
    up = over_space(up, range(4), lambda n: [(i, i + 1) for i in range(n - 1)])
    down = over_space(down, range(4), lambda n: [(i + 1, i) for i in range(n - 1)])
    taps = lax.switch(
        segment,
        [
            lambda w: jnp.zeros((576, 384), BF16),
            lambda w: by_tap(w, C2, C1),
            lambda w: by_tap(w, C3, C2),
            lambda w: by_tap(w, C4, C3),
        ],
        weights,
    )
    next_own = lax.ppermute(own, "segment", [(1, 0)])
    next_taps = lax.ppermute(taps, "segment", [(1, 0)])

    grad2 = call(
        section3_kernel,
        ((64, 2048), BF16),
        [((128, 768), BF16), ((384, 768), BF16), ((576, 768), F32)],
        top,
        up,
        down,
        own3,
        taps,
        flops=2 * 576 * 384 * 768,
    )
    grad2 = lax.ppermute(grad2, "segment", [(3, 2)])
    grad1 = call(
        section2_kernel,
        ((32, 6144), BF16),
        [((192, 2048), BF16), ((288, 2048), F32)],
        grad2,
        up,
        down,
        own,
        taps,
        flops=2 * 288 * 192 * 2048,
    )
    grad1_first = lax.ppermute(grad1, "segment", [(2, 0)])
    local2 = call(
        functools.partial(weights2_kernel, scales[2]),
        ((192, 288), F32),
        [((192, 1024), BF16), ((288, 1024), BF16)],
        grad2,
        up,
        down,
        own,
        flops=2 * 288 * 192 * 1024,
    )
    grad1_second = lax.ppermute(grad1, "segment", [(2, 1)])
    local01 = call(
        functools.partial(section01_kernel, scales[1], scales[0]),
        ((96, 144), F32),
        [
            ((96, 6144), BF16),
            ((144, 6144), F32),
            ((16, 4096), BF16),
            ((144, 4096), BF16),
            ((48, 4096), BF16),
            ((144, 4096), BF16),
        ],
        grad1_first,
        grad1_second,
        up,
        down,
        own,
        next_own,
        next_taps,
        flops=2 * 144 * 96 * 6144,
    )

    blocks = jnp.concatenate([own3, down[:, :256], top], 1)[None]
    places = [0]
    if count <= GATHER_LIMIT and not count & (count - 1):
        bit = count // 2
        while bit:
            received = over_space(
                blocks, [3], lambda n, bit=bit: [(i, i ^ bit) for i in range(n)]
            )
            blocks = jnp.concatenate([blocks, received], 0)
            places = places + [place ^ bit for place in places]
            bit //= 2
    held = len(places)
    sum3 = call(
        functools.partial(weights3_kernel, scales[3], places),
        ((384, 576), F32),
        [((128, 256 * held), BF16), ((384, 256 * held), BF16), ((576, 256 * held), BF16)],
        blocks,
        flops=2 * 384 * 576 * 256 * held,
    )
    if held < count:
        sum3 = summed(sum3, [3])
    sum2 = summed(local2, [2])
    sum01 = summed(local01, [0, 1])

    def finish0(sum01, sum2, sum3):
        parts = sum01[:48].reshape(3, 16, 3, 3, C1)[:, :C0]
        return flat_row(jnp.transpose(parts, (0, 2, 3, 4, 1)), room)

    def finish(total, chan_out, chan_in):
        parts = total.reshape(3, chan_out, 9, chan_in)
        return flat_row(jnp.transpose(parts, (2, 0, 1, 3)), room)

    return lax.switch(
        segment,
        [
            finish0,
            lambda a, b, c: finish(a, C2, C1),
            lambda a, b, c: finish(b, C3, C2),
            lambda a, b, c: finish(c, C4, C3),
        ],
        sum01,
        sum2,
        sum3,
    )


def solution(mesh):
    return jax.shard_map(
        shards,
        mesh=mesh,
        in_specs=(P("segment", "space"), P("segment", None), P(None, "space", None, None)),
        out_specs=P("segment", None),
        check_vma=False,
    )
```

```python
import functools
import math

import jax
import jax.numpy as jnp
from jax import lax
from jax.experimental import pallas as pl
from jax.experimental.pallas import tpu as pltpu
from jax.sharding import PartitionSpec as P

C0, C1, C2, C3, C4 = 4, 16, 32, 64, 128
LANES = 128
SLOPE = 0.3
BF16 = jnp.bfloat16
F32 = jnp.float32
GATHER_LIMIT = 8
VMEM_LIMIT = 48 * 1024 * 1024


def on_segment(index):
    return lax.axis_index("segment") == index


def is_last_block():
    return lax.axis_index("space") == lax.axis_size("space") - 1


def cols(row, count=1):
    return slice(LANES * row, LANES * (row + count))


def moved_lanes(block, distance):
    lane = lax.broadcasted_iota(jnp.int32, block.shape, 1)
    rolled = pltpu.roll(block.astype(F32), distance % LANES, 1)
    kept = lane >= distance if distance > 0 else lane < LANES + distance
    return jnp.where(kept, rolled, 0.0).astype(BF16)


def stack_moved(read, target, chans, rows, distances):
    for row in range(rows):
        block = read(row)
        for place, distance in enumerate(distances):
            moved = moved_lanes(block, distance) if distance else block
            target[place * chans : (place + 1) * chans, cols(row)] = moved


def spread(rows_in, rows_out, source, bound):
    entry = lax.broadcasted_iota(jnp.int32, (rows_in, rows_out), 0)
    place = lax.broadcasted_iota(jnp.int32, (rows_in, rows_out), 1)
    return jnp.where((place == source(entry)) & bound(entry), 1.0, 0.0).astype(BF16)


def taps_of(cell, low, high):
    if cell % 2:
        pairs = [(1, (cell - 1) // 2)]
    else:
        pairs = [(0, cell // 2), (2, cell // 2 - 1)]
    return [(tap, place) for tap, place in pairs if low <= place <= high]


def dot_rows(left, right):
    return lax.dot_general(left, right, (((1,), (1,)), ((), ())), preferred_element_type=F32)


def dot(left, right):
    return jnp.dot(left, right, preferred_element_type=F32)


def sloped(total, activation):
    return (total * jnp.where(activation > 0, 1.0, SLOPE)).astype(BF16)


def half_row(block, odd):
    lane = lax.broadcasted_iota(jnp.int32, block.shape, 1)
    wide = block.astype(F32)
    if odd:
        wide = pltpu.roll(wide, LANES // 2, 1)
    return jnp.where(lane < LANES // 2, wide, 0.0)


def plane_of_message(ref, chans, row):
    return ref[32 * (row // 4) : 32 * (row // 4) + chans, cols(row % 4)]


def spread_top(block):
    unit = spread(64, 2 * LANES, lambda e: LANES * (e // 32) + 2 * (e % 32), lambda e: e >= 0)
    turned = (((0,), (0,)), ((), ()))
    return lax.dot_general(block, unit, turned, preferred_element_type=F32).astype(BF16)


def section3_kernel(own_ref, up_ref, down_ref, weights_ref, out_ref, wide, stacked, terms):
    @pl.when(on_segment(3))
    def _():
        for place, ref in enumerate((up_ref, own_ref, down_ref)):
            wide[:, cols(2 * place, 2)] = spread_top(ref[:, cols(4)])
        stack_moved(lambda row: wide[:, cols(row)], stacked, C4, 6, (0, 1, 2))
        terms[...] = dot(weights_ref[...], stacked[...])
        unit = spread(LANES, LANES, lambda e: 2 * e, lambda e: e < 64)
        last = is_last_block()
        for cell_z in range(-1, 3):
            for cell_y in range(4):
                total = None
                for tap_z, place_z in taps_of(cell_z, -1, 1):
                    for tap_y, place_y in taps_of(cell_y, 0, 1):
                        first = C3 * (3 * tap_z + tap_y)
                        part = terms[first : first + C3, cols(2 * (place_z + 1) + place_y)]
                        total = part if total is None else total + part
                if cell_z == -1:
                    mask = up_ref[:, cols(2 + cell_y // 2)]
                elif cell_z == 2:
                    mask = down_ref[:, cols(cell_y // 2)]
                else:
                    mask = own_ref[:, cols(2 * cell_z + cell_y // 2)]
                result = sloped(total, half_row(mask, cell_y % 2))
                if cell_z == 2:
                    result = jnp.where(last, jnp.zeros_like(result), result)
                out_ref[:, cols(4 * (cell_z + 1) + cell_y)] = dot(result, unit).astype(BF16)


def section21_kernel(
    grad_ref,
    up_ref,
    down_ref,
    own_ref,
    weights_ref,
    next_own_ref,
    next_weights_ref,
    out1_ref,
    out0_ref,
    stacked,
    terms,
    middle,
    next_stacked,
    next_terms,
):
    @pl.when(on_segment(2))
    def _():
        stack_moved(lambda row: grad_ref[:, cols(row)], stacked, C3, 16, (0, 1, 2))
        terms[...] = dot(weights_ref[:288, :192], stacked[...])
        last = is_last_block()
        for cell_z in range(-1, 5):
            for cell_y in range(8):
                total = None
                for tap_z, place_z in taps_of(cell_z, -1, 2):
                    for tap_y, place_y in taps_of(cell_y, 0, 3):
                        first = C2 * (3 * tap_z + tap_y)
                        part = terms[first : first + C2, cols(4 * (place_z + 1) + place_y)]
                        total = part if total is None else total + part
                if cell_z == -1:
                    mask = plane_of_message(up_ref, C2, cell_y)
                elif cell_z == 4:
                    mask = plane_of_message(down_ref, C2, cell_y)
                else:
                    mask = own_ref[:, cols(8 * cell_z + cell_y)]
                result = sloped(total, mask.astype(F32))
                if cell_z == 4:
                    result = jnp.where(last, jnp.zeros_like(result), result)
                middle[:, cols(8 * (cell_z + 1) + cell_y)] = result
                if 0 <= cell_z < 4:
                    out1_ref[:, cols(8 * cell_z + cell_y)] = result
        stack_moved(lambda row: middle[:, cols(row)], next_stacked, C2, 48, (-1, 0, 1))
        next_terms[...] = dot(next_weights_ref[:, :96], next_stacked[...])
        edge = jnp.zeros((C1, LANES), F32)
        for plane in range(4):
            sums = []
            for tap_y in range(3):
                total = None
                for tap_z in range(3):
                    first = C1 * (3 * tap_z + tap_y)
                    part = next_terms[first : first + C1, cols(8 * (plane + 2 - tap_z), 8)]
                    total = part if total is None else total + part
                sums.append(total)
            later = jnp.concatenate([sums[0][:, LANES:], edge], 1)
            earlier = jnp.concatenate([edge, sums[2][:, : 7 * LANES]], 1)
            mask = next_own_ref[:, cols(8 * plane, 8)].astype(F32)
            out0_ref[:, cols(8 * plane, 8)] = sloped(sums[1] + later + earlier, mask)


def weights2_kernel(scale, grad_ref, up_ref, down_ref, own_ref, out_ref, stacked, acts):
    @pl.when(on_segment(2))
    def _():
        stack_moved(lambda row: grad_ref[:, cols(4 + row)], stacked, C3, 8, (0, 1, 2))
        for tap_z in range(3):
            for tap_y in range(3):
                first = C2 * (3 * tap_z + tap_y)
                for place_z in range(2):
                    for place_y in range(4):
                        plane, row = 2 * place_z + tap_z, 2 * place_y + tap_y
                        if row == 8:
                            block = jnp.zeros((C2, LANES), BF16)
                        elif plane == 4:
                            block = plane_of_message(down_ref, C2, row)
                        else:
                            block = own_ref[:, cols(8 * plane + row)]
                        acts[first : first + C2, cols(4 * place_z + place_y)] = block
        out_ref[:288, :] = dot_rows(acts[...], stacked[:128, :]) * scale
        out_ref[288:, :64] = dot_rows(acts[:144, :], stacked[128:, :]) * scale
        out_ref[288:, 64:] = dot_rows(acts[144:, :], stacked[128:, :]) * scale


def fine_acts(chans, up_ref, down_ref, own_ref, plane, row):
    if plane == -1:
        return plane_of_message(up_ref, chans, row)
    if plane == 4:
        return plane_of_message(down_ref, chans, row)
    return own_ref[:chans, cols(8 * plane + row)]


def weights01_kernel(
    scale1, scale0, grad0_ref, grad1_ref, up_ref, down_ref, own_ref, out_ref, stacked, acts
):
    none = jnp.zeros((C1, LANES), BF16)

    @pl.when(on_segment(0))
    def _():
        for place, distance in enumerate((-1, 0, 1)):
            for plane in range(4):
                for row in range(8):
                    block = grad0_ref[:, cols(8 * plane + row)]
                    block = moved_lanes(block, distance) if distance else block
                    for tap_y in range(3):
                        first = C1 * (3 * tap_y + place)
                        target = row + tap_y - 1
                        if 0 <= target < 8:
                            acts[first : first + C1, cols(8 * plane + target)] = block
                    if row == 0:
                        acts[C1 * (6 + place) : C1 * (7 + place), cols(8 * plane)] = none
                    if row == 7:
                        acts[C1 * place : C1 * (place + 1), cols(8 * plane + 7)] = none
        for tap_z in range(3):
            for plane in range(4):
                for row in range(8):
                    stacked[C1 * tap_z : C1 * (tap_z + 1), cols(8 * plane + row)] = fine_acts(
                        C1, up_ref, down_ref, own_ref, plane + tap_z - 1, row
                    )
        out_ref[:, :48] = dot_rows(acts[...], stacked[:48, :]) * scale0
        out_ref[:, 48:] = jnp.zeros((144, 80), F32)

    @pl.when(on_segment(1))
    def _():
        stack_moved(lambda row: grad1_ref[:, cols(row)], stacked, C2, 32, (-1, 0, 1))
        for tap_z in range(3):
            for tap_y in range(3):
                first = C1 * (3 * tap_z + tap_y)
                for plane in range(4):
                    for row in range(8):
                        source = row + tap_y - 1
                        block = none
                        if 0 <= source < 8:
                            block = fine_acts(
                                C1, up_ref, down_ref, own_ref, plane + tap_z - 1, source
                            )
                        acts[first : first + C1, cols(8 * plane + row)] = block
        out_ref[:, :96] = dot_rows(acts[...], stacked[...]) * scale1
        out_ref[:, 96:] = jnp.zeros((144, 32), F32)


def weights3_kernel(scale, places, blocks_ref, down_ref, out_ref, wide, stacked, acts):
    @pl.when(on_segment(3))
    def _():
        me = lax.axis_index("space")
        count = len(places)

        def held(block):
            wanted = lax.bitwise_xor(me, block)
            position = 0
            for bit, value in places_bits(places):
                position = position + value * lax.rem(lax.div(wanted, bit), 2)
            return blocks_ref[position]

        zero = jnp.zeros((64, LANES), BF16)
        for block in range(count):
            here = blocks_ref[0] if count == 1 else held(block)
            wide[:, cols(2 * block, 2)] = spread_top(here[:, cols(4)])
            rows = [half_row(here[:, cols(r // 2)], r % 2).astype(BF16) for r in range(8)]
            if count == 1:
                after = down_ref[:, : 2 * LANES]
            elif block + 1 < count:
                after = held(block + 1)[:, : 2 * LANES]
            else:
                after = None
            for r in range(4):
                rows.append(
                    zero if after is None else half_row(after[:, cols(r // 2)], r % 2).astype(BF16)
                )
            for tap_z in range(3):
                for tap_y in range(3):
                    first = C3 * (3 * tap_z + tap_y)
                    for place_y in range(2):
                        row = 2 * place_y + tap_y
                        source = zero if row == 4 else rows[4 * tap_z + row]
                        acts[first : first + C3, cols(2 * block + place_y)] = source
        stack_moved(lambda row: wide[:, cols(row)], stacked, C4, 2 * count, (0, 1, 2))
        out_ref[...] = dot_rows(stacked[...], acts[...]) * scale


def places_bits(places):
    count = len(places)
    bits = []
    bit = 1
    while bit < count:
        bits.append((bit, places.index(bit)))
        bit *= 2
    return bits


def call(kernel, outs, scratch, *args, flops):
    shapes = [jax.ShapeDtypeStruct(*entry) for entry in outs]
    moved = sum(a.size * a.dtype.itemsize for a in [*args, *shapes])
    return pl.pallas_call(
        kernel,
        out_shape=shapes,
        scratch_shapes=[pltpu.VMEM(*entry) for entry in scratch],
        compiler_params=pltpu.CompilerParams(vmem_limit_bytes=VMEM_LIMIT),
        cost_estimate=pl.CostEstimate(flops=flops, bytes_accessed=moved, transcendentals=0),
    )(*args)


def padded(block, rows, columns):
    return jnp.pad(block, ((0, rows - block.shape[0]), (0, columns - block.shape[1])))


def fine_message(plane):
    plane = padded(plane, 32, 1024)
    return jnp.concatenate([plane[:, :512], plane[:, 512:]], 0)


def by_tap(weights, chan_out, chan_in):
    groups = []
    size = 9 * chan_out * chan_in
    for tap_z in range(3):
        taps = weights[0, tap_z * size : (tap_z + 1) * size].reshape(3, 3, chan_out, chan_in)
        groups.append(jnp.transpose(taps, (0, 3, 1, 2)).reshape(3 * chan_in, 3 * chan_out))
    return jnp.concatenate(groups, 0)


def prepared(section, saved, weights):
    deep_taps = jnp.zeros((576, 384), BF16)
    fine_taps = jnp.zeros((144, 128), BF16)
    own2 = jnp.zeros((32, 4096), BF16)
    own01 = jnp.zeros((16, 4096), BF16)
    up = down = jnp.zeros((64, 512), BF16)
    if section == 3:
        deep_taps = by_tap(weights, C4, C3)
    else:
        chans = (C0, C1, C2)[section]
        own = saved[0, : chans * 4096].reshape(chans, 4096)
        up, down = fine_message(own[:, 3072:]), fine_message(own[:, :1024])
        if section == 2:
            own2 = own
            deep_taps = padded(by_tap(weights, C3, C2), 576, 384)
        else:
            own01 = padded(own, 16, 4096)
        if section == 1:
            fine_taps = padded(by_tap(weights, C2, C1), 144, 128)
    return deep_taps, fine_taps, own2, own01, up, down


def pairs_of(segments, route):
    total = lax.axis_size("segment")
    count = lax.axis_size("space")
    return [
        (a * total + s, b * total + s) for a, b in route(count) for s in segments
    ]


def over_space(block, segments, route):
    return lax.ppermute(block, ("space", "segment"), pairs_of(segments, route))


def summed(block, segments):
    count = lax.axis_size("space")
    if count & (count - 1):
        return lax.psum(block, "space")
    bit = 1
    while bit < count:
        block = block + over_space(
            block, segments, lambda n, bit=bit: [(i, i ^ bit) for i in range(n)]
        )
        bit *= 2
    return block


def flat_row(ordered, room):
    flat = ordered.reshape(-1)
    return jnp.pad(flat, (0, room - flat.shape[0]))[None]


def shards(saved_inputs, conv_weights, top_gradient):
    segment = lax.axis_index("segment")
    count = lax.axis_size("space")
    room = conv_weights.shape[1]
    scales = [1.0 / math.sqrt(count * cells) for cells in (4096, 4096, 512, 64)]

    def later(n):
        return [(i, i + 1) for i in range(n - 1)]

    def sooner(n):
        return [(i + 1, i) for i in range(n - 1)]

    top = jnp.transpose(top_gradient[:, 0], (1, 2, 0)).reshape(64, C4)
    deep = jnp.concatenate([saved_inputs[0, :32768].reshape(64, 512), top], 1)
    deep_up = over_space(deep, [3], later)
    deep_down = over_space(deep, [3], sooner)
    deep_taps, fine_taps, own2, own01, up, down = lax.switch(
        segment,
        [functools.partial(prepared, section) for section in range(4)],
        saved_inputs,
        conv_weights,
    )
    up = over_space(up, [0, 1, 2], later)
    down = over_space(down, [0, 1, 2], sooner)
    next_own = lax.ppermute(own01, "segment", [(1, 2)])
    next_taps = lax.ppermute(fine_taps, "segment", [(1, 2)])

    (grad2,) = call(
        section3_kernel,
        [((64, 2048), BF16)],
        [((128, 768), BF16), ((384, 768), BF16), ((576, 768), F32)],
        deep,
        deep_up,
        deep_down,
        deep_taps,
        flops=2 * 576 * 384 * 768,
    )
    grad2 = lax.ppermute(grad2, "segment", [(3, 2)])
    grad1, grad0 = call(
        section21_kernel,
        [((32, 4096), BF16), ((16, 4096), BF16)],
        [
            ((192, 2048), BF16),
            ((288, 2048), F32),
            ((32, 6144), BF16),
            ((96, 6144), BF16),
            ((144, 6144), F32),
        ],
        grad2,
        up,
        down,
        own2,
        deep_taps,
        next_own,
        next_taps,
        flops=2 * 288 * 192 * 2048,
    )
    grad0 = lax.ppermute(grad0, "segment", [(2, 0)])
    grad1 = lax.ppermute(grad1, "segment", [(2, 1)])
    (local2,) = call(
        functools.partial(weights2_kernel, scales[2]),
        [((432, 128), F32)],
        [((192, 1024), BF16), ((288, 1024), BF16)],
        grad2,
        up,
        down,
        own2,
        flops=2 * 288 * 192 * 1024,
    )
    (local01,) = call(
        functools.partial(weights01_kernel, scales[1], scales[0]),
        [((144, 128), F32)],
        [((96, 4096), BF16), ((144, 4096), BF16)],
        grad0,
        grad1,
        up,
        down,
        own01,
        flops=2 * 144 * 96 * 6144,
    )

    blocks = deep[None]
    places = [0]
    if count <= GATHER_LIMIT and not count & (count - 1):
        bit = count // 2
        while bit:
            received = over_space(
                blocks, [3], lambda n, bit=bit: [(i, i ^ bit) for i in range(n)]
            )
            blocks = jnp.concatenate([blocks, received], 0)
            places = places + [place ^ bit for place in places]
            bit //= 2
    held = len(places)
    (sum3,) = call(
        functools.partial(weights3_kernel, scales[3], places),
        [((384, 576), F32)],
        [((128, 256 * held), BF16), ((384, 256 * held), BF16), ((576, 256 * held), BF16)],
        blocks,
        deep_down,
        flops=2 * 384 * 576 * 256 * held,
    )
    if held < count:
        sum3 = summed(sum3, [3])
    sum2 = summed(local2, [2])
    sum01 = summed(local01, [0, 1])

    def finish0(sum01, sum2, sum3):
        parts = sum01[:, :48].reshape(3, 3, C1, 3, 16)[..., :C0]
        return flat_row(jnp.transpose(parts, (3, 0, 1, 2, 4)), room)

    def finish1(sum01, sum2, sum3):
        parts = sum01[:, :96].reshape(9, C1, 3, C2)
        return flat_row(jnp.transpose(parts, (0, 2, 3, 1)), room)

    def finish2(sum01, sum2, sum3):
        two = sum2[:288].reshape(9, C2, 2, C3)
        one = jnp.transpose(sum2[288:].reshape(144, 2, C3), (1, 0, 2)).reshape(9, C2, 1, C3)
        return flat_row(jnp.transpose(jnp.concatenate([two, one], 2), (0, 2, 3, 1)), room)

    def finish3(sum01, sum2, sum3):
        parts = sum3.reshape(3, C4, 9, C3)
        return flat_row(jnp.transpose(parts, (2, 0, 1, 3)), room)

    return lax.switch(segment, [finish0, finish1, finish2, finish3], sum01, sum2, sum3)


def solution(mesh):
    return jax.shard_map(
        shards,
        mesh=mesh,
        in_specs=(P("segment", "space"), P("segment", None), P(None, "space", None, None)),
        out_specs=P("segment", None),
        check_vma=False,
    )
```

```python
import functools
import math

import jax
import jax.numpy as jnp
from jax import lax
from jax.experimental import pallas as pl
from jax.experimental.pallas import tpu as pltpu
from jax.sharding import PartitionSpec as P

C0, C1, C2, C3, C4 = 4, 16, 32, 64, 128
LANES = 128
SLOPE = 0.3
BF16 = jnp.bfloat16
F32 = jnp.float32
GATHER_LIMIT = 8
VMEM_LIMIT = 48 * 1024 * 1024


def on_segment(index):
    return lax.axis_index("segment") == index


def is_last_block():
    return lax.axis_index("space") == lax.axis_size("space") - 1


def cols(row, count=1):
    return slice(LANES * row, LANES * (row + count))


def moved_lanes(block, distance):
    lane = lax.broadcasted_iota(jnp.int32, block.shape, 1)
    rolled = pltpu.roll(block.astype(F32), distance % LANES, 1)
    kept = lane >= distance if distance > 0 else lane < LANES + distance
    return jnp.where(kept, rolled, 0.0).astype(BF16)


def stack_moved(read, target, chans, rows, distances):
    for row in range(rows):
        block = read(row)
        for place, distance in enumerate(distances):
            moved = moved_lanes(block, distance) if distance else block
            target[place * chans : (place + 1) * chans, cols(row)] = moved


def spread(rows_in, rows_out, source, bound):
    entry = lax.broadcasted_iota(jnp.int32, (rows_in, rows_out), 0)
    place = lax.broadcasted_iota(jnp.int32, (rows_in, rows_out), 1)
    return jnp.where((place == source(entry)) & bound(entry), 1.0, 0.0).astype(BF16)


def taps_of(cell, low, high):
    if cell % 2:
        pairs = [(1, (cell - 1) // 2)]
    else:
        pairs = [(0, cell // 2), (2, cell // 2 - 1)]
    return [(tap, place) for tap, place in pairs if low <= place <= high]


def dot_rows(left, right):
    return lax.dot_general(left, right, (((1,), (1,)), ((), ())), preferred_element_type=F32)


def dot(left, right):
    return jnp.dot(left, right, preferred_element_type=F32)


def sloped(total, activation):
    return (total * jnp.where(activation > 0, 1.0, SLOPE)).astype(BF16)


def half_row(block, odd):
    lane = lax.broadcasted_iota(jnp.int32, block.shape, 1)
    wide = block.astype(F32)
    if odd:
        wide = pltpu.roll(wide, LANES // 2, 1)
    return jnp.where(lane < LANES // 2, wide, 0.0)


def plane_of_message(ref, chans, row):
    return ref[32 * (row // 4) : 32 * (row // 4) + chans, cols(row % 4)]


def spread_top(block):
    unit = spread(64, 2 * LANES, lambda e: LANES * (e // 32) + 2 * (e % 32), lambda e: e >= 0)
    turned = (((0,), (0,)), ((), ()))
    return lax.dot_general(block, unit, turned, preferred_element_type=F32).astype(BF16)


def copy_rows(saved_ref, wide, chans, width):
    for chan in range(chans):
        source = saved_ref[:, chan * width : (chan + 1) * width]
        wide[chan : chan + 1, :width] = source.astype(F32)


def layout_kernel(saved_ref, top_ref, up_ref, down_ref, own2_ref, own01_ref, wide):
    def send(chans, place, plane, target_ref):
        for half in range(2):
            target_ref[32 * half : 32 * half + place, :512] = wide[
                :place, cols(8 * plane + 4 * half, 4)
            ].astype(BF16)

    @pl.when(on_segment(3))
    def _():
        copy_rows(saved_ref, wide, C3, 512)
        block = wide[:, :512].astype(BF16)
        for ref in (up_ref, down_ref):
            ref[:, :512] = block
            ref[:, 512:] = top_ref[...]

    for section, chans in enumerate((C0, C1, C2)):

        @pl.when(on_segment(section))
        def _(section=section, chans=chans):
            if section == 0:
                wide[:C1, :] = jnp.zeros((C1, 4096), F32)
            copy_rows(saved_ref, wide, chans, 4096)
            place = max(chans, C1)
            own_ref = own2_ref if section == 2 else own01_ref
            own_ref[...] = wide[:place, :].astype(BF16)
            send(chans, place, 3, up_ref)
            send(chans, place, 0, down_ref)


def section3_kernel(own_ref, up_ref, down_ref, weights_ref, out_ref, wide, stacked, terms):
    @pl.when(on_segment(3))
    def _():
        for place, ref in enumerate((up_ref, own_ref, down_ref)):
            wide[:, cols(2 * place, 2)] = spread_top(ref[:, cols(4)])
        stack_moved(lambda row: wide[:, cols(row)], stacked, C4, 6, (0, 1, 2))
        terms[...] = dot(weights_ref[...], stacked[...])
        unit = spread(LANES, LANES, lambda e: 2 * e, lambda e: e < 64)
        last = is_last_block()
        for cell_z in range(-1, 3):
            for cell_y in range(4):
                total = None
                for tap_z, place_z in taps_of(cell_z, -1, 1):
                    for tap_y, place_y in taps_of(cell_y, 0, 1):
                        first = C3 * (3 * tap_z + tap_y)
                        part = terms[first : first + C3, cols(2 * (place_z + 1) + place_y)]
                        total = part if total is None else total + part
                if cell_z == -1:
                    mask = up_ref[:, cols(2 + cell_y // 2)]
                elif cell_z == 2:
                    mask = down_ref[:, cols(cell_y // 2)]
                else:
                    mask = own_ref[:, cols(2 * cell_z + cell_y // 2)]
                result = sloped(total, half_row(mask, cell_y % 2))
                if cell_z == 2:
                    result = jnp.where(last, jnp.zeros_like(result), result)
                out_ref[:, cols(4 * (cell_z + 1) + cell_y)] = dot(result, unit).astype(BF16)


def section21_kernel(
    grad_ref,
    up_ref,
    down_ref,
    own_ref,
    weights_ref,
    next_own_ref,
    next_weights_ref,
    out1_ref,
    out0_ref,
    stacked,
    terms,
    middle,
    next_stacked,
    next_terms,
):
    @pl.when(on_segment(2))
    def _():
        stack_moved(lambda row: grad_ref[:, cols(row)], stacked, C3, 16, (0, 1, 2))
        terms[...] = dot(weights_ref[:288, :192], stacked[...])
        last = is_last_block()
        for cell_z in range(-1, 5):
            for cell_y in range(8):
                total = None
                for tap_z, place_z in taps_of(cell_z, -1, 2):
                    for tap_y, place_y in taps_of(cell_y, 0, 3):
                        first = C2 * (3 * tap_z + tap_y)
                        part = terms[first : first + C2, cols(4 * (place_z + 1) + place_y)]
                        total = part if total is None else total + part
                if cell_z == -1:
                    mask = plane_of_message(up_ref, C2, cell_y)
                elif cell_z == 4:
                    mask = plane_of_message(down_ref, C2, cell_y)
                else:
                    mask = own_ref[:, cols(8 * cell_z + cell_y)]
                result = sloped(total, mask.astype(F32))
                if cell_z == 4:
                    result = jnp.where(last, jnp.zeros_like(result), result)
                middle[:, cols(8 * (cell_z + 1) + cell_y)] = result
                if 0 <= cell_z < 4:
                    out1_ref[:, cols(8 * cell_z + cell_y)] = result
        stack_moved(lambda row: middle[:, cols(row)], next_stacked, C2, 48, (-1, 0, 1))
        next_terms[...] = dot(next_weights_ref[:, :96], next_stacked[...])
        edge = jnp.zeros((C1, LANES), F32)
        for plane in range(4):
            sums = []
            for tap_y in range(3):
                total = None
                for tap_z in range(3):
                    first = C1 * (3 * tap_z + tap_y)
                    part = next_terms[first : first + C1, cols(8 * (plane + 2 - tap_z), 8)]
                    total = part if total is None else total + part
                sums.append(total)
            later = jnp.concatenate([sums[0][:, LANES:], edge], 1)
            earlier = jnp.concatenate([edge, sums[2][:, : 7 * LANES]], 1)
            mask = next_own_ref[:, cols(8 * plane, 8)].astype(F32)
            out0_ref[:, cols(8 * plane, 8)] = sloped(sums[1] + later + earlier, mask)


def weights2_kernel(scale, grad_ref, up_ref, down_ref, own_ref, out_ref, stacked, acts):
    @pl.when(on_segment(2))
    def _():
        stack_moved(lambda row: grad_ref[:, cols(4 + row)], stacked, C3, 8, (0, 1, 2))
        for tap_z in range(3):
            for tap_y in range(3):
                first = C2 * (3 * tap_z + tap_y)
                for place_z in range(2):
                    for place_y in range(4):
                        plane, row = 2 * place_z + tap_z, 2 * place_y + tap_y
                        if row == 8:
                            block = jnp.zeros((C2, LANES), BF16)
                        elif plane == 4:
                            block = plane_of_message(down_ref, C2, row)
                        else:
                            block = own_ref[:, cols(8 * plane + row)]
                        acts[first : first + C2, cols(4 * place_z + place_y)] = block
        out_ref[:288, :] = dot_rows(acts[...], stacked[:128, :]) * scale
        out_ref[288:, :64] = dot_rows(acts[:144, :], stacked[128:, :]) * scale
        out_ref[288:, 64:] = dot_rows(acts[144:, :], stacked[128:, :]) * scale


def fine_acts(chans, up_ref, down_ref, own_ref, plane, row):
    if plane == -1:
        return plane_of_message(up_ref, chans, row)
    if plane == 4:
        return plane_of_message(down_ref, chans, row)
    return own_ref[:chans, cols(8 * plane + row)]


def weights01_kernel(
    scale1, scale0, grad0_ref, grad1_ref, up_ref, down_ref, own_ref, out_ref, stacked, acts
):
    none = jnp.zeros((C1, LANES), BF16)

    @pl.when(on_segment(0))
    def _():
        for place, distance in enumerate((-1, 0, 1)):
            for plane in range(4):
                for row in range(8):
                    block = grad0_ref[:, cols(8 * plane + row)]
                    block = moved_lanes(block, distance) if distance else block
                    for tap_y in range(3):
                        first = C1 * (3 * tap_y + place)
                        target = row + tap_y - 1
                        if 0 <= target < 8:
                            acts[first : first + C1, cols(8 * plane + target)] = block
                    if row == 0:
                        acts[C1 * (6 + place) : C1 * (7 + place), cols(8 * plane)] = none
                    if row == 7:
                        acts[C1 * place : C1 * (place + 1), cols(8 * plane + 7)] = none
        for tap_z in range(3):
            for plane in range(4):
                for row in range(8):
                    stacked[C1 * tap_z : C1 * (tap_z + 1), cols(8 * plane + row)] = fine_acts(
                        C1, up_ref, down_ref, own_ref, plane + tap_z - 1, row
                    )
        out_ref[:, :48] = dot_rows(acts[...], stacked[:48, :]) * scale0
        out_ref[:, 48:] = jnp.zeros((144, 80), F32)

    @pl.when(on_segment(1))
    def _():
        stack_moved(lambda row: grad1_ref[:, cols(row)], stacked, C2, 32, (-1, 0, 1))
        for tap_z in range(3):
            for tap_y in range(3):
                first = C1 * (3 * tap_z + tap_y)
                for plane in range(4):
                    for row in range(8):
                        source = row + tap_y - 1
                        block = none
                        if 0 <= source < 8:
                            block = fine_acts(
                                C1, up_ref, down_ref, own_ref, plane + tap_z - 1, source
                            )
                        acts[first : first + C1, cols(8 * plane + row)] = block
        out_ref[:, :96] = dot_rows(acts[...], stacked[...]) * scale1
        out_ref[:, 96:] = jnp.zeros((144, 32), F32)


def weights3_kernel(scale, places, blocks_ref, down_ref, out_ref, wide, stacked, acts):
    @pl.when(on_segment(3))
    def _():
        me = lax.axis_index("space")
        count = len(places)

        def held(block):
            wanted = lax.bitwise_xor(me, block)
            position = 0
            for bit, value in places_bits(places):
                position = position + value * lax.rem(lax.div(wanted, bit), 2)
            return blocks_ref[position]

        zero = jnp.zeros((64, LANES), BF16)
        for block in range(count):
            here = blocks_ref[0] if count == 1 else held(block)
            wide[:, cols(2 * block, 2)] = spread_top(here[:, cols(4)])
            rows = [half_row(here[:, cols(r // 2)], r % 2).astype(BF16) for r in range(8)]
            if count == 1:
                after = down_ref[:, : 2 * LANES]
            elif block + 1 < count:
                after = held(block + 1)[:, : 2 * LANES]
            else:
                after = None
            for r in range(4):
                rows.append(
                    zero if after is None else half_row(after[:, cols(r // 2)], r % 2).astype(BF16)
                )
            for tap_z in range(3):
                for tap_y in range(3):
                    first = C3 * (3 * tap_z + tap_y)
                    for place_y in range(2):
                        row = 2 * place_y + tap_y
                        source = zero if row == 4 else rows[4 * tap_z + row]
                        acts[first : first + C3, cols(2 * block + place_y)] = source
        stack_moved(lambda row: wide[:, cols(row)], stacked, C4, 2 * count, (0, 1, 2))
        out_ref[...] = dot_rows(stacked[...], acts[...]) * scale


def places_bits(places):
    count = len(places)
    bits = []
    bit = 1
    while bit < count:
        bits.append((bit, places.index(bit)))
        bit *= 2
    return bits


def call(kernel, outs, scratch, *args, flops):
    shapes = [jax.ShapeDtypeStruct(*entry) for entry in outs]
    moved = sum(a.size * a.dtype.itemsize for a in [*args, *shapes])
    return pl.pallas_call(
        kernel,
        out_shape=shapes,
        scratch_shapes=[pltpu.VMEM(*entry) for entry in scratch],
        compiler_params=pltpu.CompilerParams(vmem_limit_bytes=VMEM_LIMIT),
        cost_estimate=pl.CostEstimate(flops=flops, bytes_accessed=moved, transcendentals=0),
    )(*args)


def padded(block, rows, columns):
    return jnp.pad(block, ((0, rows - block.shape[0]), (0, columns - block.shape[1])))


def by_tap(weights, chan_out, chan_in):
    groups = []
    size = 9 * chan_out * chan_in
    for tap_z in range(3):
        taps = weights[0, tap_z * size : (tap_z + 1) * size].reshape(3, 3, chan_out, chan_in)
        groups.append(jnp.transpose(taps, (0, 3, 1, 2)).reshape(3 * chan_in, 3 * chan_out))
    return jnp.concatenate(groups, 0)


def tap_layouts(section, weights):
    deep_taps = jnp.zeros((576, 384), BF16)
    fine_taps = jnp.zeros((144, 128), BF16)
    if section == 3:
        deep_taps = by_tap(weights, C4, C3)
    if section == 2:
        deep_taps = padded(by_tap(weights, C3, C2), 576, 384)
    if section == 1:
        fine_taps = padded(by_tap(weights, C2, C1), 144, 128)
    return deep_taps, fine_taps


def pairs_of(segments, route):
    total = lax.axis_size("segment")
    count = lax.axis_size("space")
    return [
        (a * total + s, b * total + s) for a, b in route(count) for s in segments
    ]


def over_space(block, segments, route):
    return lax.ppermute(block, ("space", "segment"), pairs_of(segments, route))


def flat_row(ordered, room):
    flat = ordered.reshape(-1)
    return jnp.pad(flat, (0, room - flat.shape[0]))[None]


def shards(saved_inputs, conv_weights, top_gradient):
    segment = lax.axis_index("segment")
    count = lax.axis_size("space")
    room = conv_weights.shape[1]
    scales = [1.0 / math.sqrt(count * cells) for cells in (4096, 4096, 512, 64)]

    def later(n):
        return [(i, i + 1) for i in range(n - 1)]

    def sooner(n):
        return [(i + 1, i) for i in range(n - 1)]

    top = jnp.transpose(top_gradient[:, 0], (1, 2, 0)).reshape(64, C4)
    to_later, to_sooner, own2, own01 = call(
        layout_kernel,
        [((64, 640), BF16), ((64, 640), BF16), ((32, 4096), BF16), ((16, 4096), BF16)],
        [((64, 4096), F32)],
        saved_inputs,
        top,
        flops=0,
    )
    deep = to_later
    up = over_space(to_later, range(4), later)
    down = over_space(to_sooner, range(4), sooner)
    deep_taps, fine_taps = lax.switch(
        segment,
        [functools.partial(tap_layouts, section) for section in range(4)],
        conv_weights,
    )
    next_own = lax.ppermute(own01, "segment", [(1, 2)])
    next_taps = lax.ppermute(fine_taps, "segment", [(1, 2)])

    (grad2,) = call(
        section3_kernel,
        [((64, 2048), BF16)],
        [((128, 768), BF16), ((384, 768), BF16), ((576, 768), F32)],
        deep,
        up,
        down,
        deep_taps,
        flops=2 * 576 * 384 * 768,
    )
    grad2 = lax.ppermute(grad2, "segment", [(3, 2)])
    grad1, grad0 = call(
        section21_kernel,
        [((32, 4096), BF16), ((16, 4096), BF16)],
        [
            ((192, 2048), BF16),
            ((288, 2048), F32),
            ((32, 6144), BF16),
            ((96, 6144), BF16),
            ((144, 6144), F32),
        ],
        grad2,
        up,
        down,
        own2,
        deep_taps,
        next_own,
        next_taps,
        flops=2 * 288 * 192 * 2048,
    )
    grad0 = lax.ppermute(grad0, "segment", [(2, 0)])
    grad1 = lax.ppermute(grad1, "segment", [(2, 1)])
    (local01,) = call(
        functools.partial(weights01_kernel, scales[1], scales[0]),
        [((144, 128), F32)],
        [((96, 4096), BF16), ((144, 4096), BF16)],
        grad0,
        grad1,
        up,
        down,
        own01,
        flops=2 * 144 * 96 * 6144,
    )
    def swap(block, segments, bit):
        return over_space(block, segments, lambda n: [(i, i ^ bit) for i in range(n)])

    def behind(values, leader):
        return lax.optimization_barrier((*values, leader))[:-1]

    def kernel_gradient2(grad2):
        (local2,) = call(
            functools.partial(weights2_kernel, scales[2]),
            [((432, 128), F32)],
            [((192, 1024), BF16), ((288, 1024), BF16)],
            grad2,
            up,
            down,
            own2,
            flops=2 * 288 * 192 * 1024,
        )
        return local2

    sum01 = local01
    grad2, blocks = behind((grad2, deep[None]), sum01)
    places = [0]
    even = not count & (count - 1)
    gathers = even and count <= GATHER_LIMIT
    if even:
        bits = [1 << power for power in range(count.bit_length() - 1)]
        sum2 = None
        for bit, place_bit in zip(bits, reversed(bits)):
            received01 = swap(sum01, [0, 1], bit)
            if sum2 is None:
                sum2 = kernel_gradient2(grad2)
            received2 = swap(sum2, [2], bit)
            if gathers:
                blocks = jnp.concatenate([blocks, swap(blocks, [3], place_bit)], 0)
                places = places + [place ^ place_bit for place in places]
            sum01 = sum01 + received01
            sum2 = sum2 + received2
            if bit != bits[-1]:
                sum2, blocks = behind((sum2, blocks), sum01)
    else:
        sum2 = lax.psum(kernel_gradient2(grad2), "space")
        sum01 = lax.psum(sum01, "space")
    held = len(places)
    (sum3,) = call(
        functools.partial(weights3_kernel, scales[3], places),
        [((384, 576), F32)],
        [((128, 256 * held), BF16), ((384, 256 * held), BF16), ((576, 256 * held), BF16)],
        blocks,
        down,
        flops=2 * 384 * 576 * 256 * held,
    )
    if held < count:
        sum3 = lax.psum(sum3, "space")

    def finish0(sum01, sum2, sum3):
        parts = sum01[:, :48].reshape(3, 3, C1, 3, 16)[..., :C0]
        return flat_row(jnp.transpose(parts, (3, 0, 1, 2, 4)), room)

    def finish1(sum01, sum2, sum3):
        parts = sum01[:, :96].reshape(9, C1, 3, C2)
        return flat_row(jnp.transpose(parts, (0, 2, 3, 1)), room)

    def finish2(sum01, sum2, sum3):
        two = sum2[:288].reshape(9, C2, 2, C3)
        one = jnp.transpose(sum2[288:].reshape(144, 2, C3), (1, 0, 2)).reshape(9, C2, 1, C3)
        return flat_row(jnp.transpose(jnp.concatenate([two, one], 2), (0, 2, 3, 1)), room)

    def finish3(sum01, sum2, sum3):
        parts = sum3.reshape(3, C4, 9, C3)
        return flat_row(jnp.transpose(parts, (2, 0, 1, 3)), room)

    return lax.switch(segment, [finish0, finish1, finish2, finish3], sum01, sum2, sum3)


def solution(mesh):
    return jax.shard_map(
        shards,
        mesh=mesh,
        in_specs=(P("segment", "space"), P("segment", None), P(None, "space", None, None)),
        out_specs=P("segment", None),
        check_vma=False,
    )
```

```python
import functools
import math

import jax
import jax.numpy as jnp
from jax import lax
from jax.experimental import pallas as pl
from jax.experimental.pallas import tpu as pltpu
from jax.sharding import PartitionSpec as P

C0, C1, C2, C3, C4 = 4, 16, 32, 64, 128
LANES = 128
SLOPE = 0.3
BF16 = jnp.bfloat16
F32 = jnp.float32
GATHER_LIMIT = 8
VMEM_LIMIT = 48 * 1024 * 1024
LONG = 20_000_000_000


def on_segment(index):
    return lax.axis_index("segment") == index


def is_last_block():
    return lax.axis_index("space") == lax.axis_size("space") - 1


def cols(row, count=1):
    return slice(LANES * row, LANES * (row + count))


def moved_lanes(block, distance):
    lane = lax.broadcasted_iota(jnp.int32, block.shape, 1)
    rolled = pltpu.roll(block.astype(F32), distance % LANES, 1)
    kept = lane >= distance if distance > 0 else lane < LANES + distance
    return jnp.where(kept, rolled, 0.0).astype(BF16)


def stack_moved(read, target, chans, rows, distances):
    for row in range(rows):
        block = read(row)
        for place, distance in enumerate(distances):
            moved = moved_lanes(block, distance) if distance else block
            target[place * chans : (place + 1) * chans, cols(row)] = moved


def spread(rows_in, rows_out, source, bound):
    entry = lax.broadcasted_iota(jnp.int32, (rows_in, rows_out), 0)
    place = lax.broadcasted_iota(jnp.int32, (rows_in, rows_out), 1)
    return jnp.where((place == source(entry)) & bound(entry), 1.0, 0.0).astype(BF16)


def taps_of(cell, low, high):
    if cell % 2:
        pairs = [(1, (cell - 1) // 2)]
    else:
        pairs = [(0, cell // 2), (2, cell // 2 - 1)]
    return [(tap, place) for tap, place in pairs if low <= place <= high]


def dot_rows(left, right):
    return lax.dot_general(left, right, (((1,), (1,)), ((), ())), preferred_element_type=F32)


def dot(left, right):
    return jnp.dot(left, right, preferred_element_type=F32)


def sloped(total, activation):
    return (total * jnp.where(activation > 0, 1.0, SLOPE)).astype(BF16)


def half_row(block, odd):
    lane = lax.broadcasted_iota(jnp.int32, block.shape, 1)
    wide = block.astype(F32)
    if odd:
        wide = pltpu.roll(wide, LANES // 2, 1)
    return jnp.where(lane < LANES // 2, wide, 0.0)


def plane_of_message(ref, chans, row):
    return ref[32 * (row // 4) : 32 * (row // 4) + chans, cols(row % 4)]


def spread_top(block):
    unit = spread(64, 2 * LANES, lambda e: LANES * (e // 32) + 2 * (e % 32), lambda e: e >= 0)
    turned = (((0,), (0,)), ((), ()))
    return lax.dot_general(block, unit, turned, preferred_element_type=F32).astype(BF16)


def copy_rows(saved_ref, wide, chans, width):
    for chan in range(chans):
        source = saved_ref[:, chan * width : (chan + 1) * width]
        wide[chan : chan + 1, :width] = source.astype(F32)


def layout_kernel(
    saved_ref, top_ref, taps_ref, up_ref, down_ref, own2_ref, own01_ref, held, wide, arrived
):
    def fetch(size):
        copy = pltpu.make_async_copy(
            saved_ref.at[:, pl.ds(0, size)], held.at[:, pl.ds(0, size)], arrived
        )
        copy.start()
        copy.wait()

    def send(place, plane, target_ref):
        for half in range(2):
            target_ref[32 * half : 32 * half + place, :512] = wide[
                :place, cols(8 * plane + 4 * half, 4)
            ].astype(BF16)

    @pl.when(on_segment(3))
    def _():
        fetch(C3 * 512)
        copy_rows(held, wide, C3, 512)
        block = wide[:, :512].astype(BF16)
        for ref in (up_ref, down_ref):
            ref[:, :512] = block
            ref[:, 512:] = top_ref[...]

    for section, chans in enumerate((C0, C1, C2)):

        @pl.when(on_segment(section))
        def _(section=section, chans=chans):
            if section == 0:
                wide[:C1, :] = jnp.zeros((C1, 4096), F32)
            fetch(chans * 4096)
            copy_rows(held, wide, chans, 4096)
            place = max(chans, C1)
            own_ref = own2_ref if section == 2 else own01_ref
            own_ref[:, :4096] = wide[:place, :].astype(BF16)
            if section == 1:
                for tap in range(9):
                    own01_ref[:, cols(32 + tap)] = taps_ref[C1 * tap : C1 * (tap + 1), :]
            send(place, 3, up_ref)
            send(place, 0, down_ref)


def section3_kernel(own_ref, up_ref, down_ref, weights_ref, out_ref, wide, stacked, terms):
    @pl.when(on_segment(3))
    def _():
        for place, ref in enumerate((up_ref, own_ref, down_ref)):
            wide[:, cols(2 * place, 2)] = spread_top(ref[:, cols(4)])
        stack_moved(lambda row: wide[:, cols(row)], stacked, C4, 6, (0, 1, 2))
        terms[...] = dot(weights_ref[...], stacked[...])
        unit = spread(LANES, LANES, lambda e: 2 * e, lambda e: e < 64)
        last = is_last_block()
        for cell_z in range(-1, 3):
            for cell_y in range(4):
                total = None
                for tap_z, place_z in taps_of(cell_z, -1, 1):
                    for tap_y, place_y in taps_of(cell_y, 0, 1):
                        first = C3 * (3 * tap_z + tap_y)
                        part = terms[first : first + C3, cols(2 * (place_z + 1) + place_y)]
                        total = part if total is None else total + part
                if cell_z == -1:
                    mask = up_ref[:, cols(2 + cell_y // 2)]
                elif cell_z == 2:
                    mask = down_ref[:, cols(cell_y // 2)]
                else:
                    mask = own_ref[:, cols(2 * cell_z + cell_y // 2)]
                result = sloped(total, half_row(mask, cell_y % 2))
                if cell_z == 2:
                    result = jnp.where(last, jnp.zeros_like(result), result)
                out_ref[:, cols(4 * (cell_z + 1) + cell_y)] = dot(result, unit).astype(BF16)


def section21_kernel(
    grad_ref,
    up_ref,
    down_ref,
    own_ref,
    weights_ref,
    next_ref,
    out1_ref,
    out0_ref,
    stacked,
    terms,
    middle,
    next_weights,
    next_stacked,
    next_terms,
):
    @pl.when(on_segment(2))
    def _():
        stack_moved(lambda row: grad_ref[:, cols(row)], stacked, C3, 16, (0, 1, 2))
        terms[...] = dot(weights_ref[:288, :192], stacked[...])
        last = is_last_block()
        for cell_z in range(-1, 5):
            for cell_y in range(8):
                total = None
                for tap_z, place_z in taps_of(cell_z, -1, 2):
                    for tap_y, place_y in taps_of(cell_y, 0, 3):
                        first = C2 * (3 * tap_z + tap_y)
                        part = terms[first : first + C2, cols(4 * (place_z + 1) + place_y)]
                        total = part if total is None else total + part
                if cell_z == -1:
                    mask = plane_of_message(up_ref, C2, cell_y)
                elif cell_z == 4:
                    mask = plane_of_message(down_ref, C2, cell_y)
                else:
                    mask = own_ref[:, cols(8 * cell_z + cell_y)]
                result = sloped(total, mask.astype(F32))
                if cell_z == 4:
                    result = jnp.where(last, jnp.zeros_like(result), result)
                middle[:, cols(8 * (cell_z + 1) + cell_y)] = result
                if 0 <= cell_z < 4:
                    out1_ref[:, cols(8 * cell_z + cell_y)] = result
        stack_moved(lambda row: middle[:, cols(row)], next_stacked, C2, 48, (-1, 0, 1))
        for tap in range(9):
            next_weights[C1 * tap : C1 * (tap + 1), :] = next_ref[:, cols(32 + tap)]
        next_terms[...] = dot(next_weights[:, :96], next_stacked[...])
        edge = jnp.zeros((C1, LANES), F32)
        for plane in range(4):
            sums = []
            for tap_y in range(3):
                total = None
                for tap_z in range(3):
                    first = C1 * (3 * tap_z + tap_y)
                    part = next_terms[first : first + C1, cols(8 * (plane + 2 - tap_z), 8)]
                    total = part if total is None else total + part
                sums.append(total)
            later = jnp.concatenate([sums[0][:, LANES:], edge], 1)
            earlier = jnp.concatenate([edge, sums[2][:, : 7 * LANES]], 1)
            mask = next_ref[:, cols(8 * plane, 8)].astype(F32)
            out0_ref[:, cols(8 * plane, 8)] = sloped(sums[1] + later + earlier, mask)


def weights2_kernel(scale, grad_ref, up_ref, down_ref, own_ref, out_ref, stacked, acts):
    @pl.when(on_segment(2))
    def _():
        stack_moved(lambda row: grad_ref[:, cols(4 + row)], stacked, C3, 8, (0, 1, 2))
        for tap_z in range(3):
            for tap_y in range(3):
                first = C2 * (3 * tap_z + tap_y)
                for place_z in range(2):
                    for place_y in range(4):
                        plane, row = 2 * place_z + tap_z, 2 * place_y + tap_y
                        if row == 8:
                            block = jnp.zeros((C2, LANES), BF16)
                        elif plane == 4:
                            block = plane_of_message(down_ref, C2, row)
                        else:
                            block = own_ref[:, cols(8 * plane + row)]
                        acts[first : first + C2, cols(4 * place_z + place_y)] = block
        out_ref[:288, :] = dot_rows(acts[...], stacked[:128, :]) * scale
        out_ref[288:, :64] = dot_rows(acts[:144, :], stacked[128:, :]) * scale
        out_ref[288:, 64:] = dot_rows(acts[144:, :], stacked[128:, :]) * scale


def fine_acts(chans, up_ref, down_ref, own_ref, plane, row):
    if plane == -1:
        return plane_of_message(up_ref, chans, row)
    if plane == 4:
        return plane_of_message(down_ref, chans, row)
    return own_ref[:chans, cols(8 * plane + row)]


def weights01_kernel(
    scale1, scale0, grad0_ref, grad1_ref, up_ref, down_ref, own_ref, out_ref, stacked, acts
):
    none = jnp.zeros((C1, LANES), BF16)

    @pl.when(on_segment(0))
    def _():
        for place, distance in enumerate((-1, 0, 1)):
            for plane in range(4):
                for row in range(8):
                    block = grad0_ref[:, cols(8 * plane + row)]
                    block = moved_lanes(block, distance) if distance else block
                    for tap_y in range(3):
                        first = C1 * (3 * tap_y + place)
                        target = row + tap_y - 1
                        if 0 <= target < 8:
                            acts[first : first + C1, cols(8 * plane + target)] = block
                    if row == 0:
                        acts[C1 * (6 + place) : C1 * (7 + place), cols(8 * plane)] = none
                    if row == 7:
                        acts[C1 * place : C1 * (place + 1), cols(8 * plane + 7)] = none
        for tap_z in range(3):
            for plane in range(4):
                for row in range(8):
                    stacked[C1 * tap_z : C1 * (tap_z + 1), cols(8 * plane + row)] = fine_acts(
                        C1, up_ref, down_ref, own_ref, plane + tap_z - 1, row
                    )
        out_ref[:, :48] = dot_rows(acts[...], stacked[:48, :]) * scale0
        out_ref[:, 48:] = jnp.zeros((144, 80), F32)

    @pl.when(on_segment(1))
    def _():
        stack_moved(lambda row: grad1_ref[:, cols(row)], stacked, C2, 32, (-1, 0, 1))
        for tap_z in range(3):
            for tap_y in range(3):
                first = C1 * (3 * tap_z + tap_y)
                for plane in range(4):
                    for row in range(8):
                        source = row + tap_y - 1
                        block = none
                        if 0 <= source < 8:
                            block = fine_acts(
                                C1, up_ref, down_ref, own_ref, plane + tap_z - 1, source
                            )
                        acts[first : first + C1, cols(8 * plane + row)] = block
        out_ref[:, :96] = dot_rows(acts[...], stacked[...]) * scale1
        out_ref[:, 96:] = jnp.zeros((144, 32), F32)


def weights3_kernel(scale, places, blocks_ref, down_ref, out_ref, wide, stacked, acts):
    @pl.when(on_segment(3))
    def _():
        me = lax.axis_index("space")
        count = len(places)

        def held(block):
            wanted = lax.bitwise_xor(me, block)
            position = 0
            for bit, value in places_bits(places):
                position = position + value * lax.rem(lax.div(wanted, bit), 2)
            return blocks_ref[position]

        zero = jnp.zeros((64, LANES), BF16)
        for block in range(count):
            here = blocks_ref[0] if count == 1 else held(block)
            wide[:, cols(2 * block, 2)] = spread_top(here[:, cols(4)])
            rows = [half_row(here[:, cols(r // 2)], r % 2).astype(BF16) for r in range(8)]
            if count == 1:
                after = down_ref[:, : 2 * LANES]
            elif block + 1 < count:
                after = held(block + 1)[:, : 2 * LANES]
            else:
                after = None
            for r in range(4):
                rows.append(
                    zero if after is None else half_row(after[:, cols(r // 2)], r % 2).astype(BF16)
                )
            for tap_z in range(3):
                for tap_y in range(3):
                    first = C3 * (3 * tap_z + tap_y)
                    for place_y in range(2):
                        row = 2 * place_y + tap_y
                        source = zero if row == 4 else rows[4 * tap_z + row]
                        acts[first : first + C3, cols(2 * block + place_y)] = source
        stack_moved(lambda row: wide[:, cols(row)], stacked, C4, 2 * count, (0, 1, 2))
        out_ref[...] = dot_rows(stacked[...], acts[...]) * scale


def places_bits(places):
    count = len(places)
    bits = []
    bit = 1
    while bit < count:
        bits.append((bit, places.index(bit)))
        bit *= 2
    return bits


def call(kernel, outs, scratch, *args, flops, far=()):
    shapes = [jax.ShapeDtypeStruct(*entry) for entry in outs]
    moved = sum(a.size * a.dtype.itemsize for a in [*args, *shapes])
    near_spec = pl.BlockSpec(memory_space=pltpu.VMEM)
    far_spec = pl.BlockSpec(memory_space=pltpu.HBM)
    return pl.pallas_call(
        kernel,
        out_shape=shapes,
        in_specs=[far_spec if place in far else near_spec for place in range(len(args))],
        scratch_shapes=[
            pltpu.VMEM(*entry) if isinstance(entry, tuple) else entry for entry in scratch
        ],
        compiler_params=pltpu.CompilerParams(vmem_limit_bytes=VMEM_LIMIT),
        cost_estimate=pl.CostEstimate(flops=flops, bytes_accessed=moved, transcendentals=0),
    )(*args)


def padded(block, rows, columns):
    return jnp.pad(block, ((0, rows - block.shape[0]), (0, columns - block.shape[1])))


def by_tap(weights, chan_out, chan_in):
    groups = []
    size = 9 * chan_out * chan_in
    for tap_z in range(3):
        taps = weights[0, tap_z * size : (tap_z + 1) * size].reshape(3, 3, chan_out, chan_in)
        groups.append(jnp.transpose(taps, (0, 3, 1, 2)).reshape(3 * chan_in, 3 * chan_out))
    return jnp.concatenate(groups, 0)


def tap_layouts(section, weights):
    deep_taps = jnp.zeros((576, 384), BF16)
    fine_taps = jnp.zeros((144, 128), BF16)
    if section == 3:
        deep_taps = by_tap(weights, C4, C3)
    if section == 2:
        deep_taps = padded(by_tap(weights, C3, C2), 576, 384)
    if section == 1:
        fine_taps = padded(by_tap(weights, C2, C1), 144, 128)
    return deep_taps, fine_taps


def pairs_of(segments, route):
    total = lax.axis_size("segment")
    count = lax.axis_size("space")
    return [
        (a * total + s, b * total + s) for a, b in route(count) for s in segments
    ]


def over_space(block, segments, route):
    return lax.ppermute(block, ("space", "segment"), pairs_of(segments, route))


def flat_row(ordered, room):
    flat = ordered.reshape(-1)
    return jnp.pad(flat, (0, room - flat.shape[0]))[None]


def shards(saved_inputs, conv_weights, top_gradient):
    segment = lax.axis_index("segment")
    count = lax.axis_size("space")
    room = conv_weights.shape[1]
    scales = [1.0 / math.sqrt(count * cells) for cells in (4096, 4096, 512, 64)]

    def later(n):
        return [(i, i + 1) for i in range(n - 1)]

    def sooner(n):
        return [(i + 1, i) for i in range(n - 1)]

    def behind(values, *leaders):
        return lax.optimization_barrier((*values, *leaders))[: len(values)]

    deep_taps, fine_taps = lax.switch(
        segment,
        [functools.partial(tap_layouts, section) for section in range(4)],
        conv_weights,
    )
    top = jnp.transpose(top_gradient[:, 0], (1, 2, 0)).reshape(64, C4)
    top, fine_taps = behind((top, fine_taps), deep_taps)
    to_later, to_sooner, own2, own01 = call(
        layout_kernel,
        [((64, 640), BF16), ((64, 640), BF16), ((32, 4096), BF16), ((16, 5248), BF16)],
        [((1, 131072), BF16), ((64, 4096), F32), pltpu.SemaphoreType.DMA],
        saved_inputs,
        top,
        fine_taps,
        flops=0,
        far=(0,),
    )
    deep = to_later
    up = over_space(to_later, range(4), later)
    down = over_space(to_sooner, range(4), sooner)
    next_own = lax.ppermute(own01, "segment", [(1, 2)])
    (deep_taps,) = behind((deep_taps,), next_own)

    (grad2,) = call(
        section3_kernel,
        [((64, 2048), BF16)],
        [((128, 768), BF16), ((384, 768), BF16), ((576, 768), F32)],
        deep,
        up,
        down,
        deep_taps,
        flops=2 * 576 * 384 * 768,
    )
    grad2 = lax.ppermute(grad2, "segment", [(3, 2)])
    grad1, grad0 = call(
        section21_kernel,
        [((32, 4096), BF16), ((16, 4096), BF16)],
        [
            ((192, 2048), BF16),
            ((288, 2048), F32),
            ((32, 6144), BF16),
            ((144, 128), BF16),
            ((96, 6144), BF16),
            ((144, 6144), F32),
        ],
        grad2,
        up,
        down,
        own2,
        deep_taps,
        next_own,
        flops=2 * 288 * 192 * 2048,
    )
    def swap(block, segments, bit):
        return over_space(block, segments, lambda n: [(i, i ^ bit) for i in range(n)])

    grad2, blocks = behind((grad2, deep[None]), grad1)
    grad0 = lax.ppermute(grad0, "segment", [(2, 0)])
    grad1 = lax.ppermute(grad1, "segment", [(2, 1)])
    (sum2,) = call(
        functools.partial(weights2_kernel, scales[2]),
        [((432, 128), F32)],
        [((192, 1024), BF16), ((288, 1024), BF16)],
        grad2,
        up,
        down,
        own2,
        flops=LONG,
    )
    places = [0]
    even = not count & (count - 1)
    gathers = even and count <= GATHER_LIMIT
    bits = [1 << power for power in range(count.bit_length() - 1)] if even else []

    def gathered(blocks, bit):
        return jnp.concatenate([blocks, swap(blocks, [3], bit)], 0)

    if gathers:
        for bit in bits[:0:-1]:
            blocks = gathered(blocks, bit)
            places = places + [place ^ bit for place in places]
    grad0, grad1 = behind((grad0, grad1), sum2, blocks)
    (sum01,) = call(
        functools.partial(weights01_kernel, scales[1], scales[0]),
        [((144, 128), F32)],
        [((96, 4096), BF16), ((144, 4096), BF16)],
        grad0,
        grad1,
        up,
        down,
        own01,
        flops=2 * 144 * 96 * 6144,
    )
    for bit in bits:
        sum2 = sum2 + swap(sum2, [2], bit)
    if not even:
        sum2 = lax.psum(sum2, "space")
        sum01 = lax.psum(sum01, "space")
    if gathers:
        blocks = gathered(blocks, bits[0])
        places = places + [place ^ bits[0] for place in places]
    for bit in bits:
        sum01 = sum01 + swap(sum01, [0, 1], bit)
    held = len(places)
    (sum3,) = call(
        functools.partial(weights3_kernel, scales[3], places),
        [((384, 576), F32)],
        [((128, 256 * held), BF16), ((384, 256 * held), BF16), ((576, 256 * held), BF16)],
        blocks,
        down,
        flops=LONG,
    )
    if held < count:
        sum3 = lax.psum(sum3, "space")

    def finish0(sum01, sum2, sum3):
        parts = sum01[:, :48].reshape(3, 3, C1, 3, 16)[..., :C0]
        return flat_row(jnp.transpose(parts, (3, 0, 1, 2, 4)), room)

    def finish1(sum01, sum2, sum3):
        parts = sum01[:, :96].reshape(9, C1, 3, C2)
        return flat_row(jnp.transpose(parts, (0, 2, 3, 1)), room)

    def finish2(sum01, sum2, sum3):
        two = sum2[:288].reshape(9, C2, 2, C3)
        one = jnp.transpose(sum2[288:].reshape(144, 2, C3), (1, 0, 2)).reshape(9, C2, 1, C3)
        return flat_row(jnp.transpose(jnp.concatenate([two, one], 2), (0, 2, 3, 1)), room)

    def finish3(sum01, sum2, sum3):
        parts = sum3.reshape(3, C4, 9, C3)
        return flat_row(jnp.transpose(parts, (2, 0, 1, 3)), room)

    return lax.switch(segment, [finish0, finish1, finish2, finish3], sum01, sum2, sum3)


def solution(mesh):
    return jax.shard_map(
        shards,
        mesh=mesh,
        in_specs=(P("segment", "space"), P("segment", None), P(None, "space", None, None)),
        out_specs=P("segment", None),
        check_vma=False,
    )
```

```python
import functools
import math

import jax
import jax.numpy as jnp
from jax import lax
from jax.experimental import pallas as pl
from jax.experimental.pallas import tpu as pltpu
from jax.sharding import PartitionSpec as P

C0, C1, C2, C3, C4 = 4, 16, 32, 64, 128
LANES = 128
SLOPE = 0.3
BF16 = jnp.bfloat16
F32 = jnp.float32
GATHER_LIMIT = 8
VMEM_LIMIT = 48 * 1024 * 1024
LONG = 20_000_000_000


def on_segment(index):
    return lax.axis_index("segment") == index


def is_last_block():
    return lax.axis_index("space") == lax.axis_size("space") - 1


def cols(row, count=1):
    return slice(LANES * row, LANES * (row + count))


def moved_lanes(block, distance):
    lane = lax.broadcasted_iota(jnp.int32, block.shape, 1)
    rolled = pltpu.roll(block.astype(F32), distance % LANES, 1)
    kept = lane >= distance if distance > 0 else lane < LANES + distance
    return jnp.where(kept, rolled, 0.0).astype(BF16)


def stack_moved(read, target, chans, rows, distances):
    for row in range(rows):
        block = read(row)
        for place, distance in enumerate(distances):
            moved = moved_lanes(block, distance) if distance else block
            target[place * chans : (place + 1) * chans, cols(row)] = moved


def spread(rows_in, rows_out, source, bound):
    entry = lax.broadcasted_iota(jnp.int32, (rows_in, rows_out), 0)
    place = lax.broadcasted_iota(jnp.int32, (rows_in, rows_out), 1)
    return jnp.where((place == source(entry)) & bound(entry), 1.0, 0.0).astype(BF16)


def taps_of(cell, low, high):
    if cell % 2:
        pairs = [(1, (cell - 1) // 2)]
    else:
        pairs = [(0, cell // 2), (2, cell // 2 - 1)]
    return [(tap, place) for tap, place in pairs if low <= place <= high]


def dot_rows(left, right):
    return lax.dot_general(left, right, (((1,), (1,)), ((), ())), preferred_element_type=F32)


def dot(left, right):
    return jnp.dot(left, right, preferred_element_type=F32)


def sloped(total, activation):
    return (total * jnp.where(activation > 0, 1.0, SLOPE)).astype(BF16)


def half_row(block, odd):
    lane = lax.broadcasted_iota(jnp.int32, block.shape, 1)
    wide = block.astype(F32)
    if odd:
        wide = pltpu.roll(wide, LANES // 2, 1)
    return jnp.where(lane < LANES // 2, wide, 0.0)


def plane_of_message(ref, chans, row):
    return ref[32 * (row // 4) : 32 * (row // 4) + chans, cols(row % 4)]


def spread_top(block):
    unit = spread(64, 2 * LANES, lambda e: LANES * (e // 32) + 2 * (e % 32), lambda e: e >= 0)
    turned = (((0,), (0,)), ((), ()))
    return lax.dot_general(block, unit, turned, preferred_element_type=F32).astype(BF16)


def copy_rows(saved_ref, wide, chans, width):
    for chan in range(chans):
        source = saved_ref[:, chan * width : (chan + 1) * width]
        wide[chan : chan + 1, :width] = source.astype(F32)


def layout_kernel(
    saved_ref,
    top_ref,
    taps_ref,
    deep_ref,
    up_ref,
    down_ref,
    own2_ref,
    own01_ref,
    held,
    wide,
    arrived,
):
    def fetch(size):
        copy = pltpu.make_async_copy(
            saved_ref.at[:, pl.ds(0, size)], held.at[:, pl.ds(0, size)], arrived
        )
        copy.start()
        copy.wait()

    def send(place, plane, target_ref):
        for half in range(2):
            target_ref[32 * half : 32 * half + place, :] = wide[
                :place, cols(8 * plane + 4 * half, 4)
            ].astype(BF16)

    @pl.when(on_segment(3))
    def _():
        fetch(C3 * 512)
        copy_rows(held, wide, C3, 512)
        block = wide[:, :512].astype(BF16)
        top = top_ref[...]
        deep_ref[:, :512] = block
        deep_ref[:, 512:] = top
        for ref, half in ((up_ref, block[:, 256:]), (down_ref, block[:, :256])):
            ref[:, :256] = half
            ref[:, 256:384] = top
            ref[:, 384:] = jnp.zeros((64, LANES), BF16)

    for section, chans in enumerate((C0, C1, C2)):

        @pl.when(on_segment(section))
        def _(section=section, chans=chans):
            if section == 0:
                wide[:C1, :] = jnp.zeros((C1, 4096), F32)
            fetch(chans * 4096)
            copy_rows(held, wide, chans, 4096)
            place = max(chans, C1)
            own_ref = own2_ref if section == 2 else own01_ref
            own_ref[:, :4096] = wide[:place, :].astype(BF16)
            if section == 1:
                for tap in range(9):
                    own01_ref[:, cols(32 + tap)] = taps_ref[C1 * tap : C1 * (tap + 1), :]
            send(place, 3, up_ref)
            send(place, 0, down_ref)


def section3_kernel(own_ref, up_ref, down_ref, weights_ref, out_ref, wide, stacked, terms):
    @pl.when(on_segment(3))
    def _():
        for place, (ref, first) in enumerate(((up_ref, 2), (own_ref, 4), (down_ref, 2))):
            wide[:, cols(2 * place, 2)] = spread_top(ref[:, cols(first)])
        stack_moved(lambda row: wide[:, cols(row)], stacked, C4, 6, (0, 1, 2))
        terms[...] = dot(weights_ref[...], stacked[...])
        unit = spread(LANES, LANES, lambda e: 2 * e, lambda e: e < 64)
        last = is_last_block()
        for cell_z in range(-1, 3):
            for cell_y in range(4):
                total = None
                for tap_z, place_z in taps_of(cell_z, -1, 1):
                    for tap_y, place_y in taps_of(cell_y, 0, 1):
                        first = C3 * (3 * tap_z + tap_y)
                        part = terms[first : first + C3, cols(2 * (place_z + 1) + place_y)]
                        total = part if total is None else total + part
                if cell_z == -1:
                    mask = up_ref[:, cols(cell_y // 2)]
                elif cell_z == 2:
                    mask = down_ref[:, cols(cell_y // 2)]
                else:
                    mask = own_ref[:, cols(2 * cell_z + cell_y // 2)]
                result = sloped(total, half_row(mask, cell_y % 2))
                if cell_z == 2:
                    result = jnp.where(last, jnp.zeros_like(result), result)
                out_ref[:, cols(4 * (cell_z + 1) + cell_y)] = dot(result, unit).astype(BF16)


def section21_kernel(
    grad_ref,
    up_ref,
    down_ref,
    own_ref,
    weights_ref,
    next_ref,
    out1_ref,
    out0_ref,
    stacked,
    terms,
    middle,
    next_weights,
    next_stacked,
    next_terms,
):
    @pl.when(on_segment(2))
    def _():
        stack_moved(lambda row: grad_ref[:, cols(row)], stacked, C3, 16, (0, 1, 2))
        terms[...] = dot(weights_ref[:288, :192], stacked[...])
        last = is_last_block()
        for cell_z in range(-1, 5):
            for cell_y in range(8):
                total = None
                for tap_z, place_z in taps_of(cell_z, -1, 2):
                    for tap_y, place_y in taps_of(cell_y, 0, 3):
                        first = C2 * (3 * tap_z + tap_y)
                        part = terms[first : first + C2, cols(4 * (place_z + 1) + place_y)]
                        total = part if total is None else total + part
                if cell_z == -1:
                    mask = plane_of_message(up_ref, C2, cell_y)
                elif cell_z == 4:
                    mask = plane_of_message(down_ref, C2, cell_y)
                else:
                    mask = own_ref[:, cols(8 * cell_z + cell_y)]
                result = sloped(total, mask.astype(F32))
                if cell_z == 4:
                    result = jnp.where(last, jnp.zeros_like(result), result)
                middle[:, cols(8 * (cell_z + 1) + cell_y)] = result
                if 0 <= cell_z < 4:
                    out1_ref[:, cols(8 * cell_z + cell_y)] = result
        stack_moved(lambda row: middle[:, cols(row)], next_stacked, C2, 48, (-1, 0, 1))
        for tap in range(9):
            next_weights[C1 * tap : C1 * (tap + 1), :] = next_ref[:, cols(32 + tap)]
        next_terms[...] = dot(next_weights[:, :96], next_stacked[...])
        edge = jnp.zeros((C1, LANES), F32)
        for plane in range(4):
            sums = []
            for tap_y in range(3):
                total = None
                for tap_z in range(3):
                    first = C1 * (3 * tap_z + tap_y)
                    part = next_terms[first : first + C1, cols(8 * (plane + 2 - tap_z), 8)]
                    total = part if total is None else total + part
                sums.append(total)
            later = jnp.concatenate([sums[0][:, LANES:], edge], 1)
            earlier = jnp.concatenate([edge, sums[2][:, : 7 * LANES]], 1)
            mask = next_ref[:, cols(8 * plane, 8)].astype(F32)
            out0_ref[:, cols(8 * plane, 8)] = sloped(sums[1] + later + earlier, mask)


def weights2_kernel(scale, grad_ref, up_ref, down_ref, own_ref, out_ref, stacked, acts):
    @pl.when(on_segment(2))
    def _():
        stack_moved(lambda row: grad_ref[:, cols(4 + row)], stacked, C3, 8, (0, 1, 2))
        for tap_z in range(3):
            for tap_y in range(3):
                first = C2 * (3 * tap_z + tap_y)
                for place_z in range(2):
                    for place_y in range(4):
                        plane, row = 2 * place_z + tap_z, 2 * place_y + tap_y
                        if row == 8:
                            block = jnp.zeros((C2, LANES), BF16)
                        elif plane == 4:
                            block = plane_of_message(down_ref, C2, row)
                        else:
                            block = own_ref[:, cols(8 * plane + row)]
                        acts[first : first + C2, cols(4 * place_z + place_y)] = block
        out_ref[:288, :] = dot_rows(acts[...], stacked[:128, :]) * scale
        out_ref[288:, :64] = dot_rows(acts[:144, :], stacked[128:, :]) * scale
        out_ref[288:, 64:] = dot_rows(acts[144:, :], stacked[128:, :]) * scale


def fine_acts(chans, up_ref, down_ref, own_ref, plane, row):
    if plane == -1:
        return plane_of_message(up_ref, chans, row)
    if plane == 4:
        return plane_of_message(down_ref, chans, row)
    return own_ref[:chans, cols(8 * plane + row)]


def weights01_kernel(
    scale1, scale0, grad0_ref, grad1_ref, up_ref, down_ref, own_ref, out_ref, stacked, acts
):
    none = jnp.zeros((C1, LANES), BF16)

    @pl.when(on_segment(0))
    def _():
        for place, distance in enumerate((-1, 0, 1)):
            for plane in range(4):
                for row in range(8):
                    block = grad0_ref[:, cols(8 * plane + row)]
                    block = moved_lanes(block, distance) if distance else block
                    for tap_y in range(3):
                        first = C1 * (3 * tap_y + place)
                        target = row + tap_y - 1
                        if 0 <= target < 8:
                            acts[first : first + C1, cols(8 * plane + target)] = block
                    if row == 0:
                        acts[C1 * (6 + place) : C1 * (7 + place), cols(8 * plane)] = none
                    if row == 7:
                        acts[C1 * place : C1 * (place + 1), cols(8 * plane + 7)] = none
        for tap_z in range(3):
            for plane in range(4):
                for row in range(8):
                    stacked[C1 * tap_z : C1 * (tap_z + 1), cols(8 * plane + row)] = fine_acts(
                        C1, up_ref, down_ref, own_ref, plane + tap_z - 1, row
                    )
        out_ref[:, :48] = dot_rows(acts[...], stacked[:48, :]) * scale0
        out_ref[:, 48:] = jnp.zeros((144, 80), F32)

    @pl.when(on_segment(1))
    def _():
        stack_moved(lambda row: grad1_ref[:, cols(row)], stacked, C2, 32, (-1, 0, 1))
        for tap_z in range(3):
            for tap_y in range(3):
                first = C1 * (3 * tap_z + tap_y)
                for plane in range(4):
                    for row in range(8):
                        source = row + tap_y - 1
                        block = none
                        if 0 <= source < 8:
                            block = fine_acts(
                                C1, up_ref, down_ref, own_ref, plane + tap_z - 1, source
                            )
                        acts[first : first + C1, cols(8 * plane + row)] = block
        out_ref[:, :96] = dot_rows(acts[...], stacked[...]) * scale1
        out_ref[:, 96:] = jnp.zeros((144, 32), F32)


def weights3_kernel(scale, places, blocks_ref, down_ref, out_ref, wide, stacked, acts):
    @pl.when(on_segment(3))
    def _():
        me = lax.axis_index("space")
        count = len(places)

        def held(block):
            wanted = lax.bitwise_xor(me, block)
            position = 0
            for bit, value in places_bits(places):
                position = position + value * lax.rem(lax.div(wanted, bit), 2)
            return blocks_ref[position]

        zero = jnp.zeros((64, LANES), BF16)
        for block in range(count):
            here = blocks_ref[0] if count == 1 else held(block)
            wide[:, cols(2 * block, 2)] = spread_top(here[:, cols(4)])
            rows = [half_row(here[:, cols(r // 2)], r % 2).astype(BF16) for r in range(8)]
            if count == 1:
                after = down_ref[:, : 2 * LANES]
            elif block + 1 < count:
                after = held(block + 1)[:, : 2 * LANES]
            else:
                after = None
            for r in range(4):
                rows.append(
                    zero if after is None else half_row(after[:, cols(r // 2)], r % 2).astype(BF16)
                )
            for tap_z in range(3):
                for tap_y in range(3):
                    first = C3 * (3 * tap_z + tap_y)
                    for place_y in range(2):
                        row = 2 * place_y + tap_y
                        source = zero if row == 4 else rows[4 * tap_z + row]
                        acts[first : first + C3, cols(2 * block + place_y)] = source
        stack_moved(lambda row: wide[:, cols(row)], stacked, C4, 2 * count, (0, 1, 2))
        out_ref[...] = dot_rows(stacked[...], acts[...]) * scale


def places_bits(places):
    count = len(places)
    bits = []
    bit = 1
    while bit < count:
        bits.append((bit, places.index(bit)))
        bit *= 2
    return bits


def call(kernel, outs, scratch, *args, flops, far=()):
    shapes = [jax.ShapeDtypeStruct(*entry) for entry in outs]
    moved = sum(a.size * a.dtype.itemsize for a in [*args, *shapes])
    near_spec = pl.BlockSpec(memory_space=pltpu.VMEM)
    far_spec = pl.BlockSpec(memory_space=pltpu.HBM)
    return pl.pallas_call(
        kernel,
        out_shape=shapes,
        in_specs=[far_spec if place in far else near_spec for place in range(len(args))],
        scratch_shapes=[
            pltpu.VMEM(*entry) if isinstance(entry, tuple) else entry for entry in scratch
        ],
        compiler_params=pltpu.CompilerParams(vmem_limit_bytes=VMEM_LIMIT),
        cost_estimate=pl.CostEstimate(flops=flops, bytes_accessed=moved, transcendentals=0),
    )(*args)


def padded(block, rows, columns):
    return jnp.pad(block, ((0, rows - block.shape[0]), (0, columns - block.shape[1])))


def by_tap(weights, chan_out, chan_in):
    groups = []
    size = 9 * chan_out * chan_in
    for tap_z in range(3):
        taps = weights[0, tap_z * size : (tap_z + 1) * size].reshape(3, 3, chan_out, chan_in)
        groups.append(jnp.transpose(taps, (0, 3, 1, 2)).reshape(3 * chan_in, 3 * chan_out))
    return jnp.concatenate(groups, 0)


def deep_layout(section, weights):
    if section == 3:
        return by_tap(weights, C4, C3)
    if section == 2:
        return padded(by_tap(weights, C3, C2), 576, 384)
    return jnp.zeros((576, 384), BF16)


def fine_layout(section, weights):
    if section == 1:
        return padded(by_tap(weights, C2, C1), 144, 128)
    return jnp.zeros((144, 128), BF16)


def pairs_of(segments, route):
    total = lax.axis_size("segment")
    count = lax.axis_size("space")
    return [
        (a * total + s, b * total + s) for a, b in route(count) for s in segments
    ]


def over_space(block, segments, route):
    return lax.ppermute(block, ("space", "segment"), pairs_of(segments, route))


def flat_row(ordered, room):
    flat = ordered.reshape(-1)
    return jnp.pad(flat, (0, room - flat.shape[0]))[None]


def shards(saved_inputs, conv_weights, top_gradient):
    segment = lax.axis_index("segment")
    count = lax.axis_size("space")
    room = conv_weights.shape[1]
    scales = [1.0 / math.sqrt(count * cells) for cells in (4096, 4096, 512, 64)]

    def later(n):
        return [(i, i + 1) for i in range(n - 1)]

    def sooner(n):
        return [(i + 1, i) for i in range(n - 1)]

    def behind(values, *leaders):
        return lax.optimization_barrier((*values, *leaders))[: len(values)]

    def for_section(layout):
        branches = [functools.partial(layout, section) for section in range(4)]
        return lax.switch(segment, branches, conv_weights)

    top = jnp.transpose(top_gradient[:, 0], (1, 2, 0)).reshape(64, C4)
    deep, up, down, own2, own01 = call(
        layout_kernel,
        [
            ((64, 640), BF16),
            ((64, 512), BF16),
            ((64, 512), BF16),
            ((32, 4096), BF16),
            ((16, 5248), BF16),
        ],
        [((1, 131072), BF16), ((64, 4096), F32), pltpu.SemaphoreType.DMA],
        saved_inputs,
        top,
        for_section(fine_layout),
        flops=0,
        far=(0,),
    )
    up = over_space(up, range(4), later)
    down = over_space(down, range(4), sooner)
    next_own = lax.ppermute(own01, "segment", [(1, 2)])
    (weights,) = behind((conv_weights,), deep)
    deep_taps = lax.switch(
        segment, [functools.partial(deep_layout, section) for section in range(4)], weights
    )
    (deep_taps,) = behind((deep_taps,), next_own)

    (grad2,) = call(
        section3_kernel,
        [((64, 2048), BF16)],
        [((128, 768), BF16), ((384, 768), BF16), ((576, 768), F32)],
        deep,
        up,
        down,
        deep_taps,
        flops=2 * 576 * 384 * 768,
    )
    grad2 = lax.ppermute(grad2, "segment", [(3, 2)])
    grad1, grad0 = call(
        section21_kernel,
        [((32, 4096), BF16), ((16, 4096), BF16)],
        [
            ((192, 2048), BF16),
            ((288, 2048), F32),
            ((32, 6144), BF16),
            ((144, 128), BF16),
            ((96, 6144), BF16),
            ((144, 6144), F32),
        ],
        grad2,
        up,
        down,
        own2,
        deep_taps,
        next_own,
        flops=2 * 288 * 192 * 2048,
    )
    def swap(block, segments, bit):
        return over_space(block, segments, lambda n: [(i, i ^ bit) for i in range(n)])

    grad2, blocks = behind((grad2, deep[None]), grad1)
    grad0 = lax.ppermute(grad0, "segment", [(2, 0)])
    grad1 = lax.ppermute(grad1, "segment", [(2, 1)])
    (sum2,) = call(
        functools.partial(weights2_kernel, scales[2]),
        [((432, 128), F32)],
        [((192, 1024), BF16), ((288, 1024), BF16)],
        grad2,
        up,
        down,
        own2,
        flops=LONG,
    )
    places = [0]
    even = not count & (count - 1)
    gathers = even and count <= GATHER_LIMIT
    bits = [1 << power for power in range(count.bit_length() - 1)] if even else []

    def gathered(blocks, bit):
        return jnp.concatenate([blocks, swap(blocks, [3], bit)], 0)

    if gathers:
        for bit in bits[:0:-1]:
            blocks = gathered(blocks, bit)
            places = places + [place ^ bit for place in places]
    grad0, grad1 = behind((grad0, grad1), sum2, blocks)
    (sum01,) = call(
        functools.partial(weights01_kernel, scales[1], scales[0]),
        [((144, 128), F32)],
        [((96, 4096), BF16), ((144, 4096), BF16)],
        grad0,
        grad1,
        up,
        down,
        own01,
        flops=2 * 144 * 96 * 6144,
    )
    for bit in bits:
        sum2 = sum2 + swap(sum2, [2], bit)
    if not even:
        sum2 = lax.psum(sum2, "space")
        sum01 = lax.psum(sum01, "space")
    if gathers:
        blocks = gathered(blocks, bits[0])
        places = places + [place ^ bits[0] for place in places]
    for bit in bits:
        sum01 = sum01 + swap(sum01, [0, 1], bit)
    held = len(places)
    (sum3,) = call(
        functools.partial(weights3_kernel, scales[3], places),
        [((384, 576), F32)],
        [((128, 256 * held), BF16), ((384, 256 * held), BF16), ((576, 256 * held), BF16)],
        blocks,
        down,
        flops=LONG,
    )
    if held < count:
        sum3 = lax.psum(sum3, "space")

    def finish0(sum01, sum2, sum3):
        parts = sum01[:, :48].reshape(3, 3, C1, 3, 16)[..., :C0]
        return flat_row(jnp.transpose(parts, (3, 0, 1, 2, 4)), room)

    def finish1(sum01, sum2, sum3):
        parts = sum01[:, :96].reshape(9, C1, 3, C2)
        return flat_row(jnp.transpose(parts, (0, 2, 3, 1)), room)

    def finish2(sum01, sum2, sum3):
        two = sum2[:288].reshape(9, C2, 2, C3)
        one = jnp.transpose(sum2[288:].reshape(144, 2, C3), (1, 0, 2)).reshape(9, C2, 1, C3)
        return flat_row(jnp.transpose(jnp.concatenate([two, one], 2), (0, 2, 3, 1)), room)

    def finish3(sum01, sum2, sum3):
        parts = sum3.reshape(3, C4, 9, C3)
        return flat_row(jnp.transpose(parts, (2, 0, 1, 3)), room)

    return lax.switch(segment, [finish0, finish1, finish2, finish3], sum01, sum2, sum3)


def solution(mesh):
    return jax.shard_map(
        shards,
        mesh=mesh,
        in_specs=(P("segment", "space"), P("segment", None), P(None, "space", None, None)),
        out_specs=P("segment", None),
        check_vma=False,
    )
```

```python
import functools
import math

import jax
import jax.numpy as jnp
from jax import lax
from jax.experimental import pallas as pl
from jax.experimental.pallas import tpu as pltpu
from jax.sharding import PartitionSpec as P

C0, C1, C2, C3, C4 = 4, 16, 32, 64, 128
LANES = 128
SLOPE = 0.3
BF16 = jnp.bfloat16
F32 = jnp.float32
GATHER_LIMIT = 8
VMEM_LIMIT = 48 * 1024 * 1024
LONG = 20_000_000_000


def on_segment(index):
    return lax.axis_index("segment") == index


def is_last_block():
    return lax.axis_index("space") == lax.axis_size("space") - 1


def cols(row, count=1):
    return slice(LANES * row, LANES * (row + count))


def moved_lanes(block, distance):
    lane = lax.broadcasted_iota(jnp.int32, block.shape, 1)
    rolled = pltpu.roll(block.astype(F32), distance % LANES, 1)
    kept = lane >= distance if distance > 0 else lane < LANES + distance
    return jnp.where(kept, rolled, 0.0).astype(BF16)


def stack_moved(read, target, chans, rows, distances):
    for row in range(rows):
        block = read(row)
        for place, distance in enumerate(distances):
            moved = moved_lanes(block, distance) if distance else block
            target[place * chans : (place + 1) * chans, cols(row)] = moved


def spread(rows_in, rows_out, source, bound):
    entry = lax.broadcasted_iota(jnp.int32, (rows_in, rows_out), 0)
    place = lax.broadcasted_iota(jnp.int32, (rows_in, rows_out), 1)
    return jnp.where((place == source(entry)) & bound(entry), 1.0, 0.0).astype(BF16)


def taps_of(cell, low, high):
    if cell % 2:
        pairs = [(1, (cell - 1) // 2)]
    else:
        pairs = [(0, cell // 2), (2, cell // 2 - 1)]
    return [(tap, place) for tap, place in pairs if low <= place <= high]


def dot_rows(left, right):
    return lax.dot_general(left, right, (((1,), (1,)), ((), ())), preferred_element_type=F32)


def dot(left, right):
    return jnp.dot(left, right, preferred_element_type=F32)


def sloped(total, activation):
    return (total * jnp.where(activation > 0, 1.0, SLOPE)).astype(BF16)


def half_row(block, odd):
    lane = lax.broadcasted_iota(jnp.int32, block.shape, 1)
    wide = block.astype(F32)
    if odd:
        wide = pltpu.roll(wide, LANES // 2, 1)
    return jnp.where(lane < LANES // 2, wide, 0.0)


def plane_of_message(ref, chans, row):
    return ref[32 * (row // 4) : 32 * (row // 4) + chans, cols(row % 4)]


def spread_top(block):
    block = dot(block, halves_of(C4, 2)).astype(BF16)
    unit = spread(64, 2 * LANES, lambda e: LANES * (e // 32) + 2 * (e % 32), lambda e: e >= 0)
    turned = (((0,), (0,)), ((), ()))
    return lax.dot_general(block, unit, turned, preferred_element_type=F32).astype(BF16)


def copy_rows(saved_ref, wide, chans, width):
    for chan in range(chans):
        source = saved_ref[:, chan * width : (chan + 1) * width]
        wide[chan : chan + 1, :width] = source.astype(F32)


def layout_kernel(
    saved_ref,
    top_ref,
    taps_ref,
    deep_ref,
    up_ref,
    down_ref,
    own2_ref,
    own01_ref,
    held,
    wide,
    arrived,
):
    def fetch(size):
        copy = pltpu.make_async_copy(
            saved_ref.at[:, pl.ds(0, size)], held.at[:, pl.ds(0, size)], arrived
        )
        copy.start()
        copy.wait()

    def send(place, plane, target_ref):
        for half in range(2):
            target_ref[32 * half : 32 * half + place, :] = wide[
                :place, cols(8 * plane + 4 * half, 4)
            ].astype(BF16)

    @pl.when(on_segment(3))
    def _():
        fetch(C3 * 512)
        copy_rows(held, wide, C3, 512)
        block = wide[:, :512].astype(BF16)
        top = top_ref[...]
        deep_ref[:, :512] = block
        deep_ref[:, 512:] = top
        for ref, half in ((up_ref, block[:, 256:]), (down_ref, block[:, :256])):
            ref[:, :256] = half
            ref[:, 256:384] = top
            ref[:, 384:] = jnp.zeros((64, LANES), BF16)

    for section, chans in enumerate((C0, C1, C2)):

        @pl.when(on_segment(section))
        def _(section=section, chans=chans):
            if section == 0:
                wide[:C1, :] = jnp.zeros((C1, 4096), F32)
            fetch(chans * 4096)
            copy_rows(held, wide, chans, 4096)
            place = max(chans, C1)
            own_ref = own2_ref if section == 2 else own01_ref
            own_ref[:, :4096] = wide[:place, :].astype(BF16)
            if section == 1:
                for tap in range(9):
                    own01_ref[:, cols(32 + tap)] = taps_ref[C1 * tap : C1 * (tap + 1), :]
            send(place, 3, up_ref)
            send(place, 0, down_ref)


def weights_layout_kernel(weights_ref, out_ref, wide):
    @pl.when(on_segment(3))
    def _():
        for tap in range(27):
            first = 8192 * tap
            wide[64 * tap : 64 * tap + 64, :] = (
                weights_ref[:, first : first + 8192].astype(F32).reshape(64, LANES)
            )
        for group in range(9):
            turned = jnp.transpose(wide[192 * group : 192 * group + 192, :]).astype(BF16)
            rows = slice(C3 * group, C3 * group + C3)
            out_ref[rows, :192] = turned[:64]
            out_ref[rows, 192:] = turned[64:]


def halves_of(channels, parts):
    size = channels // parts
    return spread(channels, channels, lambda e: (e % parts) * size + e // parts, lambda e: e >= 0)


def section3_kernel(own_ref, up_ref, down_ref, weights_ref, out_ref, wide, stacked, terms):
    @pl.when(on_segment(3))
    def _():
        for place, (ref, first) in enumerate(((up_ref, 2), (own_ref, 4), (down_ref, 2))):
            wide[:, cols(2 * place, 2)] = spread_top(ref[:, cols(first)])
        for half in range(2):
            stack_moved(
                lambda row: wide[64 * half : 64 * half + 64, cols(row)],
                stacked.at[192 * half : 192 * half + 192],
                64,
                6,
                (0, 1, 2),
            )
        terms[...] = dot(weights_ref[...], stacked[...])
        unit = spread(LANES, LANES, lambda e: 2 * e, lambda e: e < 64)
        last = is_last_block()
        for cell_z in range(-1, 3):
            for cell_y in range(4):
                total = None
                for tap_z, place_z in taps_of(cell_z, -1, 1):
                    for tap_y, place_y in taps_of(cell_y, 0, 1):
                        first = C3 * (3 * tap_z + tap_y)
                        part = terms[first : first + C3, cols(2 * (place_z + 1) + place_y)]
                        total = part if total is None else total + part
                if cell_z == -1:
                    mask = up_ref[:, cols(cell_y // 2)]
                elif cell_z == 2:
                    mask = down_ref[:, cols(cell_y // 2)]
                else:
                    mask = own_ref[:, cols(2 * cell_z + cell_y // 2)]
                result = sloped(total, half_row(mask, cell_y % 2))
                if cell_z == 2:
                    result = jnp.where(last, jnp.zeros_like(result), result)
                out_ref[:, cols(4 * (cell_z + 1) + cell_y)] = dot(result, unit).astype(BF16)


def section21_kernel(
    grad_ref,
    up_ref,
    down_ref,
    own_ref,
    weights_ref,
    next_ref,
    out1_ref,
    out0_ref,
    stacked,
    terms,
    middle,
    next_weights,
    next_stacked,
    next_terms,
):
    @pl.when(on_segment(2))
    def _():
        stack_moved(lambda row: grad_ref[:, cols(row)], stacked, C3, 16, (0, 1, 2))
        terms[...] = dot(weights_ref[...], stacked[...])
        last = is_last_block()
        for cell_z in range(-1, 5):
            for cell_y in range(8):
                total = None
                for tap_z, place_z in taps_of(cell_z, -1, 2):
                    for tap_y, place_y in taps_of(cell_y, 0, 3):
                        first = C2 * (3 * tap_z + tap_y)
                        part = terms[first : first + C2, cols(4 * (place_z + 1) + place_y)]
                        total = part if total is None else total + part
                if cell_z == -1:
                    mask = plane_of_message(up_ref, C2, cell_y)
                elif cell_z == 4:
                    mask = plane_of_message(down_ref, C2, cell_y)
                else:
                    mask = own_ref[:, cols(8 * cell_z + cell_y)]
                result = sloped(total, mask.astype(F32))
                if cell_z == 4:
                    result = jnp.where(last, jnp.zeros_like(result), result)
                middle[:, cols(8 * (cell_z + 1) + cell_y)] = result
                if 0 <= cell_z < 4:
                    out1_ref[:, cols(8 * cell_z + cell_y)] = result
        stack_moved(lambda row: middle[:, cols(row)], next_stacked, C2, 48, (-1, 0, 1))
        for tap in range(9):
            next_weights[C1 * tap : C1 * (tap + 1), :] = next_ref[:, cols(32 + tap)]
        next_terms[...] = dot(next_weights[:, :96], next_stacked[...])
        edge = jnp.zeros((C1, LANES), F32)
        for plane in range(4):
            sums = []
            for tap_y in range(3):
                total = None
                for tap_z in range(3):
                    first = C1 * (3 * tap_z + tap_y)
                    part = next_terms[first : first + C1, cols(8 * (plane + 2 - tap_z), 8)]
                    total = part if total is None else total + part
                sums.append(total)
            later = jnp.concatenate([sums[0][:, LANES:], edge], 1)
            earlier = jnp.concatenate([edge, sums[2][:, : 7 * LANES]], 1)
            mask = next_ref[:, cols(8 * plane, 8)].astype(F32)
            out0_ref[:, cols(8 * plane, 8)] = sloped(sums[1] + later + earlier, mask)


def weights2_kernel(scale, grad_ref, up_ref, down_ref, own_ref, out_ref, stacked, acts):
    @pl.when(on_segment(2))
    def _():
        ordered = lax.dot_general(
            halves_of(C3, 4),
            grad_ref[:, cols(4, 8)],
            (((0,), (0,)), ((), ())),
            preferred_element_type=F32,
        ).astype(BF16)
        stack_moved(lambda row: ordered[:, cols(row)], stacked, C3, 8, (0, 1, 2))
        for tap_z in range(3):
            for tap_y in range(3):
                first = C2 * (3 * tap_z + tap_y)
                for place_z in range(2):
                    for place_y in range(4):
                        plane, row = 2 * place_z + tap_z, 2 * place_y + tap_y
                        if row == 8:
                            block = jnp.zeros((C2, LANES), BF16)
                        elif plane == 4:
                            block = plane_of_message(down_ref, C2, row)
                        else:
                            block = own_ref[:, cols(8 * plane + row)]
                        acts[first : first + C2, cols(4 * place_z + place_y)] = block
        total = dot_rows(stacked[...], acts[...]) * scale
        for group in range(9):
            for tap_x in range(3):
                first = 16 * (3 * group + tap_x)
                for part in range(4):
                    row = C3 * tap_x + 16 * part
                    out_ref[first : first + 16, 32 * part : 32 * part + 32] = total[
                        row : row + 16, 32 * group : 32 * group + 32
                    ]


def fine_acts(chans, up_ref, down_ref, own_ref, plane, row):
    if plane == -1:
        return plane_of_message(up_ref, chans, row)
    if plane == 4:
        return plane_of_message(down_ref, chans, row)
    return own_ref[:chans, cols(8 * plane + row)]


def weights01_kernel(
    scale1, scale0, grad0_ref, grad1_ref, up_ref, down_ref, own_ref, out_ref, stacked, acts
):
    none = jnp.zeros((C1, LANES), BF16)

    @pl.when(on_segment(0))
    def _():
        for place, distance in enumerate((-1, 0, 1)):
            for plane in range(4):
                for row in range(8):
                    block = grad0_ref[:, cols(8 * plane + row)]
                    block = moved_lanes(block, distance) if distance else block
                    for tap_y in range(3):
                        first = C1 * (3 * tap_y + place)
                        target = row + tap_y - 1
                        if 0 <= target < 8:
                            acts[first : first + C1, cols(8 * plane + target)] = block
                    if row == 0:
                        acts[C1 * (6 + place) : C1 * (7 + place), cols(8 * plane)] = none
                    if row == 7:
                        acts[C1 * place : C1 * (place + 1), cols(8 * plane + 7)] = none
        for tap_z in range(3):
            for plane in range(4):
                for row in range(8):
                    stacked[C1 * tap_z : C1 * (tap_z + 1), cols(8 * plane + row)] = fine_acts(
                        C1, up_ref, down_ref, own_ref, plane + tap_z - 1, row
                    )
        out_ref[:, :48] = dot_rows(acts[...], stacked[:48, :]) * scale0
        out_ref[:, 48:] = jnp.zeros((144, 80), F32)

    @pl.when(on_segment(1))
    def _():
        stack_moved(lambda row: grad1_ref[:, cols(row)], stacked, C2, 32, (-1, 0, 1))
        for tap_z in range(3):
            for tap_y in range(3):
                first = C1 * (3 * tap_z + tap_y)
                for plane in range(4):
                    for row in range(8):
                        source = row + tap_y - 1
                        block = none
                        if 0 <= source < 8:
                            block = fine_acts(
                                C1, up_ref, down_ref, own_ref, plane + tap_z - 1, source
                            )
                        acts[first : first + C1, cols(8 * plane + row)] = block
        out_ref[:, :96] = dot_rows(acts[...], stacked[...]) * scale1
        out_ref[:, 96:] = jnp.zeros((144, 32), F32)


def weights3_kernel(scale, places, blocks_ref, down_ref, out_ref, wide, stacked, acts):
    @pl.when(on_segment(3))
    def _():
        me = lax.axis_index("space")
        count = len(places)

        def held(block):
            wanted = lax.bitwise_xor(me, block)
            position = 0
            for bit, value in places_bits(places):
                position = position + value * lax.rem(lax.div(wanted, bit), 2)
            return blocks_ref[position]

        zero = jnp.zeros((64, LANES), BF16)
        for block in range(count):
            here = blocks_ref[0] if count == 1 else held(block)
            wide[:, cols(2 * block, 2)] = spread_top(here[:, cols(4)])
            rows = [half_row(here[:, cols(r // 2)], r % 2).astype(BF16) for r in range(8)]
            if count == 1:
                after = down_ref[:, : 2 * LANES]
            elif block + 1 < count:
                after = held(block + 1)[:, : 2 * LANES]
            else:
                after = None
            for r in range(4):
                rows.append(
                    zero if after is None else half_row(after[:, cols(r // 2)], r % 2).astype(BF16)
                )
            for tap_z in range(3):
                for tap_y in range(3):
                    first = C3 * (3 * tap_z + tap_y)
                    for place_y in range(2):
                        row = 2 * place_y + tap_y
                        source = zero if row == 4 else rows[4 * tap_z + row]
                        acts[first : first + C3, cols(2 * block + place_y)] = source
        stack_moved(lambda row: wide[:, cols(row)], stacked, C4, 2 * count, (0, 1, 2))
        total = dot_rows(stacked[...], acts[...]) * scale
        for group in range(9):
            for tap_x in range(3):
                first = 64 * (3 * group + tap_x)
                for part in range(2):
                    row = C4 * tap_x + 64 * part
                    out_ref[first : first + 64, 64 * part : 64 * part + 64] = total[
                        row : row + 64, C3 * group : C3 * group + C3
                    ]


def places_bits(places):
    count = len(places)
    bits = []
    bit = 1
    while bit < count:
        bits.append((bit, places.index(bit)))
        bit *= 2
    return bits


def call(kernel, outs, scratch, *args, flops, far=()):
    shapes = [jax.ShapeDtypeStruct(*entry) for entry in outs]
    moved = sum(a.size * a.dtype.itemsize for a in [*args, *shapes])
    near_spec = pl.BlockSpec(memory_space=pltpu.VMEM)
    far_spec = pl.BlockSpec(memory_space=pltpu.HBM)
    return pl.pallas_call(
        kernel,
        out_shape=shapes,
        in_specs=[far_spec if place in far else near_spec for place in range(len(args))],
        scratch_shapes=[
            pltpu.VMEM(*entry) if isinstance(entry, tuple) else entry for entry in scratch
        ],
        compiler_params=pltpu.CompilerParams(vmem_limit_bytes=VMEM_LIMIT),
        cost_estimate=pl.CostEstimate(flops=flops, bytes_accessed=moved, transcendentals=0),
    )(*args)


def padded(block, rows, columns):
    return jnp.pad(block, ((0, rows - block.shape[0]), (0, columns - block.shape[1])))


def by_tap(weights, chan_out, chan_in):
    groups = []
    size = 9 * chan_out * chan_in
    for tap_z in range(3):
        taps = weights[0, tap_z * size : (tap_z + 1) * size].reshape(3, 3, chan_out, chan_in)
        groups.append(jnp.transpose(taps, (0, 3, 1, 2)).reshape(3 * chan_in, 3 * chan_out))
    return jnp.concatenate(groups, 0)


def middle_layout(section, weights):
    if section == 2:
        return by_tap(weights, C3, C2)
    return jnp.zeros((288, 192), BF16)


def fine_layout(section, weights):
    if section == 1:
        return padded(by_tap(weights, C2, C1), 144, 128)
    return jnp.zeros((144, 128), BF16)


def pairs_of(segments, route):
    total = lax.axis_size("segment")
    count = lax.axis_size("space")
    return [
        (a * total + s, b * total + s) for a, b in route(count) for s in segments
    ]


def over_space(block, segments, route):
    return lax.ppermute(block, ("space", "segment"), pairs_of(segments, route))


def filled(ordered):
    rows = ordered.reshape(-1, LANES) if ordered.size % LANES == 0 else None
    if rows is None:
        flat = ordered.reshape(-1)
        rows = jnp.pad(flat, (0, -flat.shape[0] % LANES)).reshape(-1, LANES)
    return rows


def shards(saved_inputs, conv_weights, top_gradient):
    segment = lax.axis_index("segment")
    count = lax.axis_size("space")
    room = conv_weights.shape[1]
    scales = [1.0 / math.sqrt(count * cells) for cells in (4096, 4096, 512, 64)]

    def later(n):
        return [(i, i + 1) for i in range(n - 1)]

    def sooner(n):
        return [(i + 1, i) for i in range(n - 1)]

    def behind(values, *leaders):
        return lax.optimization_barrier((*values, *leaders))[: len(values)]

    def for_section(layout):
        branches = [functools.partial(layout, section) for section in range(4)]
        return lax.switch(segment, branches, conv_weights)

    top = jnp.transpose(top_gradient[:, 0], (1, 2, 0)).reshape(64, C4)
    deep, up, down, own2, own01 = call(
        layout_kernel,
        [
            ((64, 640), BF16),
            ((64, 512), BF16),
            ((64, 512), BF16),
            ((32, 4096), BF16),
            ((16, 5248), BF16),
        ],
        [((1, 131072), BF16), ((64, 4096), F32), pltpu.SemaphoreType.DMA],
        saved_inputs,
        top,
        for_section(fine_layout),
        flops=0,
        far=(0,),
    )
    up = over_space(up, range(4), later)
    down = over_space(down, range(4), sooner)
    next_own = lax.ppermute(own01, "segment", [(1, 2)])
    (taps3,) = call(
        weights_layout_kernel,
        [((576, 384), BF16)],
        [((1728, 128), F32)],
        conv_weights,
        flops=LONG,
    )
    (weights,) = behind((conv_weights,), deep)
    taps2 = lax.switch(
        segment, [functools.partial(middle_layout, section) for section in range(4)], weights
    )
    taps3, taps2 = behind((taps3, taps2), next_own)

    (grad2,) = call(
        section3_kernel,
        [((64, 2048), BF16)],
        [((128, 768), BF16), ((384, 768), BF16), ((576, 768), F32)],
        deep,
        up,
        down,
        taps3,
        flops=2 * 576 * 384 * 768,
    )
    grad2 = lax.ppermute(grad2, "segment", [(3, 2)])
    grad1, grad0 = call(
        section21_kernel,
        [((32, 4096), BF16), ((16, 4096), BF16)],
        [
            ((192, 2048), BF16),
            ((288, 2048), F32),
            ((32, 6144), BF16),
            ((144, 128), BF16),
            ((96, 6144), BF16),
            ((144, 6144), F32),
        ],
        grad2,
        up,
        down,
        own2,
        taps2,
        next_own,
        flops=2 * 288 * 192 * 2048,
    )
    def swap(block, segments, bit):
        return over_space(block, segments, lambda n: [(i, i ^ bit) for i in range(n)])

    grad2, blocks = behind((grad2, deep[None]), grad1)
    grad0 = lax.ppermute(grad0, "segment", [(2, 0)])
    grad1 = lax.ppermute(grad1, "segment", [(2, 1)])
    (sum2,) = call(
        functools.partial(weights2_kernel, scales[2]),
        [((432, 128), F32)],
        [((192, 1024), BF16), ((288, 1024), BF16)],
        grad2,
        up,
        down,
        own2,
        flops=LONG,
    )
    places = [0]
    even = not count & (count - 1)
    gathers = even and count <= GATHER_LIMIT
    bits = [1 << power for power in range(count.bit_length() - 1)] if even else []

    def gathered(blocks, bit):
        return jnp.concatenate([blocks, swap(blocks, [3], bit)], 0)

    if gathers:
        for bit in bits[:0:-1]:
            blocks = gathered(blocks, bit)
            places = places + [place ^ bit for place in places]
    grad0, grad1 = behind((grad0, grad1), sum2, blocks)
    (sum01,) = call(
        functools.partial(weights01_kernel, scales[1], scales[0]),
        [((144, 128), F32)],
        [((96, 4096), BF16), ((144, 4096), BF16)],
        grad0,
        grad1,
        up,
        down,
        own01,
        flops=2 * 144 * 96 * 6144,
    )
    for bit in bits:
        sum2 = sum2 + swap(sum2, [2], bit)
    if not even:
        sum2 = lax.psum(sum2, "space")
        sum01 = lax.psum(sum01, "space")
    if gathers:
        blocks = gathered(blocks, bits[0])
        places = places + [place ^ bits[0] for place in places]
    for bit in bits:
        sum01 = sum01 + swap(sum01, [0, 1], bit)
    held = len(places)
    (sum3,) = call(
        functools.partial(weights3_kernel, scales[3], places),
        [((1728, 128), F32)],
        [((128, 256 * held), BF16), ((384, 256 * held), BF16), ((576, 256 * held), BF16)],
        blocks,
        down,
        flops=LONG,
    )
    if held < count:
        sum3 = lax.psum(sum3, "space")

    def finish0(sum01, sum2, sum3):
        parts = sum01[:, :48].reshape(3, 3, C1, 3, 16)[..., :C0]
        return filled(jnp.transpose(parts, (3, 0, 1, 2, 4)))

    def finish1(sum01, sum2, sum3):
        parts = sum01[:, :96].reshape(9, C1, 3, C2)
        return filled(jnp.transpose(parts, (0, 2, 3, 1)))

    def whole(finish):
        def branch(*sums):
            rows = finish(*sums)
            return jnp.pad(rows, ((0, room // LANES - rows.shape[0]), (0, 0)))

        return branch

    ends = [finish0, finish1, lambda a, b, c: b, lambda a, b, c: c]
    rows = lax.switch(segment, [whole(end) for end in ends], sum01, sum2, sum3)
    return rows.reshape(1, room)


def solution(mesh):
    return jax.shard_map(
        shards,
        mesh=mesh,
        in_specs=(P("segment", "space"), P("segment", None), P(None, "space", None, None)),
        out_specs=P("segment", None),
        check_vma=False,
    )
```

```python
import functools
import math

import jax
import jax.numpy as jnp
from jax import lax
from jax.experimental import pallas as pl
from jax.experimental.pallas import tpu as pltpu
from jax.sharding import PartitionSpec as P

C0, C1, C2, C3, C4 = 4, 16, 32, 64, 128
LANES = 128
SLOPE = 0.3
BF16 = jnp.bfloat16
F32 = jnp.float32
GATHER_LIMIT = 8
VMEM_LIMIT = 48 * 1024 * 1024
LONG = 20_000_000_000


def on_segment(index):
    return lax.axis_index("segment") == index


def is_last_block():
    return lax.axis_index("space") == lax.axis_size("space") - 1


def cols(row, count=1):
    return slice(LANES * row, LANES * (row + count))


def moved_lanes(block, distance):
    lane = lax.broadcasted_iota(jnp.int32, block.shape, 1)
    rolled = pltpu.roll(block.astype(F32), distance % LANES, 1)
    kept = lane >= distance if distance > 0 else lane < LANES + distance
    return jnp.where(kept, rolled, 0.0).astype(BF16)


def stack_moved(read, target, chans, rows, distances):
    for row in range(rows):
        block = read(row)
        for place, distance in enumerate(distances):
            moved = moved_lanes(block, distance) if distance else block
            target[place * chans : (place + 1) * chans, cols(row)] = moved


def spread(rows_in, rows_out, source, bound):
    entry = lax.broadcasted_iota(jnp.int32, (rows_in, rows_out), 0)
    place = lax.broadcasted_iota(jnp.int32, (rows_in, rows_out), 1)
    return jnp.where((place == source(entry)) & bound(entry), 1.0, 0.0).astype(BF16)


def taps_of(cell, low, high):
    if cell % 2:
        pairs = [(1, (cell - 1) // 2)]
    else:
        pairs = [(0, cell // 2), (2, cell // 2 - 1)]
    return [(tap, place) for tap, place in pairs if low <= place <= high]


def dot_rows(left, right):
    return lax.dot_general(left, right, (((1,), (1,)), ((), ())), preferred_element_type=F32)


def dot(left, right):
    return jnp.dot(left, right, preferred_element_type=F32)


def sloped(total, activation):
    return (total * jnp.where(activation > 0, 1.0, SLOPE)).astype(BF16)


def half_row(block, odd):
    lane = lax.broadcasted_iota(jnp.int32, block.shape, 1)
    wide = block.astype(F32)
    if odd:
        wide = pltpu.roll(wide, LANES // 2, 1)
    return jnp.where(lane < LANES // 2, wide, 0.0)


def plane_of_message(ref, chans, row):
    return ref[32 * (row // 4) : 32 * (row // 4) + chans, cols(row % 4)]


def spread_top(block):
    block = dot(block, halves_of(C4, 2)).astype(BF16)
    unit = spread(64, 2 * LANES, lambda e: LANES * (e // 32) + 2 * (e % 32), lambda e: e >= 0)
    turned = (((0,), (0,)), ((), ()))
    return lax.dot_general(block, unit, turned, preferred_element_type=F32).astype(BF16)


def copy_rows(saved_ref, wide, chans, width):
    for chan in range(chans):
        source = saved_ref[:, chan * width : (chan + 1) * width]
        wide[chan : chan + 1, :width] = source.astype(F32)


def fetched(far_ref, near_ref, size, arrived):
    part = pl.ds(0, size)
    copy = pltpu.make_async_copy(far_ref.at[:, part], near_ref.at[:, part], arrived)
    copy.start()
    copy.wait()


def weight_rows(held, wide, rows):
    for tap in range(27):
        first = LANES * rows * tap
        wide[rows * tap : rows * tap + rows, :] = (
            held[:, first : first + LANES * rows].astype(F32).reshape(rows, LANES)
        )


def layout_kernel(
    saved_ref,
    weights_ref,
    top_ref,
    deep_ref,
    up_ref,
    down_ref,
    own2_ref,
    own01_ref,
    held,
    held_weights,
    wide,
    wide_weights,
    mixed,
    held_top,
    arrived,
    arrived_top,
):
    def fetch(size):
        fetched(saved_ref, held, size, arrived)

    def send(place, plane, target_ref):
        for half in range(2):
            target_ref[32 * half : 32 * half + place, :] = wide[
                :place, cols(8 * plane + 4 * half, 4)
            ].astype(BF16)

    @pl.when(on_segment(3))
    def _():
        copy = pltpu.make_async_copy(top_ref, held_top, arrived_top)
        copy.start()
        fetch(C3 * 512)
        copy_rows(held, wide, C3, 512)
        block = wide[:, :512].astype(BF16)
        copy.wait()
        top = held_top[...]
        deep_ref[:, :512] = block
        deep_ref[:, 512:] = top
        for ref, half in ((up_ref, block[:, 256:]), (down_ref, block[:, :256])):
            ref[:, :256] = half
            ref[:, 256:384] = top
            ref[:, 384:] = jnp.zeros((64, LANES), BF16)

    for section, chans in enumerate((C0, C1, C2)):

        @pl.when(on_segment(section))
        def _(section=section, chans=chans):
            if section == 0:
                wide[:C1, :] = jnp.zeros((C1, 4096), F32)
            fetch(chans * 4096)
            copy_rows(held, wide, chans, 4096)
            place = max(chans, C1)
            own_ref = own2_ref if section == 2 else own01_ref
            own_ref[:, :4096] = wide[:place, :].astype(BF16)
            if section == 1:
                fetched(weights_ref, held_weights, 27 * C1 * C2, arrived)
                weight_rows(held_weights, wide_weights, 4)
                turned = jnp.transpose(wide_weights[...])
                mixed[...] = jnp.zeros((144, LANES), F32)
                for group in range(9):
                    for part in range(8):
                        mixed[16 * group : 16 * group + 16, 12 * part : 12 * part + 12] = turned[
                            16 * part : 16 * part + 16, 12 * group : 12 * group + 12
                        ]
                ordered = spread(
                    LANES,
                    LANES,
                    lambda e: 32 * ((e % 12) // 4) + 8 * (e % 4) + e // 12,
                    lambda e: e < 96,
                )
                taps = dot(mixed[...].astype(BF16), ordered).astype(BF16)
                for group in range(9):
                    own01_ref[:, cols(32 + group)] = taps[16 * group : 16 * group + 16, :]
            send(place, 3, up_ref)
            send(place, 0, down_ref)


def weights_layout_kernel(weights_ref, out3_ref, out2_ref, held, wide, arrived):
    @pl.when(on_segment(3))
    def _():
        fetched(weights_ref, held, 27 * C3 * C4, arrived)
        weight_rows(held, wide, 64)
        for group in range(9):
            turned = jnp.transpose(wide[192 * group : 192 * group + 192, :]).astype(BF16)
            rows = slice(C3 * group, C3 * group + C3)
            for part in range(2):
                out3_ref[rows, 192 * part : 192 * part + 192] = turned[64 * part : 64 * part + 64]

    @pl.when(on_segment(2))
    def _():
        fetched(weights_ref, held, 27 * C2 * C3, arrived)
        weight_rows(held, wide, 16)
        for group in range(9):
            turned = jnp.transpose(wide[48 * group : 48 * group + 48, :]).astype(BF16)
            rows = slice(C2 * group, C2 * group + C2)
            for part in range(4):
                out2_ref[rows, 48 * part : 48 * part + 48] = turned[32 * part : 32 * part + 32]


def halves_of(channels, parts):
    size = channels // parts
    return spread(channels, channels, lambda e: (e % parts) * size + e // parts, lambda e: e >= 0)


def quarters(grad):
    turned = (((0,), (0,)), ((), ()))
    mixed = lax.dot_general(halves_of(C3, 4), grad, turned, preferred_element_type=F32)
    return mixed.astype(BF16)


def section3_kernel(own_ref, up_ref, down_ref, weights_ref, out_ref, wide, stacked, terms):
    @pl.when(on_segment(3))
    def _():
        for place, (ref, first) in enumerate(((up_ref, 2), (own_ref, 4), (down_ref, 2))):
            wide[:, cols(2 * place, 2)] = spread_top(ref[:, cols(first)])
        for half in range(2):
            stack_moved(
                lambda row: wide[64 * half : 64 * half + 64, cols(row)],
                stacked.at[192 * half : 192 * half + 192],
                64,
                6,
                (0, 1, 2),
            )
        terms[...] = dot(weights_ref[...], stacked[...])
        unit = spread(LANES, LANES, lambda e: 2 * e, lambda e: e < 64)
        last = is_last_block()
        for cell_z in range(-1, 3):
            for cell_y in range(4):
                total = None
                for tap_z, place_z in taps_of(cell_z, -1, 1):
                    for tap_y, place_y in taps_of(cell_y, 0, 1):
                        first = C3 * (3 * tap_z + tap_y)
                        part = terms[first : first + C3, cols(2 * (place_z + 1) + place_y)]
                        total = part if total is None else total + part
                if cell_z == -1:
                    mask = up_ref[:, cols(cell_y // 2)]
                elif cell_z == 2:
                    mask = down_ref[:, cols(cell_y // 2)]
                else:
                    mask = own_ref[:, cols(2 * cell_z + cell_y // 2)]
                result = sloped(total, half_row(mask, cell_y % 2))
                if cell_z == 2:
                    result = jnp.where(last, jnp.zeros_like(result), result)
                out_ref[:, cols(4 * (cell_z + 1) + cell_y)] = dot(result, unit).astype(BF16)


def section21_kernel(
    grad_ref,
    up_ref,
    down_ref,
    own_ref,
    weights_ref,
    next_ref,
    out1_ref,
    out0_ref,
    stacked,
    terms,
    middle,
    next_weights,
    next_stacked,
    next_terms,
):
    @pl.when(on_segment(2))
    def _():
        ordered = quarters(grad_ref[...])
        for part in range(4):
            stack_moved(
                lambda row: ordered[16 * part : 16 * part + 16, cols(row)],
                stacked.at[48 * part : 48 * part + 48],
                16,
                16,
                (0, 1, 2),
            )
        terms[...] = dot(weights_ref[...], stacked[...])
        last = is_last_block()
        for cell_z in range(-1, 5):
            for cell_y in range(8):
                total = None
                for tap_z, place_z in taps_of(cell_z, -1, 2):
                    for tap_y, place_y in taps_of(cell_y, 0, 3):
                        first = C2 * (3 * tap_z + tap_y)
                        part = terms[first : first + C2, cols(4 * (place_z + 1) + place_y)]
                        total = part if total is None else total + part
                if cell_z == -1:
                    mask = plane_of_message(up_ref, C2, cell_y)
                elif cell_z == 4:
                    mask = plane_of_message(down_ref, C2, cell_y)
                else:
                    mask = own_ref[:, cols(8 * cell_z + cell_y)]
                result = sloped(total, mask.astype(F32))
                if cell_z == 4:
                    result = jnp.where(last, jnp.zeros_like(result), result)
                middle[:, cols(8 * (cell_z + 1) + cell_y)] = result
                if 0 <= cell_z < 4:
                    out1_ref[:, cols(8 * cell_z + cell_y)] = result
        stack_moved(lambda row: middle[:, cols(row)], next_stacked, C2, 48, (-1, 0, 1))
        for tap in range(9):
            next_weights[C1 * tap : C1 * (tap + 1), :] = next_ref[:, cols(32 + tap)]
        next_terms[...] = dot(next_weights[:, :96], next_stacked[...])
        edge = jnp.zeros((C1, LANES), F32)
        for plane in range(4):
            sums = []
            for tap_y in range(3):
                total = None
                for tap_z in range(3):
                    first = C1 * (3 * tap_z + tap_y)
                    part = next_terms[first : first + C1, cols(8 * (plane + 2 - tap_z), 8)]
                    total = part if total is None else total + part
                sums.append(total)
            later = jnp.concatenate([sums[0][:, LANES:], edge], 1)
            earlier = jnp.concatenate([edge, sums[2][:, : 7 * LANES]], 1)
            mask = next_ref[:, cols(8 * plane, 8)].astype(F32)
            out0_ref[:, cols(8 * plane, 8)] = sloped(sums[1] + later + earlier, mask)


def weights2_kernel(scale, grad_ref, up_ref, down_ref, own_ref, out_ref, stacked, acts):
    @pl.when(on_segment(2))
    def _():
        ordered = quarters(grad_ref[:, cols(4, 8)])
        stack_moved(lambda row: ordered[:, cols(row)], stacked, C3, 8, (0, 1, 2))
        for tap_z in range(3):
            for tap_y in range(3):
                first = C2 * (3 * tap_z + tap_y)
                for place_z in range(2):
                    for place_y in range(4):
                        plane, row = 2 * place_z + tap_z, 2 * place_y + tap_y
                        if row == 8:
                            block = jnp.zeros((C2, LANES), BF16)
                        elif plane == 4:
                            block = plane_of_message(down_ref, C2, row)
                        else:
                            block = own_ref[:, cols(8 * plane + row)]
                        acts[first : first + C2, cols(4 * place_z + place_y)] = block
        total = dot_rows(stacked[...], acts[...]) * scale
        for group in range(9):
            for tap_x in range(3):
                first = 16 * (3 * group + tap_x)
                for part in range(4):
                    row = C3 * tap_x + 16 * part
                    out_ref[first : first + 16, 32 * part : 32 * part + 32] = total[
                        row : row + 16, 32 * group : 32 * group + 32
                    ]


def fine_acts(chans, up_ref, down_ref, own_ref, plane, row):
    if plane == -1:
        return plane_of_message(up_ref, chans, row)
    if plane == 4:
        return plane_of_message(down_ref, chans, row)
    return own_ref[:chans, cols(8 * plane + row)]


def weights01_kernel(
    scale1, scale0, grad0_ref, grad1_ref, up_ref, down_ref, own_ref, out_ref, stacked, acts
):
    none = jnp.zeros((C1, LANES), BF16)

    @pl.when(on_segment(0))
    def _():
        for place, distance in enumerate((-1, 0, 1)):
            for plane in range(4):
                for row in range(8):
                    block = grad0_ref[:, cols(8 * plane + row)]
                    block = moved_lanes(block, distance) if distance else block
                    for tap_y in range(3):
                        first = C1 * (3 * tap_y + place)
                        target = row + tap_y - 1
                        if 0 <= target < 8:
                            acts[first : first + C1, cols(8 * plane + target)] = block
                    if row == 0:
                        acts[C1 * (6 + place) : C1 * (7 + place), cols(8 * plane)] = none
                    if row == 7:
                        acts[C1 * place : C1 * (place + 1), cols(8 * plane + 7)] = none
        for tap_z in range(3):
            for plane in range(4):
                for row in range(8):
                    stacked[C1 * tap_z : C1 * (tap_z + 1), cols(8 * plane + row)] = fine_acts(
                        C1, up_ref, down_ref, own_ref, plane + tap_z - 1, row
                    )
        out_ref[:, :48] = dot_rows(acts[...], stacked[:48, :]) * scale0
        out_ref[:, 48:] = jnp.zeros((144, 80), F32)

    @pl.when(on_segment(1))
    def _():
        stack_moved(lambda row: grad1_ref[:, cols(row)], stacked, C2, 32, (-1, 0, 1))
        for tap_z in range(3):
            for tap_y in range(3):
                first = C1 * (3 * tap_z + tap_y)
                for plane in range(4):
                    for row in range(8):
                        source = row + tap_y - 1
                        block = none
                        if 0 <= source < 8:
                            block = fine_acts(
                                C1, up_ref, down_ref, own_ref, plane + tap_z - 1, source
                            )
                        acts[first : first + C1, cols(8 * plane + row)] = block
        out_ref[:, :96] = dot_rows(acts[...], stacked[...]) * scale1
        out_ref[:, 96:] = jnp.zeros((144, 32), F32)


def weights3_kernel(scale, places, blocks_ref, down_ref, out_ref, wide, stacked, acts):
    @pl.when(on_segment(3))
    def _():
        me = lax.axis_index("space")
        count = len(places)

        def held(block):
            wanted = lax.bitwise_xor(me, block)
            position = 0
            for bit, value in places_bits(places):
                position = position + value * lax.rem(lax.div(wanted, bit), 2)
            return blocks_ref[position]

        zero = jnp.zeros((64, LANES), BF16)
        for block in range(count):
            here = blocks_ref[0] if count == 1 else held(block)
            wide[:, cols(2 * block, 2)] = spread_top(here[:, cols(4)])
            rows = [half_row(here[:, cols(r // 2)], r % 2).astype(BF16) for r in range(8)]
            if count == 1:
                after = down_ref[:, : 2 * LANES]
            elif block + 1 < count:
                after = held(block + 1)[:, : 2 * LANES]
            else:
                after = None
            for r in range(4):
                rows.append(
                    zero if after is None else half_row(after[:, cols(r // 2)], r % 2).astype(BF16)
                )
            for tap_z in range(3):
                for tap_y in range(3):
                    first = C3 * (3 * tap_z + tap_y)
                    for place_y in range(2):
                        row = 2 * place_y + tap_y
                        source = zero if row == 4 else rows[4 * tap_z + row]
                        acts[first : first + C3, cols(2 * block + place_y)] = source
        stack_moved(lambda row: wide[:, cols(row)], stacked, C4, 2 * count, (0, 1, 2))
        total = dot_rows(stacked[...], acts[...]) * scale
        for group in range(9):
            for tap_x in range(3):
                first = 64 * (3 * group + tap_x)
                for part in range(2):
                    row = C4 * tap_x + 64 * part
                    out_ref[first : first + 64, 64 * part : 64 * part + 64] = total[
                        row : row + 64, C3 * group : C3 * group + C3
                    ]


def places_bits(places):
    count = len(places)
    bits = []
    bit = 1
    while bit < count:
        bits.append((bit, places.index(bit)))
        bit *= 2
    return bits


def call(kernel, outs, scratch, *args, flops, far=()):
    shapes = [jax.ShapeDtypeStruct(*entry) for entry in outs]
    moved = sum(a.size * a.dtype.itemsize for a in [*args, *shapes])
    near_spec = pl.BlockSpec(memory_space=pltpu.VMEM)
    far_spec = pl.BlockSpec(memory_space=pltpu.HBM)
    return pl.pallas_call(
        kernel,
        out_shape=shapes,
        in_specs=[far_spec if place in far else near_spec for place in range(len(args))],
        scratch_shapes=[
            pltpu.VMEM(*entry) if isinstance(entry, tuple) else entry for entry in scratch
        ],
        compiler_params=pltpu.CompilerParams(vmem_limit_bytes=VMEM_LIMIT),
        cost_estimate=pl.CostEstimate(flops=flops, bytes_accessed=moved, transcendentals=0),
    )(*args)


def pairs_of(segments, route):
    total = lax.axis_size("segment")
    count = lax.axis_size("space")
    return [
        (a * total + s, b * total + s) for a, b in route(count) for s in segments
    ]


def over_space(block, segments, route):
    return lax.ppermute(block, ("space", "segment"), pairs_of(segments, route))


def filled(ordered):
    rows = ordered.reshape(-1, LANES) if ordered.size % LANES == 0 else None
    if rows is None:
        flat = ordered.reshape(-1)
        rows = jnp.pad(flat, (0, -flat.shape[0] % LANES)).reshape(-1, LANES)
    return rows


def shards(saved_inputs, conv_weights, top_gradient):
    segment = lax.axis_index("segment")
    count = lax.axis_size("space")
    room = conv_weights.shape[1]
    scales = [1.0 / math.sqrt(count * cells) for cells in (4096, 4096, 512, 64)]

    def later(n):
        return [(i, i + 1) for i in range(n - 1)]

    def sooner(n):
        return [(i + 1, i) for i in range(n - 1)]

    def behind(values, *leaders):
        return lax.optimization_barrier((*values, *leaders))[: len(values)]

    saved_inputs = pltpu.with_memory_space_constraint(saved_inputs, pltpu.HBM)
    conv_weights = pltpu.with_memory_space_constraint(conv_weights, pltpu.HBM)
    top = jnp.transpose(top_gradient[:, 0], (1, 2, 0)).reshape(64, C4)
    top = pltpu.with_memory_space_constraint(top, pltpu.HBM)
    deep, up, down, own2, own01 = call(
        layout_kernel,
        [
            ((64, 640), BF16),
            ((64, 512), BF16),
            ((64, 512), BF16),
            ((32, 4096), BF16),
            ((16, 5248), BF16),
        ],
        [
            ((1, 131072), BF16),
            ((1, 13824), BF16),
            ((64, 4096), F32),
            ((128, 128), F32),
            ((144, 128), F32),
            ((64, 128), BF16),
            pltpu.SemaphoreType.DMA,
            pltpu.SemaphoreType.DMA,
        ],
        saved_inputs,
        conv_weights,
        top,
        flops=0,
        far=(0, 1, 2),
    )
    up = over_space(up, range(4), later)
    down = over_space(down, range(4), sooner)
    next_own = lax.ppermute(own01, "segment", [(1, 2)])
    (weights,) = behind((conv_weights,), deep)
    taps3, taps2 = call(
        weights_layout_kernel,
        [((576, 384), BF16), ((288, 192), BF16)],
        [((1, 221184), BF16), ((1728, 128), F32), pltpu.SemaphoreType.DMA],
        weights,
        flops=0,
        far=(0,),
    )
    taps3, taps2 = behind((taps3, taps2), next_own)

    (grad2,) = call(
        section3_kernel,
        [((64, 2048), BF16)],
        [((128, 768), BF16), ((384, 768), BF16), ((576, 768), F32)],
        deep,
        up,
        down,
        taps3,
        flops=2 * 576 * 384 * 768,
    )
    grad2 = lax.ppermute(grad2, "segment", [(3, 2)])
    grad1, grad0 = call(
        section21_kernel,
        [((32, 4096), BF16), ((16, 4096), BF16)],
        [
            ((192, 2048), BF16),
            ((288, 2048), F32),
            ((32, 6144), BF16),
            ((144, 128), BF16),
            ((96, 6144), BF16),
            ((144, 6144), F32),
        ],
        grad2,
        up,
        down,
        own2,
        taps2,
        next_own,
        flops=2 * 288 * 192 * 2048,
    )
    def swap(block, segments, bit):
        return over_space(block, segments, lambda n: [(i, i ^ bit) for i in range(n)])

    grad2, blocks = behind((grad2, deep[None]), grad1)
    grad0 = lax.ppermute(grad0, "segment", [(2, 0)])
    grad1 = lax.ppermute(grad1, "segment", [(2, 1)])
    (sum2,) = call(
        functools.partial(weights2_kernel, scales[2]),
        [((432, 128), F32)],
        [((192, 1024), BF16), ((288, 1024), BF16)],
        grad2,
        up,
        down,
        own2,
        flops=LONG,
    )
    places = [0]
    even = not count & (count - 1)
    gathers = even and count <= GATHER_LIMIT
    bits = [1 << power for power in range(count.bit_length() - 1)] if even else []

    def gathered(blocks, bit):
        return jnp.concatenate([blocks, swap(blocks, [3], bit)], 0)

    if gathers:
        for bit in bits[:0:-1]:
            blocks = gathered(blocks, bit)
            places = places + [place ^ bit for place in places]
    grad0, grad1 = behind((grad0, grad1), sum2, blocks)
    (sum01,) = call(
        functools.partial(weights01_kernel, scales[1], scales[0]),
        [((144, 128), F32)],
        [((96, 4096), BF16), ((144, 4096), BF16)],
        grad0,
        grad1,
        up,
        down,
        own01,
        flops=2 * 144 * 96 * 6144,
    )
    for bit in bits:
        sum2 = sum2 + swap(sum2, [2], bit)
    if not even:
        sum2 = lax.psum(sum2, "space")
        sum01 = lax.psum(sum01, "space")
    if gathers:
        blocks = gathered(blocks, bits[0])
        places = places + [place ^ bits[0] for place in places]
    for bit in bits:
        sum01 = sum01 + swap(sum01, [0, 1], bit)
    held = len(places)
    (sum3,) = call(
        functools.partial(weights3_kernel, scales[3], places),
        [((1728, 128), F32)],
        [((128, 256 * held), BF16), ((384, 256 * held), BF16), ((576, 256 * held), BF16)],
        blocks,
        down,
        flops=LONG,
    )
    if held < count:
        sum3 = lax.psum(sum3, "space")

    def finish0(sum01, sum2, sum3):
        parts = sum01[:, :48].reshape(3, 3, C1, 3, 16)[..., :C0]
        return filled(jnp.transpose(parts, (3, 0, 1, 2, 4)))

    def finish1(sum01, sum2, sum3):
        parts = sum01[:, :96].reshape(9, C1, 3, C2)
        return filled(jnp.transpose(parts, (0, 2, 3, 1)))

    def whole(finish):
        def branch(*sums):
            rows = finish(*sums)
            return jnp.pad(rows, ((0, room // LANES - rows.shape[0]), (0, 0)))

        return branch

    ends = [finish0, finish1, lambda a, b, c: b, lambda a, b, c: c]
    rows = lax.switch(segment, [whole(end) for end in ends], sum01, sum2, sum3)
    return rows.reshape(1, room)


def solution(mesh):
    return jax.shard_map(
        shards,
        mesh=mesh,
        in_specs=(P("segment", "space"), P("segment", None), P(None, "space", None, None)),
        out_specs=P("segment", None),
        check_vma=False,
    )
```

```python
import functools
import math

import jax
import jax.numpy as jnp
from jax import lax
from jax.experimental import pallas as pl
from jax.experimental.pallas import tpu as pltpu
from jax.sharding import PartitionSpec as P

C0, C1, C2, C3, C4 = 4, 16, 32, 64, 128
LANES = 128
SLOPE = 0.3
BF16 = jnp.bfloat16
F32 = jnp.float32
GATHER_LIMIT = 8
VMEM_LIMIT = 48 * 1024 * 1024
LONG = 20_000_000_000


def on_segment(index):
    return lax.axis_index("segment") == index


def is_last_block():
    return lax.axis_index("space") == lax.axis_size("space") - 1


def cols(row, count=1):
    return slice(LANES * row, LANES * (row + count))


def moved_lanes(block, distance):
    lane = lax.broadcasted_iota(jnp.int32, block.shape, 1)
    rolled = pltpu.roll(block.astype(F32), distance % LANES, 1)
    kept = lane >= distance if distance > 0 else lane < LANES + distance
    return jnp.where(kept, rolled, 0.0).astype(BF16)


def stack_moved(read, target, chans, rows, distances):
    for row in range(rows):
        block = read(row)
        for place, distance in enumerate(distances):
            moved = moved_lanes(block, distance) if distance else block
            target[place * chans : (place + 1) * chans, cols(row)] = moved


def spread(rows_in, rows_out, source, bound):
    entry = lax.broadcasted_iota(jnp.int32, (rows_in, rows_out), 0)
    place = lax.broadcasted_iota(jnp.int32, (rows_in, rows_out), 1)
    return jnp.where((place == source(entry)) & bound(entry), 1.0, 0.0).astype(BF16)


def taps_of(cell, low, high):
    if cell % 2:
        pairs = [(1, (cell - 1) // 2)]
    else:
        pairs = [(0, cell // 2), (2, cell // 2 - 1)]
    return [(tap, place) for tap, place in pairs if low <= place <= high]


def dot_rows(left, right):
    return lax.dot_general(left, right, (((1,), (1,)), ((), ())), preferred_element_type=F32)


def dot(left, right):
    return jnp.dot(left, right, preferred_element_type=F32)


def sloped(total, activation):
    return (total * jnp.where(activation > 0, 1.0, SLOPE)).astype(BF16)


def half_row(block, odd):
    lane = lax.broadcasted_iota(jnp.int32, block.shape, 1)
    wide = block.astype(F32)
    if odd:
        wide = pltpu.roll(wide, LANES // 2, 1)
    return jnp.where(lane < LANES // 2, wide, 0.0)


def plane_of_message(ref, chans, row):
    return ref[32 * (row // 4) : 32 * (row // 4) + chans, cols(row % 4)]


def spread_top(block):
    block = dot(block, halves_of(C4, 2)).astype(BF16)
    unit = spread(64, 2 * LANES, lambda e: LANES * (e // 32) + 2 * (e % 32), lambda e: e >= 0)
    turned = (((0,), (0,)), ((), ()))
    return lax.dot_general(block, unit, turned, preferred_element_type=F32).astype(BF16)


def copy_rows(saved_ref, wide, chans, width):
    for chan in range(chans):
        source = saved_ref[:, chan * width : (chan + 1) * width]
        wide[chan : chan + 1, :width] = source.astype(F32)


def fetched(far_ref, near_ref, size, arrived):
    part = pl.ds(0, size)
    copy = pltpu.make_async_copy(far_ref.at[:, part], near_ref.at[:, part], arrived)
    copy.start()
    copy.wait()


def weight_rows(held, wide, rows):
    for tap in range(27):
        first = LANES * rows * tap
        wide[rows * tap : rows * tap + rows, :] = (
            held[:, first : first + LANES * rows].astype(F32).reshape(rows, LANES)
        )


def layout_kernel(
    saved_ref,
    weights_ref,
    top_ref,
    deep_ref,
    up_ref,
    down_ref,
    own2_ref,
    own01_ref,
    held,
    held_weights,
    wide,
    wide_weights,
    mixed,
    held_top,
    arrived,
    arrived_top,
):
    def fetch(size):
        fetched(saved_ref, held, size, arrived)

    def send(place, plane, target_ref):
        for half in range(2):
            target_ref[32 * half : 32 * half + place, :] = wide[
                :place, cols(8 * plane + 4 * half, 4)
            ].astype(BF16)

    @pl.when(on_segment(3))
    def _():
        copy = pltpu.make_async_copy(top_ref, held_top, arrived_top)
        copy.start()
        fetch(C3 * 512)
        copy_rows(held, wide, C3, 512)
        block = wide[:, :512].astype(BF16)
        copy.wait()
        top = held_top[...]
        deep_ref[:, :512] = block
        deep_ref[:, 512:] = top
        for ref, half in ((up_ref, block[:, 256:]), (down_ref, block[:, :256])):
            ref[:, :256] = half
            ref[:, 256:384] = top
            ref[:, 384:] = jnp.zeros((64, LANES), BF16)

    for section, chans in enumerate((C0, C1, C2)):

        @pl.when(on_segment(section))
        def _(section=section, chans=chans):
            if section == 0:
                wide[:C1, :] = jnp.zeros((C1, 4096), F32)
            fetch(chans * 4096)
            copy_rows(held, wide, chans, 4096)
            place = max(chans, C1)
            own_ref = own2_ref if section == 2 else own01_ref
            own_ref[:, :4096] = wide[:place, :].astype(BF16)
            if section == 1:
                fetched(weights_ref, held_weights, 27 * C1 * C2, arrived)
                weight_rows(held_weights, wide_weights, 4)
                turned = jnp.transpose(wide_weights[...])
                mixed[...] = jnp.zeros((144, LANES), F32)
                for group in range(9):
                    for part in range(8):
                        mixed[16 * group : 16 * group + 16, 12 * part : 12 * part + 12] = turned[
                            16 * part : 16 * part + 16, 12 * group : 12 * group + 12
                        ]
                ordered = spread(
                    LANES,
                    LANES,
                    lambda e: 32 * ((e % 12) // 4) + 8 * (e % 4) + e // 12,
                    lambda e: e < 96,
                )
                taps = dot(mixed[...].astype(BF16), ordered).astype(BF16)
                for group in range(9):
                    own01_ref[:, cols(32 + group)] = taps[16 * group : 16 * group + 16, :]
            send(place, 3, up_ref)
            send(place, 0, down_ref)


def weights_layout_kernel(weights_ref, out3_ref, out2_ref, held, wide, arrived):
    @pl.when(on_segment(3))
    def _():
        fetched(weights_ref, held, 27 * C3 * C4, arrived)
        weight_rows(held, wide, 64)
        for group in range(9):
            turned = jnp.transpose(wide[192 * group : 192 * group + 192, :]).astype(BF16)
            rows = slice(C3 * group, C3 * group + C3)
            for part in range(2):
                out3_ref[rows, 192 * part : 192 * part + 192] = turned[64 * part : 64 * part + 64]

    @pl.when(on_segment(2))
    def _():
        fetched(weights_ref, held, 27 * C2 * C3, arrived)
        weight_rows(held, wide, 16)
        for group in range(9):
            turned = jnp.transpose(wide[48 * group : 48 * group + 48, :]).astype(BF16)
            rows = slice(C2 * group, C2 * group + C2)
            for part in range(4):
                out2_ref[rows, 48 * part : 48 * part + 48] = turned[32 * part : 32 * part + 32]


def halves_of(channels, parts):
    size = channels // parts
    return spread(channels, channels, lambda e: (e % parts) * size + e // parts, lambda e: e >= 0)


def quarters(grad):
    turned = (((0,), (0,)), ((), ()))
    mixed = lax.dot_general(halves_of(C3, 4), grad, turned, preferred_element_type=F32)
    return mixed.astype(BF16)


def section3_kernel(own_ref, up_ref, down_ref, weights_ref, out_ref, wide, stacked, terms):
    @pl.when(on_segment(3))
    def _():
        for place, (ref, first) in enumerate(((up_ref, 2), (own_ref, 4), (down_ref, 2))):
            wide[:, cols(2 * place, 2)] = spread_top(ref[:, cols(first)])
        for half in range(2):
            stack_moved(
                lambda row: wide[64 * half : 64 * half + 64, cols(row)],
                stacked.at[192 * half : 192 * half + 192],
                64,
                6,
                (0, 1, 2),
            )
        terms[...] = dot(weights_ref[...], stacked[...])
        unit = spread(LANES, LANES, lambda e: 2 * e, lambda e: e < 64)
        last = is_last_block()
        for cell_z in range(-1, 3):
            for cell_y in range(4):
                total = None
                for tap_z, place_z in taps_of(cell_z, -1, 1):
                    for tap_y, place_y in taps_of(cell_y, 0, 1):
                        first = C3 * (3 * tap_z + tap_y)
                        part = terms[first : first + C3, cols(2 * (place_z + 1) + place_y)]
                        total = part if total is None else total + part
                if cell_z == -1:
                    mask = up_ref[:, cols(cell_y // 2)]
                elif cell_z == 2:
                    mask = down_ref[:, cols(cell_y // 2)]
                else:
                    mask = own_ref[:, cols(2 * cell_z + cell_y // 2)]
                result = sloped(total, half_row(mask, cell_y % 2))
                if cell_z == 2:
                    result = jnp.where(last, jnp.zeros_like(result), result)
                out_ref[:, cols(4 * (cell_z + 1) + cell_y)] = dot(result, unit).astype(BF16)


def section21_kernel(
    scale2,
    scale1,
    grad_ref,
    up_ref,
    down_ref,
    own_ref,
    weights_ref,
    next_ref,
    out0_ref,
    sum2_ref,
    sum1_ref,
    stacked,
    terms,
    middle,
    next_weights,
    next_stacked,
    next_terms,
    acts2,
    acts1,
):
    @pl.when(on_segment(2))
    def _():
        ordered = quarters(grad_ref[...])
        for part in range(4):
            stack_moved(
                lambda row: ordered[16 * part : 16 * part + 16, cols(row)],
                stacked.at[48 * part : 48 * part + 48],
                16,
                16,
                (0, 1, 2),
            )
        terms[...] = dot(weights_ref[...], stacked[...])
        last = is_last_block()
        for cell_z in range(-1, 5):
            for cell_y in range(8):
                total = None
                for tap_z, place_z in taps_of(cell_z, -1, 2):
                    for tap_y, place_y in taps_of(cell_y, 0, 3):
                        first = C2 * (3 * tap_z + tap_y)
                        part = terms[first : first + C2, cols(4 * (place_z + 1) + place_y)]
                        total = part if total is None else total + part
                if cell_z == -1:
                    mask = plane_of_message(up_ref, C2, cell_y)
                elif cell_z == 4:
                    mask = plane_of_message(down_ref, C2, cell_y)
                else:
                    mask = own_ref[:, cols(8 * cell_z + cell_y)]
                result = sloped(total, mask.astype(F32))
                if cell_z == 4:
                    result = jnp.where(last, jnp.zeros_like(result), result)
                middle[:, cols(8 * (cell_z + 1) + cell_y)] = result
        stack_moved(lambda row: middle[:, cols(row)], next_stacked, C2, 48, (-1, 0, 1))
        for tap in range(9):
            next_weights[C1 * tap : C1 * (tap + 1), :] = next_ref[:, cols(32 + tap)]
        next_terms[...] = dot(next_weights[:, :96], next_stacked[...])
        edge = jnp.zeros((C1, LANES), F32)
        for plane in range(4):
            sums = []
            for tap_y in range(3):
                total = None
                for tap_z in range(3):
                    first = C1 * (3 * tap_z + tap_y)
                    part = next_terms[first : first + C1, cols(8 * (plane + 2 - tap_z), 8)]
                    total = part if total is None else total + part
                sums.append(total)
            later = jnp.concatenate([sums[0][:, LANES:], edge], 1)
            earlier = jnp.concatenate([edge, sums[2][:, : 7 * LANES]], 1)
            mask = next_ref[:, cols(8 * plane, 8)].astype(F32)
            out0_ref[:, cols(8 * plane, 8)] = sloped(sums[1] + later + earlier, mask)
        for tap_z in range(3):
            for tap_y in range(3):
                first = C2 * (3 * tap_z + tap_y)
                for place_z in range(2):
                    for place_y in range(4):
                        plane, row = 2 * place_z + tap_z, 2 * place_y + tap_y
                        if row == 8:
                            block = jnp.zeros((C2, LANES), BF16)
                        elif plane == 4:
                            block = plane_of_message(down_ref, C2, row)
                        else:
                            block = own_ref[:, cols(8 * plane + row)]
                        acts2[first : first + C2, cols(4 * place_z + place_y)] = block
        total = dot_rows(stacked[:, 512:1536], acts2[...]) * scale2
        for group in range(9):
            for tap_x in range(3):
                first = 16 * (3 * group + tap_x)
                for part in range(4):
                    row = 48 * part + 16 * tap_x
                    sum2_ref[first : first + 16, 32 * part : 32 * part + 32] = total[
                        row : row + 16, 32 * group : 32 * group + 32
                    ]
        none = jnp.zeros((C1, LANES), BF16)
        for tap_y in range(3):
            for plane in range(4):
                for row in range(8):
                    source = row + tap_y - 1
                    inside = 0 <= source < 8
                    acts1[C1 * tap_y : C1 * (tap_y + 1), cols(8 * plane + row)] = (
                        next_ref[:, cols(8 * plane + source)] if inside else none
                    )
        for tap_z in range(3):
            grads = next_stacked[:, cols(8 * (2 - tap_z), 32)]
            sum1_ref[48 * tap_z : 48 * tap_z + 48, :96] = dot_rows(acts1[...], grads) * scale1
        sum1_ref[:, 96:] = jnp.zeros((144, 32), F32)


def fine_acts(chans, up_ref, down_ref, own_ref, plane, row):
    if plane == -1:
        return plane_of_message(up_ref, chans, row)
    if plane == 4:
        return plane_of_message(down_ref, chans, row)
    return own_ref[:chans, cols(8 * plane + row)]


def weights01_kernel(
    scale, grad0_ref, sum1_ref, up_ref, down_ref, own_ref, out_ref, stacked, acts
):
    none = jnp.zeros((C1, LANES), BF16)

    @pl.when(on_segment(0))
    def _():
        for place, distance in enumerate((-1, 0, 1)):
            for plane in range(4):
                for row in range(8):
                    block = grad0_ref[:, cols(8 * plane + row)]
                    block = moved_lanes(block, distance) if distance else block
                    for tap_y in range(3):
                        first = C1 * (3 * tap_y + place)
                        target = row + tap_y - 1
                        if 0 <= target < 8:
                            acts[first : first + C1, cols(8 * plane + target)] = block
                    if row == 0:
                        acts[C1 * (6 + place) : C1 * (7 + place), cols(8 * plane)] = none
                    if row == 7:
                        acts[C1 * place : C1 * (place + 1), cols(8 * plane + 7)] = none
        for tap_z in range(3):
            for plane in range(4):
                for row in range(8):
                    stacked[C1 * tap_z : C1 * (tap_z + 1), cols(8 * plane + row)] = fine_acts(
                        C1, up_ref, down_ref, own_ref, plane + tap_z - 1, row
                    )
        out_ref[:, :48] = dot_rows(acts[...], stacked[...]) * scale
        out_ref[:, 48:] = jnp.zeros((144, 80), F32)

    @pl.when(on_segment(1))
    def _():
        out_ref[...] = sum1_ref[...]


def weights3_kernel(scale, places, blocks_ref, down_ref, out_ref, wide, stacked, acts):
    @pl.when(on_segment(3))
    def _():
        me = lax.axis_index("space")
        count = len(places)

        def held(block):
            wanted = lax.bitwise_xor(me, block)
            position = 0
            for bit, value in places_bits(places):
                position = position + value * lax.rem(lax.div(wanted, bit), 2)
            return blocks_ref[position]

        zero = jnp.zeros((64, LANES), BF16)
        for block in range(count):
            here = blocks_ref[0] if count == 1 else held(block)
            wide[:, cols(2 * block, 2)] = spread_top(here[:, cols(4)])
            rows = [half_row(here[:, cols(r // 2)], r % 2).astype(BF16) for r in range(8)]
            if count == 1:
                after = down_ref[:, : 2 * LANES]
            elif block + 1 < count:
                after = held(block + 1)[:, : 2 * LANES]
            else:
                after = None
            for r in range(4):
                rows.append(
                    zero if after is None else half_row(after[:, cols(r // 2)], r % 2).astype(BF16)
                )
            for tap_z in range(3):
                for tap_y in range(3):
                    first = C3 * (3 * tap_z + tap_y)
                    for place_y in range(2):
                        row = 2 * place_y + tap_y
                        source = zero if row == 4 else rows[4 * tap_z + row]
                        acts[first : first + C3, cols(2 * block + place_y)] = source
        stack_moved(lambda row: wide[:, cols(row)], stacked, C4, 2 * count, (0, 1, 2))
        total = dot_rows(stacked[...], acts[...]) * scale
        for group in range(9):
            for tap_x in range(3):
                first = 64 * (3 * group + tap_x)
                for part in range(2):
                    row = C4 * tap_x + 64 * part
                    out_ref[first : first + 64, 64 * part : 64 * part + 64] = total[
                        row : row + 64, C3 * group : C3 * group + C3
                    ]


def places_bits(places):
    count = len(places)
    bits = []
    bit = 1
    while bit < count:
        bits.append((bit, places.index(bit)))
        bit *= 2
    return bits


def call(kernel, outs, scratch, *args, flops, far=()):
    shapes = [jax.ShapeDtypeStruct(*entry) for entry in outs]
    moved = sum(a.size * a.dtype.itemsize for a in [*args, *shapes])
    near_spec = pl.BlockSpec(memory_space=pltpu.VMEM)
    far_spec = pl.BlockSpec(memory_space=pltpu.HBM)
    return pl.pallas_call(
        kernel,
        out_shape=shapes,
        in_specs=[far_spec if place in far else near_spec for place in range(len(args))],
        scratch_shapes=[
            pltpu.VMEM(*entry) if isinstance(entry, tuple) else entry for entry in scratch
        ],
        compiler_params=pltpu.CompilerParams(vmem_limit_bytes=VMEM_LIMIT),
        cost_estimate=pl.CostEstimate(flops=flops, bytes_accessed=moved, transcendentals=0),
    )(*args)


def pairs_of(segments, route):
    total = lax.axis_size("segment")
    count = lax.axis_size("space")
    return [
        (a * total + s, b * total + s) for a, b in route(count) for s in segments
    ]


def over_space(block, segments, route):
    return lax.ppermute(block, ("space", "segment"), pairs_of(segments, route))


def filled(ordered):
    rows = ordered.reshape(-1, LANES) if ordered.size % LANES == 0 else None
    if rows is None:
        flat = ordered.reshape(-1)
        rows = jnp.pad(flat, (0, -flat.shape[0] % LANES)).reshape(-1, LANES)
    return rows


def shards(saved_inputs, conv_weights, top_gradient):
    segment = lax.axis_index("segment")
    count = lax.axis_size("space")
    room = conv_weights.shape[1]
    scales = [1.0 / math.sqrt(count * cells) for cells in (4096, 4096, 512, 64)]

    def later(n):
        return [(i, i + 1) for i in range(n - 1)]

    def sooner(n):
        return [(i + 1, i) for i in range(n - 1)]

    def behind(values, *leaders):
        return lax.optimization_barrier((*values, *leaders))[: len(values)]

    saved_inputs = pltpu.with_memory_space_constraint(saved_inputs, pltpu.HBM)
    conv_weights = pltpu.with_memory_space_constraint(conv_weights, pltpu.HBM)
    top = jnp.transpose(top_gradient[:, 0], (1, 2, 0)).reshape(64, C4)
    top = pltpu.with_memory_space_constraint(top, pltpu.HBM)
    deep, up, down, own2, own01 = call(
        layout_kernel,
        [
            ((64, 640), BF16),
            ((64, 512), BF16),
            ((64, 512), BF16),
            ((32, 4096), BF16),
            ((16, 5248), BF16),
        ],
        [
            ((1, 131072), BF16),
            ((1, 13824), BF16),
            ((64, 4096), F32),
            ((128, 128), F32),
            ((144, 128), F32),
            ((64, 128), BF16),
            pltpu.SemaphoreType.DMA,
            pltpu.SemaphoreType.DMA,
        ],
        saved_inputs,
        conv_weights,
        top,
        flops=0,
        far=(0, 1, 2),
    )
    up = over_space(up, range(4), later)
    down = over_space(down, range(4), sooner)
    next_own = lax.ppermute(own01, "segment", [(1, 2)])
    (weights,) = behind((conv_weights,), deep)
    taps3, taps2 = call(
        weights_layout_kernel,
        [((576, 384), BF16), ((288, 192), BF16)],
        [((1, 221184), BF16), ((1728, 128), F32), pltpu.SemaphoreType.DMA],
        weights,
        flops=0,
        far=(0,),
    )
    taps3, taps2 = behind((taps3, taps2), next_own)

    (grad2,) = call(
        section3_kernel,
        [((64, 2048), BF16)],
        [((128, 768), BF16), ((384, 768), BF16), ((576, 768), F32)],
        deep,
        up,
        down,
        taps3,
        flops=2 * 576 * 384 * 768,
    )
    grad2 = lax.ppermute(grad2, "segment", [(3, 2)])
    grad0, sum2, sum1 = call(
        functools.partial(section21_kernel, scales[2], scales[1]),
        [((16, 4096), BF16), ((432, 128), F32), ((144, 128), F32)],
        [
            ((192, 2048), BF16),
            ((288, 2048), F32),
            ((32, 6144), BF16),
            ((144, 128), BF16),
            ((96, 6144), BF16),
            ((144, 6144), F32),
            ((288, 1024), BF16),
            ((48, 4096), BF16),
        ],
        grad2,
        up,
        down,
        own2,
        taps2,
        next_own,
        flops=2 * 288 * 192 * 2048,
    )
    def swap(block, segments, bit):
        return over_space(block, segments, lambda n: [(i, i ^ bit) for i in range(n)])

    (blocks,) = behind((deep[None],), grad0)
    grad0 = lax.ppermute(grad0, "segment", [(2, 0)])
    sum1 = lax.ppermute(sum1, "segment", [(2, 1)])
    places = [0]
    even = not count & (count - 1)
    gathers = even and count <= GATHER_LIMIT
    bits = [1 << power for power in range(count.bit_length() - 1)] if even else []

    def gathered(blocks, bit):
        return jnp.concatenate([blocks, swap(blocks, [3], bit)], 0)

    if gathers:
        for bit in bits[:0:-1]:
            blocks = gathered(blocks, bit)
            places = places + [place ^ bit for place in places]
    grad0, sum1 = behind((grad0, sum1), blocks)
    (sum01,) = call(
        functools.partial(weights01_kernel, scales[0]),
        [((144, 128), F32)],
        [((48, 4096), BF16), ((144, 4096), BF16)],
        grad0,
        sum1,
        up,
        down,
        own01,
        flops=2 * 144 * 96 * 6144,
    )
    for bit in bits:
        sum2 = sum2 + swap(sum2, [2], bit)
    if not even:
        sum2 = lax.psum(sum2, "space")
        sum01 = lax.psum(sum01, "space")
    if gathers:
        blocks = gathered(blocks, bits[0])
        places = places + [place ^ bits[0] for place in places]
    for bit in bits:
        sum01 = sum01 + swap(sum01, [0, 1], bit)
    held = len(places)
    (sum3,) = call(
        functools.partial(weights3_kernel, scales[3], places),
        [((1728, 128), F32)],
        [((128, 256 * held), BF16), ((384, 256 * held), BF16), ((576, 256 * held), BF16)],
        blocks,
        down,
        flops=LONG,
    )
    if held < count:
        sum3 = lax.psum(sum3, "space")

    def finish0(sum01, sum2, sum3):
        parts = sum01[:, :48].reshape(3, 3, C1, 3, 16)[..., :C0]
        return filled(jnp.transpose(parts, (3, 0, 1, 2, 4)))

    def finish1(sum01, sum2, sum3):
        parts = sum01[:, :96].reshape(9, C1, 3, C2)
        return filled(jnp.transpose(parts, (0, 2, 3, 1)))

    def whole(finish):
        def branch(*sums):
            rows = finish(*sums)
            return jnp.pad(rows, ((0, room // LANES - rows.shape[0]), (0, 0)))

        return branch

    ends = [finish0, finish1, lambda a, b, c: b, lambda a, b, c: c]
    rows = lax.switch(segment, [whole(end) for end in ends], sum01, sum2, sum3)
    return rows.reshape(1, room)


def solution(mesh):
    return jax.shard_map(
        shards,
        mesh=mesh,
        in_specs=(P("segment", "space"), P("segment", None), P(None, "space", None, None)),
        out_specs=P("segment", None),
        check_vma=False,
    )
```

```python
import functools
import math

import jax
import jax.numpy as jnp
from jax import lax
from jax.experimental import pallas as pl
from jax.experimental.pallas import tpu as pltpu
from jax.sharding import PartitionSpec as P

C0, C1, C2, C3, C4 = 4, 16, 32, 64, 128
LANES = 128
SLOPE = 0.3
BF16 = jnp.bfloat16
F32 = jnp.float32
GATHER_LIMIT = 8
VMEM_LIMIT = 48 * 1024 * 1024
LONG = 20_000_000_000


def on_segment(index):
    return lax.axis_index("segment") == index


def is_last_block():
    return lax.axis_index("space") == lax.axis_size("space") - 1


def cols(row, count=1):
    return slice(LANES * row, LANES * (row + count))


def moved_lanes(block, distance):
    lane = lax.broadcasted_iota(jnp.int32, block.shape, 1)
    rolled = pltpu.roll(block.astype(F32), distance % LANES, 1)
    kept = lane >= distance if distance > 0 else lane < LANES + distance
    return jnp.where(kept, rolled, 0.0).astype(BF16)


def stack_moved(read, target, chans, rows, distances):
    for row in range(rows):
        block = read(row)
        for place, distance in enumerate(distances):
            moved = moved_lanes(block, distance) if distance else block
            target[place * chans : (place + 1) * chans, cols(row)] = moved


def spread(rows_in, rows_out, source, bound):
    entry = lax.broadcasted_iota(jnp.int32, (rows_in, rows_out), 0)
    place = lax.broadcasted_iota(jnp.int32, (rows_in, rows_out), 1)
    return jnp.where((place == source(entry)) & bound(entry), 1.0, 0.0).astype(BF16)


def taps_of(cell, low, high):
    if cell % 2:
        pairs = [(1, (cell - 1) // 2)]
    else:
        pairs = [(0, cell // 2), (2, cell // 2 - 1)]
    return [(tap, place) for tap, place in pairs if low <= place <= high]


def dot_rows(left, right):
    return lax.dot_general(left, right, (((1,), (1,)), ((), ())), preferred_element_type=F32)


def dot(left, right):
    return jnp.dot(left, right, preferred_element_type=F32)


def sloped(total, activation):
    return (total * jnp.where(activation > 0, 1.0, SLOPE)).astype(BF16)


def half_row(block, odd):
    lane = lax.broadcasted_iota(jnp.int32, block.shape, 1)
    wide = block.astype(F32)
    if odd:
        wide = pltpu.roll(wide, LANES // 2, 1)
    return jnp.where(lane < LANES // 2, wide, 0.0)


def plane_of_message(ref, chans, row):
    return ref[32 * (row // 4) : 32 * (row // 4) + chans, cols(row % 4)]


def spread_top(block):
    block = dot(block, halves_of(C4, 2)).astype(BF16)
    unit = spread(64, 2 * LANES, lambda e: LANES * (e // 32) + 2 * (e % 32), lambda e: e >= 0)
    turned = (((0,), (0,)), ((), ()))
    return lax.dot_general(block, unit, turned, preferred_element_type=F32).astype(BF16)


def copy_rows(saved_ref, wide, chans, width):
    for chan in range(chans):
        source = saved_ref[:, chan * width : (chan + 1) * width]
        wide[chan : chan + 1, :width] = source.astype(F32)


def fetched(far_ref, near_ref, size, arrived):
    part = pl.ds(0, size)
    copy = pltpu.make_async_copy(far_ref.at[:, part], near_ref.at[:, part], arrived)
    copy.start()
    copy.wait()


def weight_rows(held, wide, rows):
    for tap in range(27):
        first = LANES * rows * tap
        wide[rows * tap : rows * tap + rows, :] = (
            held[:, first : first + LANES * rows].astype(F32).reshape(rows, LANES)
        )


def layout_kernel(
    saved_ref,
    weights_ref,
    top_ref,
    deep_ref,
    up_ref,
    down_ref,
    own2_ref,
    own01_ref,
    held,
    held_weights,
    wide,
    wide_weights,
    mixed,
    held_top,
    arrived,
    arrived_top,
):
    def fetch(size):
        fetched(saved_ref, held, size, arrived)

    def send(place, plane, target_ref):
        for half in range(2):
            target_ref[32 * half : 32 * half + place, :] = wide[
                :place, cols(8 * plane + 4 * half, 4)
            ].astype(BF16)

    @pl.when(on_segment(3))
    def _():
        copy = pltpu.make_async_copy(top_ref, held_top, arrived_top)
        copy.start()
        fetch(C3 * 512)
        copy_rows(held, wide, C3, 512)
        block = wide[:, :512].astype(BF16)
        copy.wait()
        top = held_top[...]
        deep_ref[:, :512] = block
        deep_ref[:, 512:] = top
        for ref, half in ((up_ref, block[:, 256:]), (down_ref, block[:, :256])):
            ref[:, :256] = half
            ref[:, 256:384] = top
            ref[:, 384:] = jnp.zeros((64, LANES), BF16)

    for section, chans in enumerate((C0, C1, C2)):

        @pl.when(on_segment(section))
        def _(section=section, chans=chans):
            if section == 0:
                wide[:C1, :] = jnp.zeros((C1, 4096), F32)
            fetch(chans * 4096)
            copy_rows(held, wide, chans, 4096)
            place = max(chans, C1)
            own_ref = own2_ref if section == 2 else own01_ref
            own_ref[:, :4096] = wide[:place, :].astype(BF16)
            if section == 1:
                fetched(weights_ref, held_weights, 27 * C1 * C2, arrived)
                weight_rows(held_weights, wide_weights, 4)
                turned = jnp.transpose(wide_weights[...])
                mixed[...] = jnp.zeros((144, LANES), F32)
                for group in range(9):
                    for part in range(8):
                        mixed[16 * group : 16 * group + 16, 12 * part : 12 * part + 12] = turned[
                            16 * part : 16 * part + 16, 12 * group : 12 * group + 12
                        ]
                ordered = spread(
                    LANES,
                    LANES,
                    lambda e: 32 * ((e % 12) // 4) + 8 * (e % 4) + e // 12,
                    lambda e: e < 96,
                )
                taps = dot(mixed[...].astype(BF16), ordered).astype(BF16)
                for group in range(9):
                    own01_ref[:, cols(32 + group)] = taps[16 * group : 16 * group + 16, :]
            send(place, 3, up_ref)
            send(place, 0, down_ref)


def weights_layout_kernel(weights_ref, out3_ref, out2_ref, held, wide, arrived):
    @pl.when(on_segment(3))
    def _():
        fetched(weights_ref, held, 27 * C3 * C4, arrived)
        weight_rows(held, wide, 64)
        for group in range(9):
            turned = jnp.transpose(wide[192 * group : 192 * group + 192, :]).astype(BF16)
            rows = slice(C3 * group, C3 * group + C3)
            for part in range(2):
                out3_ref[rows, 192 * part : 192 * part + 192] = turned[64 * part : 64 * part + 64]

    @pl.when(on_segment(2))
    def _():
        fetched(weights_ref, held, 27 * C2 * C3, arrived)
        weight_rows(held, wide, 16)
        for group in range(9):
            turned = jnp.transpose(wide[48 * group : 48 * group + 48, :]).astype(BF16)
            rows = slice(C2 * group, C2 * group + C2)
            for part in range(4):
                out2_ref[rows, 48 * part : 48 * part + 48] = turned[32 * part : 32 * part + 32]


def halves_of(channels, parts):
    size = channels // parts
    return spread(channels, channels, lambda e: (e % parts) * size + e // parts, lambda e: e >= 0)


def quarters(grad):
    turned = (((0,), (0,)), ((), ()))
    mixed = lax.dot_general(halves_of(C3, 4), grad, turned, preferred_element_type=F32)
    return mixed.astype(BF16)


def section3_kernel(own_ref, up_ref, down_ref, weights_ref, out_ref, wide, stacked, terms):
    @pl.when(on_segment(3))
    def _():
        for place, (ref, first) in enumerate(((up_ref, 2), (own_ref, 4), (down_ref, 2))):
            wide[:, cols(2 * place, 2)] = spread_top(ref[:, cols(first)])
        for half in range(2):
            stack_moved(
                lambda row: wide[64 * half : 64 * half + 64, cols(row)],
                stacked.at[192 * half : 192 * half + 192],
                64,
                6,
                (0, 1, 2),
            )
        terms[...] = dot(weights_ref[...], stacked[...])
        unit = spread(LANES, LANES, lambda e: 2 * e, lambda e: e < 64)
        last = is_last_block()
        for cell_z in range(-1, 3):
            for cell_y in range(4):
                total = None
                for tap_z, place_z in taps_of(cell_z, -1, 1):
                    for tap_y, place_y in taps_of(cell_y, 0, 1):
                        first = C3 * (3 * tap_z + tap_y)
                        part = terms[first : first + C3, cols(2 * (place_z + 1) + place_y)]
                        total = part if total is None else total + part
                if cell_z == -1:
                    mask = up_ref[:, cols(cell_y // 2)]
                elif cell_z == 2:
                    mask = down_ref[:, cols(cell_y // 2)]
                else:
                    mask = own_ref[:, cols(2 * cell_z + cell_y // 2)]
                result = sloped(total, half_row(mask, cell_y % 2))
                if cell_z == 2:
                    result = jnp.where(last, jnp.zeros_like(result), result)
                out_ref[:, cols(4 * (cell_z + 1) + cell_y)] = dot(result, unit).astype(BF16)


def section21_kernel(
    grad_ref,
    up_ref,
    down_ref,
    own_ref,
    weights_ref,
    next_ref,
    out0_ref,
    stacked,
    next_stacked,
    terms,
    middle,
    next_weights,
    next_terms,
):
    @pl.when(on_segment(2))
    def _():
        ordered = quarters(grad_ref[...])
        for part in range(4):
            stack_moved(
                lambda row: ordered[16 * part : 16 * part + 16, cols(row)],
                stacked.at[48 * part : 48 * part + 48],
                16,
                16,
                (0, 1, 2),
            )
        terms[...] = dot(weights_ref[...], stacked[...])
        last = is_last_block()
        for cell_z in range(-1, 5):
            for cell_y in range(8):
                total = None
                for tap_z, place_z in taps_of(cell_z, -1, 2):
                    for tap_y, place_y in taps_of(cell_y, 0, 3):
                        first = C2 * (3 * tap_z + tap_y)
                        part = terms[first : first + C2, cols(4 * (place_z + 1) + place_y)]
                        total = part if total is None else total + part
                if cell_z == -1:
                    mask = plane_of_message(up_ref, C2, cell_y)
                elif cell_z == 4:
                    mask = plane_of_message(down_ref, C2, cell_y)
                else:
                    mask = own_ref[:, cols(8 * cell_z + cell_y)]
                result = sloped(total, mask.astype(F32))
                if cell_z == 4:
                    result = jnp.where(last, jnp.zeros_like(result), result)
                middle[:, cols(8 * (cell_z + 1) + cell_y)] = result
        stack_moved(lambda row: middle[:, cols(row)], next_stacked, C2, 48, (-1, 0, 1))
        for tap in range(9):
            next_weights[C1 * tap : C1 * (tap + 1), :] = next_ref[:, cols(32 + tap)]
        next_terms[...] = dot(next_weights[:, :96], next_stacked[...])
        edge = jnp.zeros((C1, LANES), F32)
        for plane in range(4):
            sums = []
            for tap_y in range(3):
                total = None
                for tap_z in range(3):
                    first = C1 * (3 * tap_z + tap_y)
                    part = next_terms[first : first + C1, cols(8 * (plane + 2 - tap_z), 8)]
                    total = part if total is None else total + part
                sums.append(total)
            later = jnp.concatenate([sums[0][:, LANES:], edge], 1)
            earlier = jnp.concatenate([edge, sums[2][:, : 7 * LANES]], 1)
            mask = next_ref[:, cols(8 * plane, 8)].astype(F32)
            out0_ref[:, cols(8 * plane, 8)] = sloped(sums[1] + later + earlier, mask)


def weights21_kernel(
    scale2,
    scale1,
    stacked,
    next_stacked,
    down_ref,
    own_ref,
    next_ref,
    sum2_ref,
    sum1_ref,
    acts2,
    acts1,
):
    @pl.when(on_segment(2))
    def _():
        for tap_z in range(3):
            for tap_y in range(3):
                first = C2 * (3 * tap_z + tap_y)
                for place_z in range(2):
                    for place_y in range(4):
                        plane, row = 2 * place_z + tap_z, 2 * place_y + tap_y
                        if row == 8:
                            block = jnp.zeros((C2, LANES), BF16)
                        elif plane == 4:
                            block = plane_of_message(down_ref, C2, row)
                        else:
                            block = own_ref[:, cols(8 * plane + row)]
                        acts2[first : first + C2, cols(4 * place_z + place_y)] = block
        total = dot_rows(stacked[:, 512:1536], acts2[...]) * scale2
        for group in range(9):
            for tap_x in range(3):
                first = 16 * (3 * group + tap_x)
                for part in range(4):
                    row = 48 * part + 16 * tap_x
                    sum2_ref[first : first + 16, 32 * part : 32 * part + 32] = total[
                        row : row + 16, 32 * group : 32 * group + 32
                    ]
        none = jnp.zeros((C1, LANES), BF16)
        for tap_y in range(3):
            for plane in range(4):
                for row in range(8):
                    source = row + tap_y - 1
                    inside = 0 <= source < 8
                    acts1[C1 * tap_y : C1 * (tap_y + 1), cols(8 * plane + row)] = (
                        next_ref[:, cols(8 * plane + source)] if inside else none
                    )
        for tap_z in range(3):
            grads = next_stacked[:, cols(8 * (2 - tap_z), 32)]
            sum1_ref[48 * tap_z : 48 * tap_z + 48, :96] = dot_rows(acts1[...], grads) * scale1
        sum1_ref[:, 96:] = jnp.zeros((144, 32), F32)


def fine_acts(chans, up_ref, down_ref, own_ref, plane, row):
    if plane == -1:
        return plane_of_message(up_ref, chans, row)
    if plane == 4:
        return plane_of_message(down_ref, chans, row)
    return own_ref[:chans, cols(8 * plane + row)]


def weights01_kernel(
    scale, grad0_ref, sum1_ref, up_ref, down_ref, own_ref, out_ref, stacked, acts
):
    none = jnp.zeros((C1, LANES), BF16)

    @pl.when(on_segment(0))
    def _():
        for place, distance in enumerate((-1, 0, 1)):
            for plane in range(4):
                for row in range(8):
                    block = grad0_ref[:, cols(8 * plane + row)]
                    block = moved_lanes(block, distance) if distance else block
                    for tap_y in range(3):
                        first = C1 * (3 * tap_y + place)
                        target = row + tap_y - 1
                        if 0 <= target < 8:
                            acts[first : first + C1, cols(8 * plane + target)] = block
                    if row == 0:
                        acts[C1 * (6 + place) : C1 * (7 + place), cols(8 * plane)] = none
                    if row == 7:
                        acts[C1 * place : C1 * (place + 1), cols(8 * plane + 7)] = none
        for tap_z in range(3):
            for plane in range(4):
                for row in range(8):
                    stacked[C1 * tap_z : C1 * (tap_z + 1), cols(8 * plane + row)] = fine_acts(
                        C1, up_ref, down_ref, own_ref, plane + tap_z - 1, row
                    )
        out_ref[:, :48] = dot_rows(acts[...], stacked[...]) * scale
        out_ref[:, 48:] = jnp.zeros((144, 80), F32)

    @pl.when(on_segment(1))
    def _():
        out_ref[...] = sum1_ref[...]


def weights3_kernel(scale, places, blocks_ref, down_ref, out_ref, wide, stacked, acts):
    @pl.when(on_segment(3))
    def _():
        me = lax.axis_index("space")
        count = len(places)

        def held(block):
            wanted = lax.bitwise_xor(me, block)
            position = 0
            for bit, value in places_bits(places):
                position = position + value * lax.rem(lax.div(wanted, bit), 2)
            return blocks_ref[position]

        zero = jnp.zeros((64, LANES), BF16)
        for block in range(count):
            here = blocks_ref[0] if count == 1 else held(block)
            wide[:, cols(2 * block, 2)] = spread_top(here[:, cols(4)])
            rows = [half_row(here[:, cols(r // 2)], r % 2).astype(BF16) for r in range(8)]
            if count == 1:
                after = down_ref[:, : 2 * LANES]
            elif block + 1 < count:
                after = held(block + 1)[:, : 2 * LANES]
            else:
                after = None
            for r in range(4):
                rows.append(
                    zero if after is None else half_row(after[:, cols(r // 2)], r % 2).astype(BF16)
                )
            for tap_z in range(3):
                for tap_y in range(3):
                    first = C3 * (3 * tap_z + tap_y)
                    for place_y in range(2):
                        row = 2 * place_y + tap_y
                        source = zero if row == 4 else rows[4 * tap_z + row]
                        acts[first : first + C3, cols(2 * block + place_y)] = source
        stack_moved(lambda row: wide[:, cols(row)], stacked, C4, 2 * count, (0, 1, 2))
        total = dot_rows(stacked[...], acts[...]) * scale
        for group in range(9):
            for tap_x in range(3):
                first = 64 * (3 * group + tap_x)
                for part in range(2):
                    row = C4 * tap_x + 64 * part
                    out_ref[first : first + 64, 64 * part : 64 * part + 64] = total[
                        row : row + 64, C3 * group : C3 * group + C3
                    ]


def places_bits(places):
    count = len(places)
    bits = []
    bit = 1
    while bit < count:
        bits.append((bit, places.index(bit)))
        bit *= 2
    return bits


def call(kernel, outs, scratch, *args, flops, far=()):
    shapes = [jax.ShapeDtypeStruct(*entry) for entry in outs]
    moved = sum(a.size * a.dtype.itemsize for a in [*args, *shapes])
    near_spec = pl.BlockSpec(memory_space=pltpu.VMEM)
    far_spec = pl.BlockSpec(memory_space=pltpu.HBM)
    return pl.pallas_call(
        kernel,
        out_shape=shapes,
        in_specs=[far_spec if place in far else near_spec for place in range(len(args))],
        scratch_shapes=[
            pltpu.VMEM(*entry) if isinstance(entry, tuple) else entry for entry in scratch
        ],
        compiler_params=pltpu.CompilerParams(vmem_limit_bytes=VMEM_LIMIT),
        cost_estimate=pl.CostEstimate(flops=flops, bytes_accessed=moved, transcendentals=0),
    )(*args)


def pairs_of(segments, route):
    total = lax.axis_size("segment")
    count = lax.axis_size("space")
    return [
        (a * total + s, b * total + s) for a, b in route(count) for s in segments
    ]


def over_space(block, segments, route):
    return lax.ppermute(block, ("space", "segment"), pairs_of(segments, route))


def filled(ordered):
    rows = ordered.reshape(-1, LANES) if ordered.size % LANES == 0 else None
    if rows is None:
        flat = ordered.reshape(-1)
        rows = jnp.pad(flat, (0, -flat.shape[0] % LANES)).reshape(-1, LANES)
    return rows


def shards(saved_inputs, conv_weights, top_gradient):
    segment = lax.axis_index("segment")
    count = lax.axis_size("space")
    room = conv_weights.shape[1]
    scales = [1.0 / math.sqrt(count * cells) for cells in (4096, 4096, 512, 64)]

    def later(n):
        return [(i, i + 1) for i in range(n - 1)]

    def sooner(n):
        return [(i + 1, i) for i in range(n - 1)]

    def behind(values, *leaders):
        return lax.optimization_barrier((*values, *leaders))[: len(values)]

    saved_inputs = pltpu.with_memory_space_constraint(saved_inputs, pltpu.HBM)
    conv_weights = pltpu.with_memory_space_constraint(conv_weights, pltpu.HBM)
    top = jnp.transpose(top_gradient[:, 0], (1, 2, 0)).reshape(64, C4)
    top = pltpu.with_memory_space_constraint(top, pltpu.HBM)
    deep, up, down, own2, own01 = call(
        layout_kernel,
        [
            ((64, 640), BF16),
            ((64, 512), BF16),
            ((64, 512), BF16),
            ((32, 4096), BF16),
            ((16, 5248), BF16),
        ],
        [
            ((1, 131072), BF16),
            ((1, 13824), BF16),
            ((64, 4096), F32),
            ((128, 128), F32),
            ((144, 128), F32),
            ((64, 128), BF16),
            pltpu.SemaphoreType.DMA,
            pltpu.SemaphoreType.DMA,
        ],
        saved_inputs,
        conv_weights,
        top,
        flops=0,
        far=(0, 1, 2),
    )
    up = over_space(up, range(4), later)
    down = over_space(down, range(4), sooner)
    next_own = lax.ppermute(own01, "segment", [(1, 2)])
    (weights,) = behind((conv_weights,), deep)
    taps3, taps2 = call(
        weights_layout_kernel,
        [((576, 384), BF16), ((288, 192), BF16)],
        [((1, 221184), BF16), ((1728, 128), F32), pltpu.SemaphoreType.DMA],
        weights,
        flops=0,
        far=(0,),
    )
    taps3, taps2 = behind((taps3, taps2), next_own)

    (grad2,) = call(
        section3_kernel,
        [((64, 2048), BF16)],
        [((128, 768), BF16), ((384, 768), BF16), ((576, 768), F32)],
        deep,
        up,
        down,
        taps3,
        flops=2 * 576 * 384 * 768,
    )
    places = [0]
    even = not count & (count - 1)
    gathers = even and count <= GATHER_LIMIT
    bits = [1 << power for power in range(count.bit_length() - 1)] if even else []


    def swap(block, segments, bit):
        return over_space(block, segments, lambda n: [(i, i ^ bit) for i in range(n)])

    def gathered(blocks, bit):
        return jnp.concatenate([blocks, swap(blocks, [3], bit)], 0)

    (blocks,) = behind((deep[None],), grad2)
    if gathers:
        for bit in bits[:0:-1][:1]:
            blocks = gathered(blocks, bit)
            places = places + [place ^ bit for place in places]
    grad2 = lax.ppermute(grad2, "segment", [(3, 2)])
    (grad2,) = behind((grad2,), blocks)
    grad0, stacked2, stacked1 = call(
        section21_kernel,
        [((16, 4096), BF16), ((192, 2048), BF16), ((96, 6144), BF16)],
        [
            ((288, 2048), F32),
            ((32, 6144), BF16),
            ((144, 128), BF16),
            ((144, 6144), F32),
        ],
        grad2,
        up,
        down,
        own2,
        taps2,
        next_own,
        flops=2 * 288 * 192 * 2048,
    )
    sum2, sum1 = call(
        functools.partial(weights21_kernel, scales[2], scales[1]),
        [((432, 128), F32), ((144, 128), F32)],
        [((288, 1024), BF16), ((48, 4096), BF16)],
        stacked2,
        stacked1,
        down,
        own2,
        next_own,
        flops=LONG,
    )
    (blocks,) = behind((blocks,), grad0)
    grad0 = lax.ppermute(grad0, "segment", [(2, 0)])
    sum1 = lax.ppermute(sum1, "segment", [(2, 1)])
    if gathers:
        for bit in bits[:0:-1][1:]:
            blocks = gathered(blocks, bit)
            places = places + [place ^ bit for place in places]
    grad0, sum1 = behind((grad0, sum1), blocks)
    (sum01,) = call(
        functools.partial(weights01_kernel, scales[0]),
        [((144, 128), F32)],
        [((48, 4096), BF16), ((144, 4096), BF16)],
        grad0,
        sum1,
        up,
        down,
        own01,
        flops=2 * 144 * 96 * 6144,
    )
    for bit in bits:
        sum2 = sum2 + swap(sum2, [2], bit)
    if not even:
        sum2 = lax.psum(sum2, "space")
        sum01 = lax.psum(sum01, "space")
    if gathers:
        blocks = gathered(blocks, bits[0])
        places = places + [place ^ bits[0] for place in places]
    for bit in bits:
        sum01 = sum01 + swap(sum01, [0, 1], bit)
    held = len(places)
    (sum3,) = call(
        functools.partial(weights3_kernel, scales[3], places),
        [((1728, 128), F32)],
        [((128, 256 * held), BF16), ((384, 256 * held), BF16), ((576, 256 * held), BF16)],
        blocks,
        down,
        flops=LONG,
    )
    if held < count:
        sum3 = lax.psum(sum3, "space")

    def finish0(sum01, sum2, sum3):
        parts = sum01[:, :48].reshape(3, 3, C1, 3, 16)[..., :C0]
        return filled(jnp.transpose(parts, (3, 0, 1, 2, 4)))

    def finish1(sum01, sum2, sum3):
        parts = sum01[:, :96].reshape(9, C1, 3, C2)
        return filled(jnp.transpose(parts, (0, 2, 3, 1)))

    def whole(finish):
        def branch(*sums):
            rows = finish(*sums)
            return jnp.pad(rows, ((0, room // LANES - rows.shape[0]), (0, 0)))

        return branch

    ends = [finish0, finish1, lambda a, b, c: b, lambda a, b, c: c]
    rows = lax.switch(segment, [whole(end) for end in ends], sum01, sum2, sum3)
    return rows.reshape(1, room)


def solution(mesh):
    return jax.shard_map(
        shards,
        mesh=mesh,
        in_specs=(P("segment", "space"), P("segment", None), P(None, "space", None, None)),
        out_specs=P("segment", None),
        check_vma=False,
    )
```

```python
import functools
import math

import jax
import jax.numpy as jnp
from jax import lax
from jax.experimental import pallas as pl
from jax.experimental.pallas import tpu as pltpu
from jax.sharding import PartitionSpec as P

C0, C1, C2, C3, C4 = 4, 16, 32, 64, 128
LANES = 128
SLOPE = 0.3
BF16 = jnp.bfloat16
F32 = jnp.float32
GATHER_LIMIT = 8
VMEM_LIMIT = 48 * 1024 * 1024
LONG = 20_000_000_000


def on_segment(index):
    return lax.axis_index("segment") == index


def is_last_block():
    return lax.axis_index("space") == lax.axis_size("space") - 1


def cols(row, count=1):
    return slice(LANES * row, LANES * (row + count))


def moved_lanes(block, distance):
    lane = lax.broadcasted_iota(jnp.int32, block.shape, 1)
    rolled = pltpu.roll(block.astype(F32), distance % LANES, 1)
    kept = lane >= distance if distance > 0 else lane < LANES + distance
    return jnp.where(kept, rolled, 0.0).astype(BF16)


def stack_moved(read, target, chans, rows, distances):
    for row in range(rows):
        block = read(row)
        for place, distance in enumerate(distances):
            moved = moved_lanes(block, distance) if distance else block
            target[place * chans : (place + 1) * chans, cols(row)] = moved


def spread(rows_in, rows_out, source, bound):
    entry = lax.broadcasted_iota(jnp.int32, (rows_in, rows_out), 0)
    place = lax.broadcasted_iota(jnp.int32, (rows_in, rows_out), 1)
    return jnp.where((place == source(entry)) & bound(entry), 1.0, 0.0).astype(BF16)


def taps_of(cell, low, high):
    if cell % 2:
        pairs = [(1, (cell - 1) // 2)]
    else:
        pairs = [(0, cell // 2), (2, cell // 2 - 1)]
    return [(tap, place) for tap, place in pairs if low <= place <= high]


def dot_rows(left, right):
    return lax.dot_general(left, right, (((1,), (1,)), ((), ())), preferred_element_type=F32)


def dot(left, right):
    return jnp.dot(left, right, preferred_element_type=F32)


def sloped(total, activation):
    return (total * jnp.where(activation > 0, 1.0, SLOPE)).astype(BF16)


def half_row(block, odd):
    lane = lax.broadcasted_iota(jnp.int32, block.shape, 1)
    wide = block.astype(F32)
    if odd:
        wide = pltpu.roll(wide, LANES // 2, 1)
    return jnp.where(lane < LANES // 2, wide, 0.0)


def plane_of_message(ref, chans, row):
    return ref[32 * (row // 4) : 32 * (row // 4) + chans, cols(row % 4)]


def spread_top(block):
    block = dot(block, halves_of(C4, 2)).astype(BF16)
    unit = spread(64, 2 * LANES, lambda e: LANES * (e // 32) + 2 * (e % 32), lambda e: e >= 0)
    turned = (((0,), (0,)), ((), ()))
    return lax.dot_general(block, unit, turned, preferred_element_type=F32).astype(BF16)


def copy_rows(saved_ref, wide, chans, width):
    for chan in range(chans):
        source = saved_ref[:, chan * width : (chan + 1) * width]
        wide[chan : chan + 1, :width] = source.astype(F32)


def fetched(far_ref, near_ref, size, arrived):
    part = pl.ds(0, size)
    copy = pltpu.make_async_copy(far_ref.at[:, part], near_ref.at[:, part], arrived)
    copy.start()
    copy.wait()


def weight_rows(held, wide, rows):
    for tap in range(27):
        first = LANES * rows * tap
        wide[rows * tap : rows * tap + rows, :] = (
            held[:, first : first + LANES * rows].astype(F32).reshape(rows, LANES)
        )


def layout_kernel(
    saved_ref,
    weights_ref,
    top_ref,
    deep_ref,
    up_ref,
    down_ref,
    own2_ref,
    own01_ref,
    held,
    held_weights,
    wide,
    wide_weights,
    mixed,
    held_top,
    arrived,
    arrived_top,
):
    def fetch(size):
        fetched(saved_ref, held, size, arrived)

    def send(place, plane, target_ref):
        for half in range(2):
            target_ref[32 * half : 32 * half + place, :] = wide[
                :place, cols(8 * plane + 4 * half, 4)
            ].astype(BF16)

    @pl.when(on_segment(3))
    def _():
        copy = pltpu.make_async_copy(top_ref, held_top, arrived_top)
        copy.start()
        fetch(C3 * 512)
        copy_rows(held, wide, C3, 512)
        block = wide[:, :512].astype(BF16)
        copy.wait()
        top = held_top[...]
        deep_ref[:, :512] = block
        deep_ref[:, 512:] = top
        for ref, half in ((up_ref, block[:, 256:]), (down_ref, block[:, :256])):
            ref[:, :256] = half
            ref[:, 256:384] = top
            ref[:, 384:] = jnp.zeros((64, LANES), BF16)

    for section, chans in enumerate((C0, C1, C2)):

        @pl.when(on_segment(section))
        def _(section=section, chans=chans):
            if section == 0:
                wide[:C1, :] = jnp.zeros((C1, 4096), F32)
            fetch(chans * 4096)
            copy_rows(held, wide, chans, 4096)
            place = max(chans, C1)
            own_ref = own2_ref if section == 2 else own01_ref
            own_ref[:, :4096] = wide[:place, :].astype(BF16)
            if section == 1:
                fetched(weights_ref, held_weights, 27 * C1 * C2, arrived)
                weight_rows(held_weights, wide_weights, 4)
                turned = jnp.transpose(wide_weights[...])
                mixed[...] = jnp.zeros((144, LANES), F32)
                for group in range(9):
                    for part in range(8):
                        mixed[16 * group : 16 * group + 16, 12 * part : 12 * part + 12] = turned[
                            16 * part : 16 * part + 16, 12 * group : 12 * group + 12
                        ]
                ordered = spread(
                    LANES,
                    LANES,
                    lambda e: 32 * ((e % 12) // 4) + 8 * (e % 4) + e // 12,
                    lambda e: e < 96,
                )
                taps = dot(mixed[...].astype(BF16), ordered).astype(BF16)
                for group in range(9):
                    own01_ref[:, cols(32 + group)] = taps[16 * group : 16 * group + 16, :]
            send(place, 3, up_ref)
            send(place, 0, down_ref)


def weights_layout_kernel(weights_ref, out3_ref, out2_ref, held, wide, arrived):
    @pl.when(on_segment(3))
    def _():
        fetched(weights_ref, held, 27 * C3 * C4, arrived)
        weight_rows(held, wide, 64)
        for group in range(9):
            turned = jnp.transpose(wide[192 * group : 192 * group + 192, :]).astype(BF16)
            rows = slice(C3 * group, C3 * group + C3)
            for part in range(2):
                out3_ref[rows, 192 * part : 192 * part + 192] = turned[64 * part : 64 * part + 64]

    @pl.when(on_segment(2))
    def _():
        fetched(weights_ref, held, 27 * C2 * C3, arrived)
        weight_rows(held, wide, 16)
        for group in range(9):
            turned = jnp.transpose(wide[48 * group : 48 * group + 48, :]).astype(BF16)
            rows = slice(C2 * group, C2 * group + C2)
            for part in range(4):
                out2_ref[rows, 48 * part : 48 * part + 48] = turned[32 * part : 32 * part + 32]


def halves_of(channels, parts):
    size = channels // parts
    return spread(channels, channels, lambda e: (e % parts) * size + e // parts, lambda e: e >= 0)


def quarters(grad):
    turned = (((0,), (0,)), ((), ()))
    mixed = lax.dot_general(halves_of(C3, 4), grad, turned, preferred_element_type=F32)
    return mixed.astype(BF16)


def section3_kernel(own_ref, up_ref, down_ref, weights_ref, out_ref, wide, stacked, terms):
    @pl.when(on_segment(3))
    def _():
        for place, (ref, first) in enumerate(((up_ref, 2), (own_ref, 4), (down_ref, 2))):
            wide[:, cols(2 * place, 2)] = spread_top(ref[:, cols(first)])
        for half in range(2):
            stack_moved(
                lambda row: wide[64 * half : 64 * half + 64, cols(row)],
                stacked.at[192 * half : 192 * half + 192],
                64,
                6,
                (0, 1, 2),
            )
        terms[...] = dot(weights_ref[...], stacked[...])
        unit = spread(LANES, LANES, lambda e: 2 * e, lambda e: e < 64)
        last = is_last_block()
        for cell_z in range(-1, 3):
            for cell_y in range(4):
                total = None
                for tap_z, place_z in taps_of(cell_z, -1, 1):
                    for tap_y, place_y in taps_of(cell_y, 0, 1):
                        first = C3 * (3 * tap_z + tap_y)
                        part = terms[first : first + C3, cols(2 * (place_z + 1) + place_y)]
                        total = part if total is None else total + part
                if cell_z == -1:
                    mask = up_ref[:, cols(cell_y // 2)]
                elif cell_z == 2:
                    mask = down_ref[:, cols(cell_y // 2)]
                else:
                    mask = own_ref[:, cols(2 * cell_z + cell_y // 2)]
                result = sloped(total, half_row(mask, cell_y % 2))
                if cell_z == 2:
                    result = jnp.where(last, jnp.zeros_like(result), result)
                out_ref[:, cols(4 * (cell_z + 1) + cell_y)] = dot(result, unit).astype(BF16)


def section21_kernel(
    grad_ref,
    up_ref,
    down_ref,
    own_ref,
    weights_ref,
    next_ref,
    out0_ref,
    stacked,
    next_stacked,
    terms,
    middle,
    next_weights,
    next_terms,
):
    @pl.when(on_segment(2))
    def _():
        ordered = quarters(grad_ref[...])
        for part in range(4):
            stack_moved(
                lambda row: ordered[16 * part : 16 * part + 16, cols(row)],
                stacked.at[48 * part : 48 * part + 48],
                16,
                16,
                (0, 1, 2),
            )
        terms[...] = dot(weights_ref[...], stacked[...])
        last = is_last_block()
        for cell_z in range(-1, 5):
            for cell_y in range(8):
                total = None
                for tap_z, place_z in taps_of(cell_z, -1, 2):
                    for tap_y, place_y in taps_of(cell_y, 0, 3):
                        first = C2 * (3 * tap_z + tap_y)
                        part = terms[first : first + C2, cols(4 * (place_z + 1) + place_y)]
                        total = part if total is None else total + part
                if cell_z == -1:
                    mask = plane_of_message(up_ref, C2, cell_y)
                elif cell_z == 4:
                    mask = plane_of_message(down_ref, C2, cell_y)
                else:
                    mask = own_ref[:, cols(8 * cell_z + cell_y)]
                result = sloped(total, mask.astype(F32))
                if cell_z == 4:
                    result = jnp.where(last, jnp.zeros_like(result), result)
                middle[:, cols(8 * (cell_z + 1) + cell_y)] = result
        stack_moved(lambda row: middle[:, cols(row)], next_stacked, C2, 48, (-1, 0, 1))
        for tap in range(9):
            next_weights[C1 * tap : C1 * (tap + 1), :] = next_ref[:, cols(32 + tap)]
        next_terms[...] = dot(next_weights[:, :96], next_stacked[...])
        edge = jnp.zeros((C1, LANES), F32)
        for plane in range(4):
            sums = []
            for tap_y in range(3):
                total = None
                for tap_z in range(3):
                    first = C1 * (3 * tap_z + tap_y)
                    part = next_terms[first : first + C1, cols(8 * (plane + 2 - tap_z), 8)]
                    total = part if total is None else total + part
                sums.append(total)
            later = jnp.concatenate([sums[0][:, LANES:], edge], 1)
            earlier = jnp.concatenate([edge, sums[2][:, : 7 * LANES]], 1)
            mask = next_ref[:, cols(8 * plane, 8)].astype(F32)
            out0_ref[:, cols(8 * plane, 8)] = sloped(sums[1] + later + earlier, mask)


def weights21_kernel(
    scale2,
    scale1,
    stacked,
    next_stacked,
    down_ref,
    own_ref,
    next_ref,
    sum2_ref,
    sum1_ref,
    acts2,
    acts1,
):
    @pl.when(on_segment(2))
    def _():
        for tap_z in range(3):
            for tap_y in range(3):
                first = C2 * (3 * tap_z + tap_y)
                for place_z in range(2):
                    for place_y in range(4):
                        plane, row = 2 * place_z + tap_z, 2 * place_y + tap_y
                        if row == 8:
                            block = jnp.zeros((C2, LANES), BF16)
                        elif plane == 4:
                            block = plane_of_message(down_ref, C2, row)
                        else:
                            block = own_ref[:, cols(8 * plane + row)]
                        acts2[first : first + C2, cols(4 * place_z + place_y)] = block
        total = dot_rows(stacked[:, 512:1536], acts2[...]) * scale2
        for group in range(9):
            for tap_x in range(3):
                first = 16 * (3 * group + tap_x)
                for part in range(4):
                    row = 48 * part + 16 * tap_x
                    sum2_ref[first : first + 16, 32 * part : 32 * part + 32] = total[
                        row : row + 16, 32 * group : 32 * group + 32
                    ]
        none = jnp.zeros((C1, LANES), BF16)
        for tap_y in range(3):
            for plane in range(4):
                for row in range(8):
                    source = row + tap_y - 1
                    inside = 0 <= source < 8
                    acts1[C1 * tap_y : C1 * (tap_y + 1), cols(8 * plane + row)] = (
                        next_ref[:, cols(8 * plane + source)] if inside else none
                    )
        for tap_z in range(3):
            grads = next_stacked[:, cols(8 * (2 - tap_z), 32)]
            sum1_ref[48 * tap_z : 48 * tap_z + 48, :96] = dot_rows(acts1[...], grads) * scale1
        sum1_ref[:, 96:] = jnp.zeros((144, 32), F32)


def fine_acts(chans, up_ref, down_ref, own_ref, plane, row):
    if plane == -1:
        return plane_of_message(up_ref, chans, row)
    if plane == 4:
        return plane_of_message(down_ref, chans, row)
    return own_ref[:chans, cols(8 * plane + row)]


def weights01_kernel(
    scale, grad0_ref, sum1_ref, up_ref, down_ref, own_ref, out_ref, stacked, acts
):
    none = jnp.zeros((C1, LANES), BF16)

    @pl.when(on_segment(0))
    def _():
        for place, distance in enumerate((-1, 0, 1)):
            for plane in range(4):
                for row in range(8):
                    block = grad0_ref[:, cols(8 * plane + row)]
                    block = moved_lanes(block, distance) if distance else block
                    for tap_y in range(3):
                        first = C1 * (3 * tap_y + place)
                        target = row + tap_y - 1
                        if 0 <= target < 8:
                            acts[first : first + C1, cols(8 * plane + target)] = block
                    if row == 0:
                        acts[C1 * (6 + place) : C1 * (7 + place), cols(8 * plane)] = none
                    if row == 7:
                        acts[C1 * place : C1 * (place + 1), cols(8 * plane + 7)] = none
        for tap_z in range(3):
            for plane in range(4):
                for row in range(8):
                    stacked[C1 * tap_z : C1 * (tap_z + 1), cols(8 * plane + row)] = fine_acts(
                        C1, up_ref, down_ref, own_ref, plane + tap_z - 1, row
                    )
        out_ref[:, :48] = dot_rows(acts[...], stacked[...]) * scale
        out_ref[:, 48:] = jnp.zeros((144, 80), F32)

    @pl.when(on_segment(1))
    def _():
        out_ref[...] = sum1_ref[...]


def weights3_kernel(scale, places, blocks_ref, down_ref, out_ref, wide, stacked, acts):
    @pl.when(on_segment(3))
    def _():
        me = lax.axis_index("space")
        count = len(places)

        def held(block):
            wanted = lax.bitwise_xor(me, block)
            position = 0
            for bit, value in places_bits(places):
                position = position + value * lax.rem(lax.div(wanted, bit), 2)
            return blocks_ref[position]

        zero = jnp.zeros((64, LANES), BF16)
        for block in range(count):
            here = blocks_ref[0] if count == 1 else held(block)
            wide[:, cols(2 * block, 2)] = spread_top(here[:, cols(4)])
            rows = [half_row(here[:, cols(r // 2)], r % 2).astype(BF16) for r in range(8)]
            if count == 1:
                after = down_ref[:, : 2 * LANES]
            elif block + 1 < count:
                after = held(block + 1)[:, : 2 * LANES]
            else:
                after = None
            for r in range(4):
                rows.append(
                    zero if after is None else half_row(after[:, cols(r // 2)], r % 2).astype(BF16)
                )
            for tap_z in range(3):
                for tap_y in range(3):
                    first = C3 * (3 * tap_z + tap_y)
                    for place_y in range(2):
                        row = 2 * place_y + tap_y
                        source = zero if row == 4 else rows[4 * tap_z + row]
                        acts[first : first + C3, cols(2 * block + place_y)] = source
        stack_moved(lambda row: wide[:, cols(row)], stacked, C4, 2 * count, (0, 1, 2))
        total = dot_rows(stacked[...], acts[...]) * scale
        for group in range(9):
            for tap_x in range(3):
                first = 64 * (3 * group + tap_x)
                for part in range(2):
                    row = C4 * tap_x + 64 * part
                    out_ref[first : first + 64, 64 * part : 64 * part + 64] = total[
                        row : row + 64, C3 * group : C3 * group + C3
                    ]


def places_bits(places):
    count = len(places)
    bits = []
    bit = 1
    while bit < count:
        bits.append((bit, places.index(bit)))
        bit *= 2
    return bits


def call(kernel, outs, scratch, *args, flops, far=()):
    shapes = [jax.ShapeDtypeStruct(*entry) for entry in outs]
    moved = sum(a.size * a.dtype.itemsize for a in [*args, *shapes])
    near_spec = pl.BlockSpec(memory_space=pltpu.VMEM)
    far_spec = pl.BlockSpec(memory_space=pltpu.HBM)
    return pl.pallas_call(
        kernel,
        out_shape=shapes,
        in_specs=[far_spec if place in far else near_spec for place in range(len(args))],
        scratch_shapes=[
            pltpu.VMEM(*entry) if isinstance(entry, tuple) else entry for entry in scratch
        ],
        compiler_params=pltpu.CompilerParams(vmem_limit_bytes=VMEM_LIMIT),
        cost_estimate=pl.CostEstimate(flops=flops, bytes_accessed=moved, transcendentals=0),
    )(*args)


def pairs_of(segments, route):
    total = lax.axis_size("segment")
    count = lax.axis_size("space")
    return [
        (a * total + s, b * total + s) for a, b in route(count) for s in segments
    ]


def over_space(block, segments, route):
    return lax.ppermute(block, ("space", "segment"), pairs_of(segments, route))


def filled(ordered):
    rows = ordered.reshape(-1, LANES) if ordered.size % LANES == 0 else None
    if rows is None:
        flat = ordered.reshape(-1)
        rows = jnp.pad(flat, (0, -flat.shape[0] % LANES)).reshape(-1, LANES)
    return rows


def shards(saved_inputs, conv_weights, top_gradient):
    segment = lax.axis_index("segment")
    count = lax.axis_size("space")
    room = conv_weights.shape[1]
    scales = [1.0 / math.sqrt(count * cells) for cells in (4096, 4096, 512, 64)]

    def later(n):
        return [(i, i + 1) for i in range(n - 1)]

    def sooner(n):
        return [(i + 1, i) for i in range(n - 1)]

    def behind(values, *leaders):
        return lax.optimization_barrier((*values, *leaders))[: len(values)]

    saved_inputs = pltpu.with_memory_space_constraint(saved_inputs, pltpu.HBM)
    conv_weights = pltpu.with_memory_space_constraint(conv_weights, pltpu.HBM)
    top = jnp.transpose(top_gradient[:, 0], (1, 2, 0)).reshape(64, C4)
    top = pltpu.with_memory_space_constraint(top, pltpu.HBM)
    deep, up, down, own2, own01 = call(
        layout_kernel,
        [
            ((64, 640), BF16),
            ((64, 512), BF16),
            ((64, 512), BF16),
            ((32, 4096), BF16),
            ((16, 5248), BF16),
        ],
        [
            ((1, 131072), BF16),
            ((1, 13824), BF16),
            ((64, 4096), F32),
            ((128, 128), F32),
            ((144, 128), F32),
            ((64, 128), BF16),
            pltpu.SemaphoreType.DMA,
            pltpu.SemaphoreType.DMA,
        ],
        saved_inputs,
        conv_weights,
        top,
        flops=0,
        far=(0, 1, 2),
    )
    up = over_space(up, range(4), later)
    down = over_space(down, range(4), sooner)
    next_own = lax.ppermute(own01, "segment", [(1, 2)])
    (weights,) = behind((conv_weights,), deep)
    taps3, taps2 = call(
        weights_layout_kernel,
        [((576, 384), BF16), ((288, 192), BF16)],
        [((1, 221184), BF16), ((1728, 128), F32), pltpu.SemaphoreType.DMA],
        weights,
        flops=0,
        far=(0,),
    )
    taps3, taps2 = behind((taps3, taps2), next_own)

    (grad2,) = call(
        section3_kernel,
        [((64, 2048), BF16)],
        [((128, 768), BF16), ((384, 768), BF16), ((576, 768), F32)],
        deep,
        up,
        down,
        taps3,
        flops=2 * 576 * 384 * 768,
    )
    places = [0]
    even = not count & (count - 1)
    gathers = even and count <= GATHER_LIMIT
    bits = [1 << power for power in range(count.bit_length() - 1)] if even else []


    def swap(block, segments, bit):
        return over_space(block, segments, lambda n: [(i, i ^ bit) for i in range(n)])

    def gathered(blocks, bit):
        return jnp.concatenate([blocks, swap(blocks, [3], bit)], 0)

    (blocks,) = behind((deep[None],), grad2)
    if gathers:
        for bit in bits[:0:-1][:1]:
            blocks = gathered(blocks, bit)
            places = places + [place ^ bit for place in places]
    grad2 = lax.ppermute(grad2, "segment", [(3, 2)])
    (grad2,) = behind((grad2,), blocks)
    grad0, stacked2, stacked1 = call(
        section21_kernel,
        [((16, 4096), BF16), ((192, 2048), BF16), ((96, 6144), BF16)],
        [
            ((288, 2048), F32),
            ((32, 6144), BF16),
            ((144, 128), BF16),
            ((144, 6144), F32),
        ],
        grad2,
        up,
        down,
        own2,
        taps2,
        next_own,
        flops=2 * 288 * 192 * 2048,
    )
    sum2, sum1 = call(
        functools.partial(weights21_kernel, scales[2], scales[1]),
        [((432, 128), F32), ((144, 128), F32)],
        [((288, 1024), BF16), ((48, 4096), BF16)],
        stacked2,
        stacked1,
        down,
        own2,
        next_own,
        flops=LONG,
    )
    (blocks,) = behind((blocks,), grad0)
    grad0 = lax.ppermute(grad0, "segment", [(2, 0)])
    sum1 = lax.ppermute(sum1, "segment", [(2, 1)])
    if gathers:
        for bit in bits[:0:-1][1:]:
            blocks = gathered(blocks, bit)
            places = places + [place ^ bit for place in places]
    grad0, sum1 = behind((grad0, sum1), sum2)
    (sum01,) = call(
        functools.partial(weights01_kernel, scales[0]),
        [((144, 128), F32)],
        [((48, 4096), BF16), ((144, 4096), BF16)],
        grad0,
        sum1,
        up,
        down,
        own01,
        flops=2 * 144 * 96 * 6144,
    )
    for bit in bits:
        sum2 = sum2 + swap(sum2, [2], bit)
    if not even:
        sum2 = lax.psum(sum2, "space")
        sum01 = lax.psum(sum01, "space")
    if gathers:
        blocks = gathered(blocks, bits[0])
        places = places + [place ^ bits[0] for place in places]
    for bit in bits:
        sum01 = sum01 + swap(sum01, [0, 1], bit)
    held = len(places)
    (sum3,) = call(
        functools.partial(weights3_kernel, scales[3], places),
        [((1728, 128), F32)],
        [((128, 256 * held), BF16), ((384, 256 * held), BF16), ((576, 256 * held), BF16)],
        blocks,
        down,
        flops=LONG,
    )
    if held < count:
        sum3 = lax.psum(sum3, "space")

    def finish0(sum01, sum2, sum3):
        parts = sum01[:, :48].reshape(3, 3, C1, 3, 16)[..., :C0]
        return filled(jnp.transpose(parts, (3, 0, 1, 2, 4)))

    def finish1(sum01, sum2, sum3):
        parts = sum01[:, :96].reshape(9, C1, 3, C2)
        return filled(jnp.transpose(parts, (0, 2, 3, 1)))

    def whole(finish):
        def branch(*sums):
            rows = finish(*sums)
            return jnp.pad(rows, ((0, room // LANES - rows.shape[0]), (0, 0)))

        return branch

    ends = [finish0, finish1, lambda a, b, c: b, lambda a, b, c: c]
    rows = lax.switch(segment, [whole(end) for end in ends], sum01, sum2, sum3)
    return rows.reshape(1, room)


def solution(mesh):
    return jax.shard_map(
        shards,
        mesh=mesh,
        in_specs=(P("segment", "space"), P("segment", None), P(None, "space", None, None)),
        out_specs=P("segment", None),
        check_vma=False,
    )
```

```python
import functools
import math

import jax
import jax.numpy as jnp
from jax import lax
from jax.experimental import pallas as pl
from jax.experimental.pallas import tpu as pltpu
from jax.sharding import PartitionSpec as P

C0, C1, C2, C3, C4 = 4, 16, 32, 64, 128
LANES = 128
SLOPE = 0.3
BF16 = jnp.bfloat16
F32 = jnp.float32
GATHER_LIMIT = 8
VMEM_LIMIT = 48 * 1024 * 1024
LONG = 20_000_000_000


def on_segment(index):
    return lax.axis_index("segment") == index


def is_last_block():
    return lax.axis_index("space") == lax.axis_size("space") - 1


def cols(row, count=1):
    return slice(LANES * row, LANES * (row + count))


def moved_lanes(block, distance):
    lane = lax.broadcasted_iota(jnp.int32, block.shape, 1)
    rolled = pltpu.roll(block.astype(F32), distance % LANES, 1)
    kept = lane >= distance if distance > 0 else lane < LANES + distance
    return jnp.where(kept, rolled, 0.0).astype(BF16)


def stack_moved(read, target, chans, rows, distances):
    for row in range(rows):
        block = read(row)
        for place, distance in enumerate(distances):
            moved = moved_lanes(block, distance) if distance else block
            target[place * chans : (place + 1) * chans, cols(row)] = moved


def spread(rows_in, rows_out, source, bound):
    entry = lax.broadcasted_iota(jnp.int32, (rows_in, rows_out), 0)
    place = lax.broadcasted_iota(jnp.int32, (rows_in, rows_out), 1)
    return jnp.where((place == source(entry)) & bound(entry), 1.0, 0.0).astype(BF16)


def taps_of(cell, low, high):
    if cell % 2:
        pairs = [(1, (cell - 1) // 2)]
    else:
        pairs = [(0, cell // 2), (2, cell // 2 - 1)]
    return [(tap, place) for tap, place in pairs if low <= place <= high]


def dot_rows(left, right):
    return lax.dot_general(left, right, (((1,), (1,)), ((), ())), preferred_element_type=F32)


def dot(left, right):
    return jnp.dot(left, right, preferred_element_type=F32)


def sloped(total, activation):
    return (total * jnp.where(activation > 0, 1.0, SLOPE)).astype(BF16)


def half_row(block, odd):
    lane = lax.broadcasted_iota(jnp.int32, block.shape, 1)
    wide = block.astype(F32)
    if odd:
        wide = pltpu.roll(wide, LANES // 2, 1)
    return jnp.where(lane < LANES // 2, wide, 0.0)


def plane_of_message(ref, chans, row):
    return ref[32 * (row // 4) : 32 * (row // 4) + chans, cols(row % 4)]


def spread_top(block):
    block = dot(block, halves_of(C4, 2)).astype(BF16)
    unit = spread(64, 2 * LANES, lambda e: LANES * (e // 32) + 2 * (e % 32), lambda e: e >= 0)
    turned = (((0,), (0,)), ((), ()))
    return lax.dot_general(block, unit, turned, preferred_element_type=F32).astype(BF16)


def copy_rows(saved_ref, wide, chans, width):
    for chan in range(chans):
        source = saved_ref[:, chan * width : (chan + 1) * width]
        wide[chan : chan + 1, :width] = source.astype(F32)


def fetched(far_ref, near_ref, size, arrived):
    part = pl.ds(0, size)
    copy = pltpu.make_async_copy(far_ref.at[:, part], near_ref.at[:, part], arrived)
    copy.start()
    copy.wait()


def weight_rows(held, wide, rows):
    for tap in range(27):
        first = LANES * rows * tap
        wide[rows * tap : rows * tap + rows, :] = (
            held[:, first : first + LANES * rows].astype(F32).reshape(rows, LANES)
        )


def layout_kernel(
    saved_ref,
    weights_ref,
    top_ref,
    deep_ref,
    up_ref,
    down_ref,
    own2_ref,
    own01_ref,
    held,
    held_weights,
    wide,
    wide_weights,
    mixed,
    held_top,
    arrived,
    arrived_top,
):
    def fetch(size):
        fetched(saved_ref, held, size, arrived)

    def send(place, plane, target_ref):
        for half in range(2):
            target_ref[32 * half : 32 * half + place, :] = wide[
                :place, cols(8 * plane + 4 * half, 4)
            ].astype(BF16)

    @pl.when(on_segment(3))
    def _():
        copy = pltpu.make_async_copy(top_ref, held_top, arrived_top)
        copy.start()
        fetch(C3 * 512)
        copy_rows(held, wide, C3, 512)
        block = wide[:, :512].astype(BF16)
        copy.wait()
        top = held_top[...]
        deep_ref[:, :512] = block
        deep_ref[:, 512:] = top
        for ref, half in ((up_ref, block[:, 256:]), (down_ref, block[:, :256])):
            ref[:, :256] = half
            ref[:, 256:384] = top
            ref[:, 384:] = jnp.zeros((64, LANES), BF16)

    for section, chans in enumerate((C0, C1, C2)):

        @pl.when(on_segment(section))
        def _(section=section, chans=chans):
            if section == 0:
                wide[:C1, :] = jnp.zeros((C1, 4096), F32)
            fetch(chans * 4096)
            copy_rows(held, wide, chans, 4096)
            place = max(chans, C1)
            own_ref = own2_ref if section == 2 else own01_ref
            own_ref[:, :4096] = wide[:place, :].astype(BF16)
            if section == 1:
                fetched(weights_ref, held_weights, 27 * C1 * C2, arrived)
                weight_rows(held_weights, wide_weights, 4)
                turned = jnp.transpose(wide_weights[...])
                mixed[...] = jnp.zeros((144, LANES), F32)
                for group in range(9):
                    for part in range(8):
                        mixed[16 * group : 16 * group + 16, 12 * part : 12 * part + 12] = turned[
                            16 * part : 16 * part + 16, 12 * group : 12 * group + 12
                        ]
                ordered = spread(
                    LANES,
                    LANES,
                    lambda e: 32 * ((e % 12) // 4) + 8 * (e % 4) + e // 12,
                    lambda e: e < 96,
                )
                taps = dot(mixed[...].astype(BF16), ordered).astype(BF16)
                for group in range(9):
                    own01_ref[:, cols(32 + group)] = taps[16 * group : 16 * group + 16, :]
            send(place, 3, up_ref)
            send(place, 0, down_ref)


def weights_layout_kernel(weights_ref, out3_ref, out2_ref, held, wide, arrived):
    @pl.when(on_segment(3))
    def _():
        fetched(weights_ref, held, 27 * C3 * C4, arrived)
        weight_rows(held, wide, 64)
        for group in range(9):
            turned = jnp.transpose(wide[192 * group : 192 * group + 192, :]).astype(BF16)
            rows = slice(C3 * group, C3 * group + C3)
            for part in range(2):
                out3_ref[rows, 192 * part : 192 * part + 192] = turned[64 * part : 64 * part + 64]

    @pl.when(on_segment(2))
    def _():
        fetched(weights_ref, held, 27 * C2 * C3, arrived)
        weight_rows(held, wide, 16)
        for group in range(9):
            turned = jnp.transpose(wide[48 * group : 48 * group + 48, :]).astype(BF16)
            rows = slice(C2 * group, C2 * group + C2)
            for part in range(4):
                out2_ref[rows, 48 * part : 48 * part + 48] = turned[32 * part : 32 * part + 32]


def halves_of(channels, parts):
    size = channels // parts
    return spread(channels, channels, lambda e: (e % parts) * size + e // parts, lambda e: e >= 0)


def quarters(grad):
    turned = (((0,), (0,)), ((), ()))
    mixed = lax.dot_general(halves_of(C3, 4), grad, turned, preferred_element_type=F32)
    return mixed.astype(BF16)


def section3_kernel(own_ref, up_ref, down_ref, weights_ref, out_ref, wide, stacked, terms):
    @pl.when(on_segment(3))
    def _():
        for place, (ref, first) in enumerate(((up_ref, 2), (own_ref, 4), (down_ref, 2))):
            wide[:, cols(2 * place, 2)] = spread_top(ref[:, cols(first)])
        for half in range(2):
            stack_moved(
                lambda row: wide[64 * half : 64 * half + 64, cols(row)],
                stacked.at[192 * half : 192 * half + 192],
                64,
                6,
                (0, 1, 2),
            )
        terms[...] = dot(weights_ref[...], stacked[...])
        unit = spread(LANES, LANES, lambda e: 2 * e, lambda e: e < 64)
        last = is_last_block()
        for cell_z in range(-1, 3):
            for cell_y in range(4):
                total = None
                for tap_z, place_z in taps_of(cell_z, -1, 1):
                    for tap_y, place_y in taps_of(cell_y, 0, 1):
                        first = C3 * (3 * tap_z + tap_y)
                        part = terms[first : first + C3, cols(2 * (place_z + 1) + place_y)]
                        total = part if total is None else total + part
                if cell_z == -1:
                    mask = up_ref[:, cols(cell_y // 2)]
                elif cell_z == 2:
                    mask = down_ref[:, cols(cell_y // 2)]
                else:
                    mask = own_ref[:, cols(2 * cell_z + cell_y // 2)]
                result = sloped(total, half_row(mask, cell_y % 2))
                if cell_z == 2:
                    result = jnp.where(last, jnp.zeros_like(result), result)
                out_ref[:, cols(4 * (cell_z + 1) + cell_y)] = dot(result, unit).astype(BF16)


def section21_kernel(
    grad_ref,
    up_ref,
    down_ref,
    own_ref,
    weights_ref,
    next_ref,
    out0_ref,
    stacked,
    next_stacked,
    terms,
    middle,
    next_weights,
    next_terms,
):
    @pl.when(on_segment(2))
    def _():
        ordered = quarters(grad_ref[...])
        for part in range(4):
            stack_moved(
                lambda row: ordered[16 * part : 16 * part + 16, cols(row)],
                stacked.at[48 * part : 48 * part + 48],
                16,
                16,
                (0, 1, 2),
            )
        terms[...] = dot(weights_ref[...], stacked[...])
        last = is_last_block()
        for cell_z in range(-1, 5):
            for cell_y in range(8):
                total = None
                for tap_z, place_z in taps_of(cell_z, -1, 2):
                    for tap_y, place_y in taps_of(cell_y, 0, 3):
                        first = C2 * (3 * tap_z + tap_y)
                        part = terms[first : first + C2, cols(4 * (place_z + 1) + place_y)]
                        total = part if total is None else total + part
                if cell_z == -1:
                    mask = plane_of_message(up_ref, C2, cell_y)
                elif cell_z == 4:
                    mask = plane_of_message(down_ref, C2, cell_y)
                else:
                    mask = own_ref[:, cols(8 * cell_z + cell_y)]
                result = sloped(total, mask.astype(F32))
                if cell_z == 4:
                    result = jnp.where(last, jnp.zeros_like(result), result)
                middle[:, cols(8 * (cell_z + 1) + cell_y)] = result
        stack_moved(lambda row: middle[:, cols(row)], next_stacked, C2, 48, (-1, 0, 1))
        for tap in range(9):
            next_weights[C1 * tap : C1 * (tap + 1), :] = next_ref[:, cols(32 + tap)]
        next_terms[...] = dot(next_weights[:, :96], next_stacked[...])
        edge = jnp.zeros((C1, LANES), F32)
        for plane in range(4):
            sums = []
            for tap_y in range(3):
                total = None
                for tap_z in range(3):
                    first = C1 * (3 * tap_z + tap_y)
                    part = next_terms[first : first + C1, cols(8 * (plane + 2 - tap_z), 8)]
                    total = part if total is None else total + part
                sums.append(total)
            later = jnp.concatenate([sums[0][:, LANES:], edge], 1)
            earlier = jnp.concatenate([edge, sums[2][:, : 7 * LANES]], 1)
            mask = next_ref[:, cols(8 * plane, 8)].astype(F32)
            out0_ref[:, cols(8 * plane, 8)] = sloped(sums[1] + later + earlier, mask)


def weights21_kernel(
    scale2,
    scale1,
    stacked,
    next_stacked,
    down_ref,
    own_ref,
    next_ref,
    sum2_ref,
    sum1_ref,
    acts2,
    acts1,
):
    @pl.when(on_segment(2))
    def _():
        for tap_z in range(3):
            for tap_y in range(3):
                first = C2 * (3 * tap_z + tap_y)
                for place_z in range(2):
                    for place_y in range(4):
                        plane, row = 2 * place_z + tap_z, 2 * place_y + tap_y
                        if row == 8:
                            block = jnp.zeros((C2, LANES), BF16)
                        elif plane == 4:
                            block = plane_of_message(down_ref, C2, row)
                        else:
                            block = own_ref[:, cols(8 * plane + row)]
                        acts2[first : first + C2, cols(4 * place_z + place_y)] = block
        total = dot_rows(stacked[:, 512:1536], acts2[...]) * scale2
        for group in range(9):
            for tap_x in range(3):
                first = 16 * (3 * group + tap_x)
                for part in range(4):
                    row = 48 * part + 16 * tap_x
                    sum2_ref[first : first + 16, 32 * part : 32 * part + 32] = total[
                        row : row + 16, 32 * group : 32 * group + 32
                    ]
        none = jnp.zeros((C1, LANES), BF16)
        for tap_y in range(3):
            for plane in range(4):
                for row in range(8):
                    source = row + tap_y - 1
                    inside = 0 <= source < 8
                    acts1[C1 * tap_y : C1 * (tap_y + 1), cols(8 * plane + row)] = (
                        next_ref[:, cols(8 * plane + source)] if inside else none
                    )
        for tap_z in range(3):
            grads = next_stacked[:, cols(8 * (2 - tap_z), 32)]
            sum1_ref[48 * tap_z : 48 * tap_z + 48, :96] = dot_rows(acts1[...], grads) * scale1
        sum1_ref[:, 96:] = jnp.zeros((144, 32), F32)


def fine_acts(chans, up_ref, down_ref, own_ref, plane, row):
    if plane == -1:
        return plane_of_message(up_ref, chans, row)
    if plane == 4:
        return plane_of_message(down_ref, chans, row)
    return own_ref[:chans, cols(8 * plane + row)]


def weights01_kernel(
    scale, grad0_ref, sum1_ref, up_ref, down_ref, own_ref, out_ref, stacked, acts
):
    none = jnp.zeros((C1, LANES), BF16)

    @pl.when(on_segment(0))
    def _():
        for place, distance in enumerate((-1, 0, 1)):
            for plane in range(4):
                for row in range(8):
                    block = grad0_ref[:, cols(8 * plane + row)]
                    block = moved_lanes(block, distance) if distance else block
                    for tap_y in range(3):
                        first = C1 * (3 * tap_y + place)
                        target = row + tap_y - 1
                        if 0 <= target < 8:
                            acts[first : first + C1, cols(8 * plane + target)] = block
                    if row == 0:
                        acts[C1 * (6 + place) : C1 * (7 + place), cols(8 * plane)] = none
                    if row == 7:
                        acts[C1 * place : C1 * (place + 1), cols(8 * plane + 7)] = none
        for tap_z in range(3):
            for plane in range(4):
                for row in range(8):
                    stacked[C1 * tap_z : C1 * (tap_z + 1), cols(8 * plane + row)] = fine_acts(
                        C1, up_ref, down_ref, own_ref, plane + tap_z - 1, row
                    )
        out_ref[:, :48] = dot_rows(acts[...], stacked[...]) * scale
        out_ref[:, 48:] = jnp.zeros((144, 80), F32)

    @pl.when(on_segment(1))
    def _():
        out_ref[...] = sum1_ref[...]


def weights3_kernel(scale, places, blocks_ref, down_ref, out_ref, wide, stacked, acts):
    @pl.when(on_segment(3))
    def _():
        me = lax.axis_index("space")
        count = len(places)

        def held(block):
            wanted = lax.bitwise_xor(me, block)
            position = 0
            for bit, value in places_bits(places):
                position = position + value * lax.rem(lax.div(wanted, bit), 2)
            return blocks_ref[position]

        zero = jnp.zeros((64, LANES), BF16)
        for block in range(count):
            here = blocks_ref[0] if count == 1 else held(block)
            wide[:, cols(2 * block, 2)] = spread_top(here[:, cols(4)])
            rows = [half_row(here[:, cols(r // 2)], r % 2).astype(BF16) for r in range(8)]
            if count == 1:
                after = down_ref[:, : 2 * LANES]
            elif block + 1 < count:
                after = held(block + 1)[:, : 2 * LANES]
            else:
                after = None
            for r in range(4):
                rows.append(
                    zero if after is None else half_row(after[:, cols(r // 2)], r % 2).astype(BF16)
                )
            for tap_z in range(3):
                for tap_y in range(3):
                    first = C3 * (3 * tap_z + tap_y)
                    for place_y in range(2):
                        row = 2 * place_y + tap_y
                        source = zero if row == 4 else rows[4 * tap_z + row]
                        acts[first : first + C3, cols(2 * block + place_y)] = source
        stack_moved(lambda row: wide[:, cols(row)], stacked, C4, 2 * count, (0, 1, 2))
        total = dot_rows(stacked[...], acts[...]) * scale
        for group in range(9):
            for tap_x in range(3):
                first = 64 * (3 * group + tap_x)
                for part in range(2):
                    row = C4 * tap_x + 64 * part
                    out_ref[first : first + 64, 64 * part : 64 * part + 64] = total[
                        row : row + 64, C3 * group : C3 * group + C3
                    ]


def places_bits(places):
    count = len(places)
    bits = []
    bit = 1
    while bit < count:
        bits.append((bit, places.index(bit)))
        bit *= 2
    return bits


def call(kernel, outs, scratch, *args, flops, far=()):
    shapes = [jax.ShapeDtypeStruct(*entry) for entry in outs]
    moved = sum(a.size * a.dtype.itemsize for a in [*args, *shapes])
    near_spec = pl.BlockSpec(memory_space=pltpu.VMEM)
    far_spec = pl.BlockSpec(memory_space=pltpu.HBM)
    return pl.pallas_call(
        kernel,
        out_shape=shapes,
        in_specs=[far_spec if place in far else near_spec for place in range(len(args))],
        scratch_shapes=[
            pltpu.VMEM(*entry) if isinstance(entry, tuple) else entry for entry in scratch
        ],
        compiler_params=pltpu.CompilerParams(vmem_limit_bytes=VMEM_LIMIT),
        cost_estimate=pl.CostEstimate(flops=flops, bytes_accessed=moved, transcendentals=0),
    )(*args)


def pairs_of(segments, route):
    total = lax.axis_size("segment")
    count = lax.axis_size("space")
    return [
        (a * total + s, b * total + s) for a, b in route(count) for s in segments
    ]


def over_space(block, segments, route):
    return lax.ppermute(block, ("space", "segment"), pairs_of(segments, route))


def filled(ordered):
    rows = ordered.reshape(-1, LANES) if ordered.size % LANES == 0 else None
    if rows is None:
        flat = ordered.reshape(-1)
        rows = jnp.pad(flat, (0, -flat.shape[0] % LANES)).reshape(-1, LANES)
    return rows


def shards(saved_inputs, conv_weights, top_gradient):
    segment = lax.axis_index("segment")
    count = lax.axis_size("space")
    room = conv_weights.shape[1]
    scales = [1.0 / math.sqrt(count * cells) for cells in (4096, 4096, 512, 64)]

    def later(n):
        return [(i, i + 1) for i in range(n - 1)]

    def sooner(n):
        return [(i + 1, i) for i in range(n - 1)]

    def behind(values, *leaders):
        return lax.optimization_barrier((*values, *leaders))[: len(values)]

    saved_inputs = pltpu.with_memory_space_constraint(saved_inputs, pltpu.HBM)
    conv_weights = pltpu.with_memory_space_constraint(conv_weights, pltpu.HBM)
    top = jnp.transpose(top_gradient[:, 0], (1, 2, 0)).reshape(64, C4)
    top = pltpu.with_memory_space_constraint(top, pltpu.HBM)
    deep, up, down, own2, own01 = call(
        layout_kernel,
        [
            ((64, 640), BF16),
            ((64, 512), BF16),
            ((64, 512), BF16),
            ((32, 4096), BF16),
            ((16, 5248), BF16),
        ],
        [
            ((1, 131072), BF16),
            ((1, 13824), BF16),
            ((64, 4096), F32),
            ((128, 128), F32),
            ((144, 128), F32),
            ((64, 128), BF16),
            pltpu.SemaphoreType.DMA,
            pltpu.SemaphoreType.DMA,
        ],
        saved_inputs,
        conv_weights,
        top,
        flops=0,
        far=(0, 1, 2),
    )
    up = over_space(up, [0, 2, 3], later)
    down = over_space(down, [0, 2, 3], sooner)
    next_own = lax.ppermute(own01, "segment", [(1, 2)])
    (weights,) = behind((conv_weights,), deep)
    taps3, taps2 = call(
        weights_layout_kernel,
        [((576, 384), BF16), ((288, 192), BF16)],
        [((1, 221184), BF16), ((1728, 128), F32), pltpu.SemaphoreType.DMA],
        weights,
        flops=0,
        far=(0,),
    )
    taps3, taps2 = behind((taps3, taps2), next_own)

    (grad2,) = call(
        section3_kernel,
        [((64, 2048), BF16)],
        [((128, 768), BF16), ((384, 768), BF16), ((576, 768), F32)],
        deep,
        up,
        down,
        taps3,
        flops=2 * 576 * 384 * 768,
    )
    places = [0]
    even = not count & (count - 1)
    gathers = even and count <= GATHER_LIMIT
    bits = [1 << power for power in range(count.bit_length() - 1)] if even else []


    def swap(block, segments, bit):
        return over_space(block, segments, lambda n: [(i, i ^ bit) for i in range(n)])

    def gathered(blocks, bit):
        return jnp.concatenate([blocks, swap(blocks, [3], bit)], 0)

    (blocks,) = behind((deep[None],), grad2)
    if gathers:
        for bit in bits[:0:-1][:1]:
            blocks = gathered(blocks, bit)
            places = places + [place ^ bit for place in places]
    grad2 = lax.ppermute(grad2, "segment", [(3, 2)])
    (grad2,) = behind((grad2,), blocks)
    grad0, stacked2, stacked1 = call(
        section21_kernel,
        [((16, 4096), BF16), ((192, 2048), BF16), ((96, 6144), BF16)],
        [
            ((288, 2048), F32),
            ((32, 6144), BF16),
            ((144, 128), BF16),
            ((144, 6144), F32),
        ],
        grad2,
        up,
        down,
        own2,
        taps2,
        next_own,
        flops=2 * 288 * 192 * 2048,
    )
    sum2, sum1 = call(
        functools.partial(weights21_kernel, scales[2], scales[1]),
        [((432, 128), F32), ((144, 128), F32)],
        [((288, 1024), BF16), ((48, 4096), BF16)],
        stacked2,
        stacked1,
        down,
        own2,
        next_own,
        flops=LONG,
    )
    (blocks,) = behind((blocks,), grad0)
    grad0 = lax.ppermute(grad0, "segment", [(2, 0)])
    sum1 = lax.ppermute(sum1, "segment", [(2, 1)])
    if gathers:
        for bit in bits[:0:-1][1:]:
            blocks = gathered(blocks, bit)
            places = places + [place ^ bit for place in places]
    grad0, sum1 = behind((grad0, sum1), sum2)
    (sum01,) = call(
        functools.partial(weights01_kernel, scales[0]),
        [((144, 128), F32)],
        [((48, 4096), BF16), ((144, 4096), BF16)],
        grad0,
        sum1,
        up,
        down,
        own01,
        flops=2 * 144 * 96 * 6144,
    )
    for bit in bits:
        sum2 = sum2 + swap(sum2, [2], bit)
    if not even:
        sum2 = lax.psum(sum2, "space")
        sum01 = lax.psum(sum01, "space")
    if gathers:
        blocks = gathered(blocks, bits[0])
        places = places + [place ^ bits[0] for place in places]
    for bit in bits:
        sum01 = sum01 + swap(sum01, [0, 1], bit)
    held = len(places)
    (sum3,) = call(
        functools.partial(weights3_kernel, scales[3], places),
        [((1728, 128), F32)],
        [((128, 256 * held), BF16), ((384, 256 * held), BF16), ((576, 256 * held), BF16)],
        blocks,
        down,
        flops=LONG,
    )
    if held < count:
        sum3 = lax.psum(sum3, "space")

    def finish0(sum01, sum2, sum3):
        parts = sum01[:, :48].reshape(3, 3, C1, 3, 16)[..., :C0]
        return filled(jnp.transpose(parts, (3, 0, 1, 2, 4)))

    def finish1(sum01, sum2, sum3):
        parts = sum01[:, :96].reshape(9, C1, 3, C2)
        return filled(jnp.transpose(parts, (0, 2, 3, 1)))

    def whole(finish):
        def branch(*sums):
            rows = finish(*sums)
            return jnp.pad(rows, ((0, room // LANES - rows.shape[0]), (0, 0)))

        return branch

    ends = [finish0, finish1, lambda a, b, c: b, lambda a, b, c: c]
    rows = lax.switch(segment, [whole(end) for end in ends], sum01, sum2, sum3)
    return rows.reshape(1, room)


def solution(mesh):
    return jax.shard_map(
        shards,
        mesh=mesh,
        in_specs=(P("segment", "space"), P("segment", None), P(None, "space", None, None)),
        out_specs=P("segment", None),
        check_vma=False,
    )
```
